32 devices in a mesh: stream: 2 (over core), dp: 16 (over z, y, x).
Axes of the slice: x: 2, y: 2, z: 4, core: 2. Of those that a mesh axis runs over, the one named last changes fastest.
Arguments:
- tokens: bfloat16 [2, 16384, 1024], P('stream', 'dp'), may hold values from -6 to 6
- doc_lengths: int32 [16, 8], replicated, may hold values from 104 to 152, as said below
- cand_docs: int32 [16, 2, 16, 8], P('dp', 'stream'), may hold values from 0 to 127, as said below
- group_sizes: int32 [16, 2, 16], P('dp', 'stream'), may hold values from 2 to 8, as said below
- w_qkv: bfloat16 [1024, 3072], replicated, may hold values from -0.1875 to 0.1875
- b_qkv: bfloat16 [3072], replicated, may hold values from -3 to 3
- w_attn_out: bfloat16 [1024, 1024], replicated, may hold values from -0.75 to 0.75
- b_attn_out: bfloat16 [1024], replicated, may hold values from -2 to 2
- gain_one: bfloat16 [1024], replicated, may hold values from 0.099609375 to 1.8984375
- bias_one: bfloat16 [1024], replicated, may hold values from -2 to 2
- w_up: bfloat16 [1024, 4096], replicated, may hold values from -0.1875 to 0.1875
- b_up: bfloat16 [4096], replicated, may hold values from -3 to 3
- w_down: bfloat16 [4096, 1024], replicated, may hold values from -0.09375 to 0.09375
- b_down: bfloat16 [1024], replicated, may hold values from -2 to 2
- gain_two: bfloat16 [1024], replicated, may hold values from 0.099609375 to 1.8984375
- bias_two: bfloat16 [1024], replicated, may hold values from -2 to 2
- w_proj: bfloat16 [1024, 128], replicated, may hold values from -0.1875 to 0.1875
Outputs:
- loss: float32 [16, 2, 16], P('dp', 'stream')
- grad_tokens: float32 [2, 16384, 1024], P('stream', 'dp')
- grad_w_qkv: float32 [1024, 3072], P(('stream', 'dp'))
- grad_b_qkv: float32 [3072], P(('stream', 'dp'))
- grad_w_attn_out: float32 [1024, 1024], P(('stream', 'dp'))
- grad_b_attn_out: float32 [1024], P(('stream', 'dp'))
- grad_gain_one: float32 [1024], P(('stream', 'dp'))
- grad_bias_one: float32 [1024], P(('stream', 'dp'))
- grad_w_up: float32 [1024, 4096], P(('stream', 'dp'))
- grad_b_up: float32 [4096], P(('stream', 'dp'))
- grad_w_down: float32 [4096, 1024], P(('stream', 'dp'))
- grad_b_down: float32 [1024], P(('stream', 'dp'))
- grad_gain_two: float32 [1024], P(('stream', 'dp'))
- grad_bias_two: float32 [1024], P(('stream', 'dp'))
- grad_w_proj: float32 [1024, 128], P(('stream', 'dp'))
The draws below stay inside these ranges and needn't reach their ends.
Inputs may be any that keep to these rules, and one draw needn't show every extreme that they name: `doc_lengths`: each row's lengths sum to 1024; documents 2 i and 2 i + 1 of a row form a pair whose lengths sum to 256, the longer one within 5 of 152; every row has a document of exactly 152. `cand_docs`: document n is document n mod 8 of document row n // 8; candidate 0 is the longer document of its pair, candidates 1 onward are shorter documents of their pairs. `group_sizes`: candidate 0 of a query is its positive.
All inputs are finite; a program needn't handle non-finite values.
Results may differ from the reference program's by a relative error of at most 0.018.
Values may be sent and summed in bfloat16 or wider, within the bound.
No kernel may reach another device: no remote copies, remote signals or barrier semaphores. Data moves between devices by JAX's collectives and lax.ppermute only.
A program may use at most 448 MiB of HBM per device.

```python
import math
import jax
import jax.numpy as jnp
from jax import lax

D = 1024
HD = 64
FF = 4096
PROJ = 128
TOK_DEV = 1024
QLEN = 32
CAND = 8
DOC_AVG = 128
MOST = 152
SEGS = 8
QH = 16
TOKENS = 16384
N_DP = 16


def doc_pattern(key):
    base = jax.random.fold_in(key, 7)
    pair_count = SEGS // 2
    long_first = jax.random.randint(jax.random.fold_in(base, 1), (N_DP, pair_count), 0, 2).astype(jnp.int32)
    jitter = jax.random.randint(jax.random.fold_in(base, 2), (N_DP, pair_count), 0, DOC_AVG // 32 + 2).astype(jnp.int32)
    jitter = jitter.at[:, 0].set(0)
    return (long_first, jitter)


def draw_doc_lengths(key, part):
    long_first, jitter = doc_pattern(key)
    long_len = (MOST - jitter).astype(jnp.int32)
    short_len = (2 * DOC_AVG - long_len).astype(jnp.int32)
    first = jnp.where(long_first == 1, long_len, short_len)
    second = jnp.where(long_first == 1, short_len, long_len)
    return jnp.stack([first, second], -1).reshape(N_DP, SEGS).astype(jnp.int32)


def draw_cand_docs(key, part):
    long_first, jitter = doc_pattern(key)
    picker = jax.random.fold_in(key, 11)
    shape_all = (N_DP, 2, QH, CAND)
    row_pick = jax.random.randint(jax.random.fold_in(picker, 1), shape_all, 0, N_DP).astype(jnp.int32)
    pair_pick = jax.random.randint(jax.random.fold_in(picker, 2), shape_all, 0, SEGS // 2).astype(jnp.int32)
    first_flag = long_first[row_pick, pair_pick]
    positive = (jnp.arange(CAND, dtype=jnp.int32) == 0)[None, None, None, :]
    slot_pick = jnp.where(positive, 1 - first_flag, first_flag).astype(jnp.int32)
    return (row_pick * SEGS + 2 * pair_pick + slot_pick).astype(jnp.int32)


def draw_group_sizes(key, part):
    counts = jax.random.randint(key, (N_DP, 2, QH), 2, CAND + 1).astype(jnp.int32)
    return counts.at[0, 0, 0].set(CAND)


def shard_levels(stream_key, dims, pieces, least, top_value):
    loudness, own = 1.0, jax.random.fold_in(stream_key, 6)
    for dim, blocks in pieces:
        heights = jnp.exp(jax.random.uniform(jax.random.fold_in(own, dim), (blocks,), jnp.float32, least / len(pieces), top_value / len(pieces)))
        loudness = loudness * jnp.repeat(heights, dims[dim] // blocks).reshape([-1 if axis == dim else 1 for axis in range(len(dims))])
    return loudness


def bell_draw(key, shape, scale, most, shards=(), kind=jnp.bfloat16):
    entries = scale * jax.random.normal(key, shape, jnp.float32)
    if shards:
        entries = entries * shard_levels(key, shape, shards, -0.22, 0.18)
    return jnp.clip(entries, -most, most).astype(kind)


def setup_inputs(seed: int = 0) -> dict:
    key_of = jax.random.split(jax.random.key(seed), 18)
    tokens = bell_draw(key_of[0], (2, TOKENS, D), 1.0, 6.0, ((0, 2), (1, 16)))
    doc_lengths = draw_doc_lengths(jax.random.fold_in(key_of[17], 71), 0)
    cand_docs = draw_cand_docs(jax.random.fold_in(key_of[17], 71), 0)
    group_sizes = draw_group_sizes(jax.random.fold_in(key_of[17], 71), 0)
    w_qkv = bell_draw(key_of[4], (D, 3 * D), D ** -0.5, 0.1875)
    b_qkv = bell_draw(key_of[5], (3 * D,), 0.5, 3.0)
    w_attn_out = bell_draw(key_of[6], (D, D), (D // 16) ** -0.5, 0.75)
    b_attn_out = bell_draw(key_of[7], (D,), 0.3, 2.0)
    gain_one = jnp.clip(1.0 + 0.18 * jax.random.normal(key_of[8], (D,), jnp.float32), 0.099609375, 1.8984375).astype(jnp.bfloat16)
    bias_one = bell_draw(key_of[9], (D,), 0.3, 2.0)
    w_up = bell_draw(key_of[10], (D, FF), D ** -0.5, 0.1875)
    b_up = bell_draw(key_of[11], (FF,), 0.5, 3.0)
    w_down = bell_draw(key_of[12], (FF, D), FF ** -0.5, 0.09375)
    b_down = bell_draw(key_of[13], (D,), 0.3, 2.0)
    gain_two = jnp.clip(1.0 + 0.18 * jax.random.normal(key_of[14], (D,), jnp.float32), 0.099609375, 1.8984375).astype(jnp.bfloat16)
    bias_two = bell_draw(key_of[15], (D,), 0.3, 2.0)
    w_proj = bell_draw(key_of[16], (D, PROJ), D ** -0.5, 0.1875)
    return dict(tokens=tokens, doc_lengths=doc_lengths, cand_docs=cand_docs, group_sizes=group_sizes, w_qkv=w_qkv, b_qkv=b_qkv, w_attn_out=w_attn_out, b_attn_out=b_attn_out, gain_one=gain_one, bias_one=bias_one, w_up=w_up, b_up=b_up, w_down=w_down, b_down=b_down, gain_two=gain_two, bias_two=bias_two, w_proj=w_proj)


score_scale = 0.125
sim_temp = 0.05
loss_temp = 0.08
masked_value = -1e+30
norm_eps = 1e-05
vector_eps = 1e-06

@jax.custom_vjp
def low(v):
    return lax.optimization_barrier(v.astype(jnp.bfloat16)).astype(jnp.float32)

@jax.custom_vjp
def low_back(v):
    return v

def low_keep(v):
    return (low(v), None)

def low_pass(kept, grad):
    return (grad,)

def back_keep(v):
    return (v, None)

def back_low(kept, grad):
    return (low(grad),)
low.defvjp(low_keep, low_pass)
low_back.defvjp(back_keep, back_low)

def matmul_exact(left, right):
    return jnp.dot(left, right, precision=lax.Precision.HIGHEST)

def log_total(values, axis):
    highest = lax.optimization_barrier(jnp.max(values, axis=axis, keepdims=True))
    return jnp.squeeze(highest, axis) + jnp.log(lax.optimization_barrier(jnp.sum(jnp.exp(values - highest), axis=axis)))

def layer_norm(values, scale_vec, offset):
    center = values - lax.optimization_barrier(jnp.mean(values, -1, keepdims=True))
    spread = lax.optimization_barrier(jnp.mean(center * center, -1, keepdims=True))
    return center * lax.rsqrt(spread + norm_eps) * scale_vec + offset

def angle_tables(position, size_head):
    half_size = size_head // 2
    frequency = jnp.exp(jnp.arange(half_size, dtype=jnp.float32) * (-2.0 * math.log(10000.0) / size_head))
    angles = position.astype(jnp.float32)[:, None] * frequency[None, :]
    return (jnp.cos(angles)[:, None, :], jnp.sin(angles)[:, None, :])

def rotate(values, cosine, sine):
    half_size = values.shape[-1] // 2
    leading = values[..., :half_size]
    second = values[..., half_size:]
    return jnp.concatenate([leading * cosine - second * sine, second * cosine + leading * sine], -1)

def doc_layout(lengths, tokens_here):
    doc_ends = jnp.cumsum(lengths).astype(jnp.int32)
    starts = (doc_ends - lengths).astype(jnp.int32)
    indices = jnp.arange(tokens_here, dtype=jnp.int32)
    segment = lax.optimization_barrier(jnp.sum((indices[:, None] >= doc_ends[None, :]).astype(jnp.int32), axis=1)).astype(jnp.int32)
    chosen = segment[:, None] == jnp.arange(lengths.shape[0], dtype=jnp.int32)[None, :]
    start_of = lax.optimization_barrier(jnp.sum(jnp.where(chosen, starts[None, :], 0), axis=1)).astype(jnp.int32)
    return (segment, (indices - start_of).astype(jnp.int32))

def encode(hidden, segment, position, params):
    w_qkv, b_qkv, w_attn_out, b_attn_out, gain_one, bias_one, w_up, b_up, w_down, b_down, gain_two, bias_two, w_proj = params
    tokens_here, model_width = hidden.shape
    head_count = model_width // HD
    mixed_qkv = low_back(matmul_exact(hidden, w_qkv) + b_qkv)
    shaped = mixed_qkv.reshape(tokens_here, 3, head_count, HD)
    cosine, sine = angle_tables(position, HD)
    query_vec = low(rotate(shaped[:, 0], cosine, sine))
    key_vec = low(rotate(shaped[:, 1], cosine, sine))
    value_vec = low(shaped[:, 2])
    raw_scores = low_back(jnp.einsum('thd,uhd->htu', query_vec, key_vec, precision=lax.Precision.HIGHEST) * score_scale)
    masked = jnp.where((segment[:, None] == segment[None, :])[None], raw_scores, masked_value)
    log_norm = log_total(masked, -1)
    attn_weights = low(jnp.exp(masked - log_norm[..., None]))
    attended = jnp.einsum('htu,uhd->thd', attn_weights, value_vec, precision=lax.Precision.HIGHEST)
    attended = low_back(low(attended.reshape(tokens_here, model_width)))
    branch = low_back(matmul_exact(attended, w_attn_out) + b_attn_out)
    normed = layer_norm(hidden + branch, gain_one, bias_one)
    upward = low_back(matmul_exact(low(normed), w_up) + b_up)
    active = low(jax.nn.gelu(upward, approximate=False))
    ffn_out = low_back(matmul_exact(active, w_down) + b_down)
    final_norm = layer_norm(normed + ffn_out, gain_two, bias_two)
    projected = low_back(matmul_exact(low(final_norm), w_proj))
    return low(projected * lax.rsqrt(lax.optimization_barrier(jnp.sum(projected * projected, -1, keepdims=True)) + vector_eps))

def reference(tokens, doc_lengths, cand_docs, group_sizes, w_qkv, b_qkv, w_attn_out, b_attn_out, gain_one, bias_one, w_up, b_up, w_down, b_down, gain_two, bias_two, w_proj):
    indices = jnp.arange(TOK_DEV, dtype=jnp.int32)
    doc_segment, doc_position = jax.vmap(lambda lengths: doc_layout(lengths, TOK_DEV))(doc_lengths)
    query_segment = jnp.broadcast_to(indices // QLEN, (N_DP, TOK_DEV)).astype(jnp.int32)
    query_position = jnp.broadcast_to(indices % QLEN, (N_DP, TOK_DEV)).astype(jnp.int32)
    segments = jnp.concatenate([query_segment, doc_segment], 0)
    positions = jnp.concatenate([query_position, doc_position], 0)
    doc_ends = jnp.cumsum(doc_lengths, axis=1).astype(jnp.int32)
    row_base = (jnp.arange(N_DP, dtype=jnp.int32) * TOK_DEV)[:, None]
    starts = (doc_ends - doc_lengths + row_base).astype(jnp.int32).reshape(-1)
    doc_spans = doc_lengths.reshape(-1)
    offsets = jnp.arange(MOST, dtype=jnp.int32)
    params = tuple((weight.astype(jnp.float32) for weight in (w_qkv, b_qkv, w_attn_out, b_attn_out, gain_one, bias_one, w_up, b_up, w_down, b_down, gain_two, bias_two, w_proj)))

    def objective(tokens_f, weights):
        rows_all = tokens_f.reshape(2 * N_DP, TOK_DEV, D)
        encoder = jax.checkpoint(lambda inputs: encode(inputs[0], inputs[1], inputs[2], weights))
        vectors = lax.map(encoder, (rows_all, segments, positions))
        query_vecs = vectors[:N_DP].reshape(N_DP, 2, QH, QLEN, PROJ)
        doc_vecs = vectors[N_DP:].reshape(N_DP * TOK_DEV, PROJ)

        def block_loss(inputs):
            queries, candidates, group_count = inputs
            doc_first = starts[candidates]
            doc_len = doc_spans[candidates]
            doc_rows = jnp.minimum(doc_first[..., None] + offsets, N_DP * TOK_DEV - 1)
            in_document = offsets < doc_len[..., None]
            picked = doc_vecs[doc_rows]
            sim = low_back(jnp.einsum('sqtc,sqkuc->sqktu', queries, picked, precision=lax.Precision.HIGHEST))
            best = sim_temp * log_total(jnp.where(in_document[:, :, :, None, :], sim / sim_temp, masked_value), -1)
            score = lax.optimization_barrier(jnp.sum(best, -1))
            counted = jnp.arange(CAND, dtype=jnp.int32) < group_count[..., None]
            logits = jnp.where(counted, score / loss_temp, masked_value)
            return log_total(logits, -1) - logits[..., 0]
        losses = lax.map(jax.checkpoint(block_loss), (query_vecs, cand_docs, group_sizes))
        return (jnp.sum(losses), losses)
    tokens_f = tokens.astype(jnp.float32)
    objective_value, pullback, losses = jax.vjp(objective, tokens_f, params, has_aux=True)
    grad_tokens, grad_weights = pullback(jnp.ones_like(objective_value))
    return (losses, grad_tokens, grad_weights[0], grad_weights[1], grad_weights[2], grad_weights[3], grad_weights[4], grad_weights[5], grad_weights[6], grad_weights[7], grad_weights[8], grad_weights[9], grad_weights[10], grad_weights[11], grad_weights[12])
```

```python
import functools
import math

import jax
import jax.numpy as jnp
import numpy as np
from jax import lax
from jax.experimental import pallas as pl
from jax.experimental.pallas import tpu as pltpu
from jax.sharding import PartitionSpec as P

HD = 64
PROJ = 128
QLEN = 32
CAND = 8
QH = 16
PAIR = 256

score_scale = 0.125
sim_temp = 0.05
loss_temp = 0.08
masked_value = -1e30
norm_eps = 1e-05
vector_eps = 1e-06

f32 = jnp.float32
bf16 = jnp.bfloat16
MIB = 1 << 20

NN = (((1,), (0,)), ((), ()))
NT = (((1,), (1,)), ((), ()))
TN = (((0,), (0,)), ((), ()))


def mm(left, right, dims=NN):
    return lax.dot_general(left, right, dims, preferred_element_type=f32)


def params(mib):
    return pltpu.CompilerParams(vmem_limit_bytes=mib * MIB)


def cost(flops, moved):
    return pl.CostEstimate(flops=int(flops), bytes_accessed=int(moved), transcendentals=0)


def whole(shape):
    return pl.BlockSpec(shape, lambda *_: (0,) * len(shape))


VECTORS = ("b_qkv", "b_attn_out", "gain_one", "bias_one", "b_down", "gain_two", "bias_two", "b_up")


def vector_spec(name, width, cols=None):
    place = VECTORS.index(name)
    at = 0 if place == 0 else (2 + place) * width
    if cols is None:
        cols = 3 * width if place == 0 else width
        return pl.BlockSpec((1, cols), lambda *_: (0, at // cols), pipeline_mode=pl.Buffered(1))
    return pl.BlockSpec((1, cols), lambda i, *_: (0, at // cols + i))


def once(shape):
    return pl.BlockSpec(shape, lambda *_: (0,) * len(shape), pipeline_mode=pl.Buffered(1))


def rotation_tables():
    freq = np.exp(np.arange(HD // 2) * (-2.0 * math.log(10000.0) / HD))
    lane = np.arange(2 * HD)
    angle = np.arange(PAIR)[:, None] * freq[lane % (HD // 2)][None, :]
    sign = np.where(lane % HD < HD // 2, -1.0, 1.0)[None, :]
    return np.cos(angle).astype(np.float32), (np.sin(angle) * sign).astype(np.float32)


def tables_here(stream, first_lengths):
    rows = jnp.arange(PAIR, dtype=jnp.int32)[:, None]

    def place(table):
        reps = PAIR // QLEN
        query = jnp.asarray(np.tile(table[:QLEN], (reps, 1)))
        base = jnp.asarray(table)
        padded = jnp.asarray(np.concatenate([table, table], 0))
        blocks = []
        for i in range(first_lengths.shape[0]):
            moved = lax.dynamic_slice_in_dim(padded, PAIR - first_lengths[i], PAIR, 0)
            doc = jnp.where(rows < first_lengths[i], base, moved)
            blocks.append(jnp.where(stream == 1, doc, query))
        return jnp.concatenate(blocks, 0)

    cosine, sine = rotation_tables()
    return place(cosine), place(sine)


def partner(values):
    lane = lax.broadcasted_iota(jnp.int32, values.shape, 1)
    ahead = pltpu.roll(values, 2 * HD - HD // 2, 1)
    behind = pltpu.roll(values, HD // 2, 1)
    return jnp.where(lane % HD < HD // 2, ahead, behind)


def same_segment(info_ref, block):
    is_doc = info_ref[0] == 1
    first = info_ref[1 + block]
    row = lax.broadcasted_iota(jnp.int32, (PAIR, PAIR), 0)
    col = lax.broadcasted_iota(jnp.int32, (PAIR, PAIR), 1)
    doc = ((row >= first) ^ (col >= first)).astype(jnp.int32)
    query = ((row // QLEN) ^ (col // QLEN)).astype(jnp.int32)
    return jnp.where(is_doc, doc, query) == 0


def normalise(values):
    mean = jnp.mean(values, -1, keepdims=True)
    center = values - mean
    rstd = lax.rsqrt(jnp.mean(center * center, -1, keepdims=True) + norm_eps)
    return center * rstd, rstd


def norm_back(grad, hat, rstd, gain):
    scaled = grad * gain
    return (
        scaled - jnp.mean(scaled, -1, keepdims=True) - hat * jnp.mean(scaled * hat, -1, keepdims=True)
    ) * rstd


def column_sum(values):
    return jnp.sum(values, 0, keepdims=True)


def attend_kernel(
    info_ref, x_ref, wqkv_ref, bqkv_ref, cos_ref, sin_ref, wo_ref, bo_ref, g_ref, c_ref,
    qkv_ref, att_ref, hat_ref, rstd_ref, normb_ref, mask_ref,
):
    width = x_ref.shape[1]
    x = x_ref[...]
    cosine = cos_ref[...]
    sine = sin_ref[...]
    step = 256
    for start in range(0, 3 * width, step):
        mixed = mm(x, wqkv_ref[:, start : start + step]) + bqkv_ref[:, start : start + step].astype(f32)
        if start < 2 * width:
            parts = []
            for off in range(0, step, 2 * HD):
                one = mixed[:, off : off + 2 * HD]
                one = one * cosine + partner(one) * sine
                parts.append(one.astype(bf16))
            mixed = jnp.concatenate(parts, 1)
            if start < width:
                mixed = mixed * jnp.asarray(score_scale, bf16)
        qkv_ref[:, start : start + step] = mixed.astype(bf16)
    mask_ref[...] = jnp.where(same_segment(info_ref, pl.program_id(0)), 0.0, masked_value)
    lane = lax.broadcasted_iota(jnp.int32, (PAIR, 2 * HD), 1)
    for pair in range(width // (2 * HD)):
        at = pair * 2 * HD
        query = qkv_ref[:, at : at + 2 * HD]
        key = qkv_ref[:, width + at : width + at + 2 * HD]
        value = qkv_ref[:, 2 * width + at : 2 * width + at + 2 * HD]
        total = None
        for head in range(2):
            mine = (lane < HD) if head == 0 else (lane >= HD)
            zero = jnp.zeros_like(key)
            scores = mm(query, jnp.where(mine, key, zero), NT) + mask_ref[...]
            highest = jnp.max(scores, -1, keepdims=True)
            terms = jnp.exp(scores - highest)
            weights = (terms * (1.0 / jnp.sum(terms, -1, keepdims=True))).astype(bf16)
            part = mm(weights, jnp.where(mine, value, zero))
            total = part if total is None else total + part
        att_ref[:, at : at + 2 * HD] = total.astype(bf16)
    branch = mm(att_ref[...], wo_ref[...]) + bo_ref[...].astype(f32)
    hat, rstd = normalise(x.astype(f32) + branch)
    hat_ref[...] = hat
    rstd_ref[...] = jnp.broadcast_to(rstd, rstd_ref.shape)
    normb_ref[...] = (hat * g_ref[...].astype(f32) + c_ref[...].astype(f32)).astype(bf16)


def attend(info, x, w_qkv, cosine, sine, w_out, vectors):
    rows, width = x.shape
    block = lambda cols: pl.BlockSpec((PAIR, cols), lambda i, *_: (i, 0))
    return pl.pallas_call(
        attend_kernel,
        grid_spec=pltpu.PrefetchScalarGridSpec(
            num_scalar_prefetch=1,
            grid=(rows // PAIR,),
            in_specs=[
                block(width), once((width, 3 * width)), vector_spec("b_qkv", width), block(2 * HD), block(2 * HD),
                once((width, width)), vector_spec("b_attn_out", width), vector_spec("gain_one", width),
                vector_spec("bias_one", width),
            ],
            out_specs=[block(3 * width), block(width), block(width), block(128), block(width)],
            scratch_shapes=[pltpu.VMEM((PAIR, PAIR), f32)],
        ),
        out_shape=[
            jax.ShapeDtypeStruct((rows, 3 * width), bf16),
            jax.ShapeDtypeStruct((rows, width), bf16),
            jax.ShapeDtypeStruct((rows, width), f32),
            jax.ShapeDtypeStruct((rows, 128), f32),
            jax.ShapeDtypeStruct((rows, width), bf16),
        ],
        compiler_params=params(62),
        cost_estimate=cost(2 * rows * width * 4 * width, 30 * MIB),
        name="attend",
    )(info, x, w_qkv, vectors, cosine, sine, w_out, vectors, vectors, vectors)


def feed_kernel(
    x_ref, wup_ref, bup_ref, wdown_ref, bdown_ref, hat1_ref, g1_ref, c1_ref, g2_ref, c2_ref, wproj_ref,
    act_ref, der_ref, hat2_ref, rstd2_ref, final_ref, proj_ref, vec_ref, acc_ref,
):
    step = pl.program_id(0)
    upward = mm(x_ref[...], wup_ref[...]) + bup_ref[...].astype(f32)
    below = 0.5 + 0.5 * lax.erf(upward * (2.0**-0.5))
    density = jnp.exp(-0.5 * upward * upward) * ((2.0 * math.pi) ** -0.5)
    active = (upward * below).astype(bf16)
    act_ref[...] = active
    der_ref[...] = (below + upward * density).astype(bf16)
    part = mm(active, wdown_ref[...])

    @pl.when(step == 0)
    def _():
        acc_ref[...] = part

    @pl.when(step > 0)
    def _():
        acc_ref[...] += part

    @pl.when(step == pl.num_programs(0) - 1)
    def _():
        for at in range(0, acc_ref.shape[0], PAIR):
            span = slice(at, at + PAIR)
            normed = hat1_ref[span, :] * g1_ref[...].astype(f32) + c1_ref[...].astype(f32)
            hat, rstd = normalise(normed + acc_ref[span, :] + bdown_ref[...].astype(f32))
            hat2_ref[span, :] = hat
            rstd2_ref[span, :] = jnp.broadcast_to(rstd, (PAIR, 128))
            final = (hat * g2_ref[...].astype(f32) + c2_ref[...].astype(f32)).astype(bf16)
            final_ref[span, :] = final
            projected = mm(final, wproj_ref[...])
            proj_ref[span, :] = projected
            inverse = lax.rsqrt(jnp.sum(projected * projected, -1, keepdims=True) + vector_eps)
            vec_ref[span, :] = (projected * inverse).astype(bf16)


def feed(x, w_up, w_down, hat1, w_proj, vectors):
    rows, width = x.shape
    units = w_up.shape[1]
    step = 512
    cols = pl.BlockSpec((rows, step), lambda i: (0, i))
    return pl.pallas_call(
        feed_kernel,
        grid=(units // step,),
        in_specs=[
            once((rows, width)),
            pl.BlockSpec((width, step), lambda i: (0, i)),
            vector_spec("b_up", width, step),
            pl.BlockSpec((step, width), lambda i: (i, 0)),
            vector_spec("b_down", width), once((rows, width)), vector_spec("gain_one", width),
            vector_spec("bias_one", width), vector_spec("gain_two", width), vector_spec("bias_two", width),
            once((width, PROJ)),
        ],
        out_specs=[cols, cols, whole((rows, width)), whole((rows, 128)), whole((rows, width)),
                   whole((rows, PROJ)), whole((rows, PROJ))],
        out_shape=[
            jax.ShapeDtypeStruct((rows, units), bf16),
            jax.ShapeDtypeStruct((rows, units), bf16),
            jax.ShapeDtypeStruct((rows, width), f32),
            jax.ShapeDtypeStruct((rows, 128), f32),
            jax.ShapeDtypeStruct((rows, width), bf16),
            jax.ShapeDtypeStruct((rows, PROJ), f32),
            jax.ShapeDtypeStruct((rows, PROJ), bf16),
        ],
        scratch_shapes=[pltpu.VMEM((rows, width), f32)],
        compiler_params=params(62),
        cost_estimate=cost(4 * rows * width * units, 50 * MIB),
        name="feed",
    )(x, w_up, vectors, w_down, vectors, hat1, vectors, vectors, vectors, vectors, w_proj)


def score_kernel(
    cand_ref, size_ref, length_ref, place_ref, q_ref, near_ref, far_ref,
    loss_ref, dq_ref, keep_ref, send_ref, docs_ref, acc_ref, stage_ref, in_sem, out_sem,
):
    half_rows = near_ref.shape[0]
    copies = [
        pltpu.make_async_copy(near_ref, docs_ref.at[pl.ds(0, half_rows)], in_sem.at[0]),
        pltpu.make_async_copy(far_ref, docs_ref.at[pl.ds(half_rows, half_rows)], in_sem.at[1]),
    ]
    for copy in copies:
        copy.start()
    chunk = stage_ref.shape[1]

    @pl.loop(0, 2 * half_rows // chunk)
    def _(i):
        acc_ref[pl.ds(pl.multiple_of(i * chunk, chunk), chunk), :] = jnp.zeros((chunk, PROJ), f32)

    for copy in copies:
        copy.wait()
    rows_all = length_ref.shape[0] // CAND
    lane = lax.broadcasted_iota(jnp.int32, (QLEN, PAIR), 1)

    @pl.loop(0, QH)
    def _(j):
        query = q_ref[j]
        starts, blocks, terms_of, logits = [], [], [], []
        for c in range(CAND):
            doc = cand_ref[j * CAND + c]
            row = doc // 8
            slot = doc % 8
            pair = slot // 2
            odd = slot % 2
            first = length_ref[row * 8 + 2 * pair]
            low = odd * first
            high = jnp.where(odd == 1, PAIR, first)
            start = pl.multiple_of((place_ref[(pair // 2) * rows_all + row] + pair % 2) * PAIR, PAIR)
            block = docs_ref[pl.ds(start, PAIR), :]
            scaled = mm(query, block, NT) * (1.0 / sim_temp)
            scaled = jnp.where((lane >= low) & (lane < high), scaled, masked_value)
            highest = jnp.max(scaled, -1, keepdims=True)
            terms = jnp.exp(scaled - highest)
            total = jnp.sum(terms, -1, keepdims=True)
            best = sim_temp * (highest + jnp.log(total))
            score = jnp.sum(best, 0, keepdims=True)
            logit = jnp.where(c < size_ref[j], score * (1.0 / loss_temp), masked_value)
            starts.append(start)
            blocks.append(block)
            terms_of.append(terms * (1.0 / total))
            logits.append(logit)
        top = functools.reduce(jnp.maximum, logits)
        norm = top + jnp.log(sum(jnp.exp(logit - top) for logit in logits))
        loss_ref[pl.ds(j, 1), :] = jnp.broadcast_to(norm - logits[0], (1, 128))
        dq = jnp.zeros((QLEN, PROJ), f32)
        for c in range(CAND):
            pull = (jnp.exp(logits[c] - norm) - (1.0 if c == 0 else 0.0)) * (1.0 / loss_temp)
            dsim = (pull * terms_of[c]).astype(bf16)
            dq += mm(dsim, blocks[c])
            acc_ref[pl.ds(starts[c], PAIR), :] += mm(dsim, query, TN)
        dq_ref[j] = dq

    steps = half_rows // chunk
    for part, out_ref in enumerate((send_ref, keep_ref)):
        base = half_rows * (1 - part)

        @pl.loop(0, steps)
        def _(i):
            slot = i % 2
            target = out_ref.at[pl.ds(pl.multiple_of(i * chunk, chunk), chunk)]

            @pl.when(i >= 2)
            def _():
                pltpu.make_async_copy(stage_ref.at[slot], target, out_sem.at[slot]).wait()

            stage_ref[slot] = acc_ref[pl.ds(pl.multiple_of(base + i * chunk, chunk), chunk), :].astype(bf16)
            pltpu.make_async_copy(stage_ref.at[slot], target, out_sem.at[slot]).start()

        for slot in range(2):
            pltpu.make_async_copy(stage_ref.at[slot], out_ref.at[pl.ds(0, chunk)], out_sem.at[slot]).wait()


def score(cands, sizes, lengths, places, queries, near, far):
    half_rows = near.shape[0]
    chunk = 1024
    anywhere = pl.BlockSpec(memory_space=pl.ANY)
    return pl.pallas_call(
        score_kernel,
        grid_spec=pltpu.PrefetchScalarGridSpec(
            num_scalar_prefetch=4,
            grid=(1,),
            in_specs=[whole((QH, QLEN, PROJ)), anywhere, anywhere],
            out_specs=[whole((QH, 128)), whole((QH, QLEN, PROJ)), anywhere, anywhere],
            scratch_shapes=[
                pltpu.VMEM((2 * half_rows, PROJ), bf16),
                pltpu.VMEM((2 * half_rows, PROJ), f32),
                pltpu.VMEM((2, chunk, PROJ), bf16),
                pltpu.SemaphoreType.DMA((2,)),
                pltpu.SemaphoreType.DMA((2,)),
            ],
        ),
        out_shape=[
            jax.ShapeDtypeStruct((QH, 128), f32),
            jax.ShapeDtypeStruct((QH, QLEN, PROJ), f32),
            jax.ShapeDtypeStruct((half_rows, PROJ), bf16),
            jax.ShapeDtypeStruct((half_rows, PROJ), bf16),
        ],
        compiler_params=params(62),
        cost_estimate=cost(3e10, 20 * MIB),
        name="score",
    )(cands, sizes, lengths, places, queries, near, far)


def head_kernel(
    grad_ref, proj_ref, wproj_ref, hat_ref, rstd_ref, gain_ref,
    dproj_ref, dresid_ref, dffn_ref, sums_ref,
):
    projected = proj_ref[...]
    grad = grad_ref[...]
    inverse = lax.rsqrt(jnp.sum(projected * projected, -1, keepdims=True) + vector_eps)
    inner = jnp.sum(projected * grad, -1, keepdims=True)
    dproj = (grad * inverse - projected * (inner * inverse * inverse * inverse)).astype(bf16)
    dproj_ref[...] = dproj
    dfinal = mm(dproj, wproj_ref[...], NT)
    hat = hat_ref[...]
    dresid = norm_back(dfinal, hat, rstd_ref[:, :1], gain_ref[...].astype(f32))
    dresid_ref[...] = dresid
    dffn = dresid.astype(bf16)
    dffn_ref[...] = dffn

    @pl.when(pl.program_id(0) == 0)
    def _():
        sums_ref[...] = jnp.zeros_like(sums_ref)

    sums_ref[0:1, :] += column_sum(dfinal * hat)
    sums_ref[1:2, :] += column_sum(dfinal)
    sums_ref[2:3, :] += column_sum(dffn.astype(f32))


def head_back(grad, projected, w_proj, hat, rstd, vectors):
    rows, width = hat.shape
    block = lambda cols: pl.BlockSpec((PAIR, cols), lambda i: (i, 0))
    return pl.pallas_call(
        head_kernel,
        grid=(rows // PAIR,),
        in_specs=[block(PROJ), block(PROJ), once((width, PROJ)), block(width), block(128),
                  vector_spec("gain_two", width)],
        out_specs=[block(PROJ), block(width), block(width), whole((8, width))],
        out_shape=[
            jax.ShapeDtypeStruct((rows, PROJ), bf16),
            jax.ShapeDtypeStruct((rows, width), f32),
            jax.ShapeDtypeStruct((rows, width), bf16),
            jax.ShapeDtypeStruct((8, width), f32),
        ],
        compiler_params=params(62),
        cost_estimate=cost(2 * rows * width * PROJ, 12 * MIB),
        name="head_back",
    )(grad, projected, w_proj, hat, rstd, vectors)


def active_back_kernel(dffn_ref, wdown_ref, der_ref, dup_ref, bup_ref):
    dactive = mm(dffn_ref[...], wdown_ref[...], NT)
    dup = (dactive * der_ref[...].astype(f32)).astype(bf16)
    dup_ref[...] = dup
    bup_ref[...] = column_sum(dup.astype(f32))


def active_back(dffn, w_down, der):
    rows, width = dffn.shape
    units = w_down.shape[0]
    step = 512
    cols = pl.BlockSpec((rows, step), lambda i: (0, i))
    return pl.pallas_call(
        active_back_kernel,
        grid=(units // step,),
        in_specs=[once((rows, width)), pl.BlockSpec((step, width), lambda i: (i, 0)), cols],
        out_specs=[cols, pl.BlockSpec((1, step), lambda i: (0, i))],
        out_shape=[jax.ShapeDtypeStruct((rows, units), bf16), jax.ShapeDtypeStruct((1, units), f32)],
        compiler_params=params(62),
        cost_estimate=cost(2 * rows * width * units, 27 * MIB),
        name="active_back",
    )(dffn, w_down, der)


def feed_back_kernel(
    dup_ref, wup_ref, dresid2_ref, hat_ref, rstd_ref, gain_ref, wo_ref,
    dresid1_ref, dbranch_ref, datt_ref, sums_ref, acc_ref,
):
    step = pl.program_id(0)
    part = mm(dup_ref[...], wup_ref[...], NT)

    @pl.when(step == 0)
    def _():
        acc_ref[...] = part

    @pl.when(step > 0)
    def _():
        acc_ref[...] += part

    @pl.when(step == pl.num_programs(0) - 1)
    def _():
        sums = [0.0, 0.0, 0.0]
        for at in range(0, acc_ref.shape[0], PAIR):
            span = slice(at, at + PAIR)
            dnormed = acc_ref[span, :] + dresid2_ref[span, :]
            hat = hat_ref[span, :]
            dresid = norm_back(dnormed, hat, rstd_ref[span, :1], gain_ref[...].astype(f32))
            dresid1_ref[span, :] = dresid
            dbranch = dresid.astype(bf16)
            dbranch_ref[span, :] = dbranch
            datt_ref[span, :] = mm(dbranch, wo_ref[...], NT).astype(bf16)
            sums[0] += column_sum(dnormed * hat)
            sums[1] += column_sum(dnormed)
            sums[2] += column_sum(dbranch.astype(f32))
        for i in range(3):
            sums_ref[i : i + 1, :] = sums[i]


def feed_back(dup, w_up, dresid2, hat, rstd, w_out, vectors):
    rows, width = hat.shape
    units = w_up.shape[1]
    step = 1024
    return pl.pallas_call(
        feed_back_kernel,
        grid=(units // step,),
        in_specs=[
            pl.BlockSpec((rows, step), lambda i: (0, i)),
            pl.BlockSpec((width, step), lambda i: (0, i)),
            once((rows, width)), once((rows, width)), once((rows, 128)), vector_spec("gain_one", width),
            once((width, width)),
        ],
        out_specs=[whole((rows, width)), whole((rows, width)), whole((rows, width)), whole((8, width))],
        out_shape=[
            jax.ShapeDtypeStruct((rows, width), f32),
            jax.ShapeDtypeStruct((rows, width), bf16),
            jax.ShapeDtypeStruct((rows, width), bf16),
            jax.ShapeDtypeStruct((8, width), f32),
        ],
        scratch_shapes=[pltpu.VMEM((rows, width), f32)],
        compiler_params=params(62),
        cost_estimate=cost(2 * rows * width * units, 36 * MIB),
        name="feed_back",
    )(dup, w_up, dresid2, hat, rstd, vectors, w_out)


def attend_back_kernel(info_ref, qkv_ref, datt_ref, cos_ref, sin_ref, dmixed_ref, sums_ref, mask_ref):
    width = datt_ref.shape[1]
    cosine = cos_ref[...]
    sine = sin_ref[...]
    mask_ref[...] = jnp.where(same_segment(info_ref, pl.program_id(0)), 0.0, masked_value)
    lane = lax.broadcasted_iota(jnp.int32, (PAIR, 2 * HD), 1)

    @pl.when(pl.program_id(0) == 0)
    def _():
        sums_ref[...] = jnp.zeros_like(sums_ref)

    for pair in range(width // (2 * HD)):
        at = pair * 2 * HD
        query = qkv_ref[:, at : at + 2 * HD]
        key = qkv_ref[:, width + at : width + at + 2 * HD]
        value = qkv_ref[:, 2 * width + at : 2 * width + at + 2 * HD]
        datt = datt_ref[:, at : at + 2 * HD]
        dquery = dkey = dvalue = None
        for head in range(2):
            mine = (lane < HD) if head == 0 else (lane >= HD)
            zero = jnp.zeros_like(key)
            query_h = jnp.where(mine, query, zero)
            key_h = jnp.where(mine, key, zero)
            datt_h = jnp.where(mine, datt, zero)
            scores = mm(key, query_h, NT) + mask_ref[...]
            terms = jnp.exp(scores - jnp.max(scores, 0, keepdims=True))
            weights = terms * (1.0 / jnp.sum(terms, 0, keepdims=True))
            dweights = mm(value, datt_h, NT)
            inner = jnp.sum(weights * dweights, 0, keepdims=True)
            dscores = (weights * (dweights - inner)).astype(bf16)
            dv = mm(weights.astype(bf16), datt_h)
            dk = mm(dscores, query_h)
            dq = mm(dscores, key_h, TN)
            dquery = dq if head == 0 else dquery + dq
            dkey = dk if head == 0 else dkey + dk
            dvalue = dv if head == 0 else dvalue + dv
        dquery = dquery * score_scale
        dquery = dquery * cosine - partner(dquery) * sine
        dkey = dkey * cosine - partner(dkey) * sine
        for i, grad in enumerate((dquery, dkey, dvalue)):
            low = grad.astype(bf16)
            dmixed_ref[:, i * width + at : i * width + at + 2 * HD] = low
            sums_ref[:, i * width + at : i * width + at + 2 * HD] += column_sum(low.astype(f32))


def attend_back(info, qkv, datt, cosine, sine):
    rows, width = datt.shape
    block = lambda cols: pl.BlockSpec((PAIR, cols), lambda i, *_: (i, 0))
    return pl.pallas_call(
        attend_back_kernel,
        grid_spec=pltpu.PrefetchScalarGridSpec(
            num_scalar_prefetch=1,
            grid=(rows // PAIR,),
            in_specs=[block(3 * width), block(width), block(2 * HD), block(2 * HD)],
            out_specs=[block(3 * width), whole((1, 3 * width))],
            scratch_shapes=[pltpu.VMEM((PAIR, PAIR), f32)],
        ),
        out_shape=[jax.ShapeDtypeStruct((rows, 3 * width), bf16), jax.ShapeDtypeStruct((1, 3 * width), f32)],
        compiler_params=params(62),
        cost_estimate=cost(2e10, 16 * MIB),
        name="attend_back",
    )(info, qkv, datt, cosine, sine)


def input_grad_kernel(dmixed_ref, w_ref, dresid_ref, out_ref):
    out_ref[...] = dresid_ref[...] + mm(dmixed_ref[...], w_ref[...], NT)


def input_grad(dmixed, w_qkv, dresid):
    rows, width = dresid.shape
    block = lambda cols: pl.BlockSpec((PAIR, cols), lambda i: (i, 0))
    return pl.pallas_call(
        input_grad_kernel,
        grid=(rows // PAIR,),
        in_specs=[block(3 * width), once((width, 3 * width)), block(width)],
        out_specs=block(width),
        out_shape=jax.ShapeDtypeStruct((rows, width), f32),
        compiler_params=params(62),
        cost_estimate=cost(6 * rows * width * width, 20 * MIB),
        name="input_grad",
    )(dmixed, w_qkv, dresid)


def place_blocks(value_ref, slots, received, out_refs):
    for slot, block in slots:
        each = out_refs[0].shape[-2]
        value = value_ref[pl.ds(pl.multiple_of(block * each, each), each), :]
        if received is None:
            out_refs[0][slot] = value
        else:
            value = value + received[slot]
            half = out_refs[0].shape[0]
            if slot < half:
                out_refs[0][slot] = value
            else:
                at = slot - half
                out_refs[1 + at // (half // 2)][at % (half // 2)] = value.astype(bf16)


def outer_cols_kernel(counts, keep, order_ref, *refs):
    used = 2 * len(counts)
    received = refs[used] if keep else None
    out_refs, value_ref = refs[used + 1 if keep else used : -1], refs[-1]
    step = pl.program_id(0)
    slots = (received if keep else out_refs[0]).shape[0]
    done = 0
    for i, count in enumerate(counts):

        @pl.when((step >= done) & (step < done + count))
        def _(left_ref=refs[2 * i], right_ref=refs[2 * i + 1]):
            value_ref[...] = mm(left_ref[...], right_ref[...], TN)

        done += count
    place_blocks(value_ref, [(k, order_ref[1 + k]) for k in range(slots)], received, out_refs)


def outer_cols(order, pairs, received=None, step=512):
    slots = order.shape[0] - 1
    rows = pairs[0][0].shape[1] // 2
    each = rows // slots
    keep = received is not None
    specs, args, counts = [], [], []
    for left, right in pairs:
        count = right.shape[1] // step
        first = sum(counts)
        specs.append(pl.BlockSpec((left.shape[0], rows), lambda i, order: (0, order[0]), pipeline_mode=pl.Buffered(1)))
        specs.append(
            pl.BlockSpec(
                (right.shape[0], step),
                lambda i, *_, first=first, count=count: (0, jnp.clip(i - first, 0, count - 1)),
            )
        )
        args += [left, right]
        counts.append(count)
    cols = sum(counts) * step
    spec = lambda count: pl.BlockSpec((count, each, step), lambda i, *_: (0, 0, i))
    shape = lambda count, kind: jax.ShapeDtypeStruct((count, each, cols), kind)
    if keep:
        specs.append(spec(slots))
        args.append(received)
        outs = [spec(slots // 2), spec(slots // 4), spec(slots // 4)]
        shapes = [shape(slots // 2, f32), shape(slots // 4, bf16), shape(slots // 4, bf16)]
    else:
        outs, shapes = [spec(slots)], [shape(slots, f32)]
    out = pl.pallas_call(
        functools.partial(outer_cols_kernel, counts, keep),
        grid_spec=pltpu.PrefetchScalarGridSpec(
            num_scalar_prefetch=1, grid=(sum(counts),), in_specs=specs, out_specs=outs,
            scratch_shapes=[pltpu.VMEM((rows, step), f32)],
        ),
        out_shape=shapes,
        compiler_params=params(62),
        cost_estimate=cost(2 * args[0].shape[0] * rows * cols, (20 if keep else 15) * MIB),
        name="outer_cols",
    )(order, *args)
    return out if keep else out[0]


def outer_rows_kernel(group, keep, order_ref, left_ref, right_ref, final_ref, dproj_ref, *refs):
    received = refs[0] if keep else None
    out_refs, value_ref, proj_ref = refs[1 if keep else 0 : -2], refs[-2], refs[-1]
    value_ref[...] = mm(left_ref[...], right_ref[...], TN)
    proj_ref[...] = mm(final_ref[...], dproj_ref[...], TN)
    _, tall, width = value_ref.shape[0], out_refs[0].shape[-2], value_ref.shape[1]
    each = value_ref.shape[0] // group
    short = proj_ref.shape[0] // group
    pieces = width // PROJ
    half = group // 2
    for j in range(group):
        block = order_ref[1 + pl.program_id(0) * group + j]
        value = value_ref[pl.ds(pl.multiple_of(block * each, each), each), :]
        small = proj_ref[pl.ds(pl.multiple_of(block * short, short), short), :]
        fold = short // pieces if short >= pieces else 1
        low = [small[i * fold : (i + 1) * fold, :] for i in range(short // fold)]
        if keep:
            value = value + received[j, 0, :each, :]
            low = [
                part + received[j, 0, each : each + fold, i * PROJ : (i + 1) * PROJ] for i, part in enumerate(low)
            ]
            out_ref, at = (out_refs[0], j) if j < half else (out_refs[1 + 2 * (j - half) // half], j % (half // 2))
        else:
            out_ref, at = out_refs[0], j
        kind = out_ref.dtype
        out_ref[at, 0, :each, :] = value.astype(kind)
        out_ref[at, 0, each:, :] = jnp.zeros((tall - each, width), kind)
        for i, part in enumerate(low):
            out_ref[at, 0, each : each + fold, i * PROJ : (i + 1) * PROJ] = part.astype(kind)


def outer_rows(order, left, right, final, dproj, slots, group, received=None):
    tokens_here, rows = left.shape
    width = right.shape[1]
    rest = slots // group
    each = rows // (2 * slots)
    tall = each + 16
    keep = received is not None
    spec = lambda count: pl.BlockSpec((count, 1, tall, width), lambda i, *_: (0, i, 0, 0))
    shape = lambda count, kind: jax.ShapeDtypeStruct((count, rest, tall, width), kind)
    cols = lambda i, order: (0, order[0] * rest + order[1 + slots + i])
    specs = [
        pl.BlockSpec((tokens_here, group * each), cols),
        once((tokens_here, width)),
        pl.BlockSpec((tokens_here, final.shape[1] // (2 * rest)), cols),
        once((tokens_here, PROJ)),
    ]
    args = [left, right, final, dproj]
    if keep:
        specs.append(spec(group))
        args.append(received.reshape(group, rest, tall, width))
        outs = [spec(group // 2), spec(group // 4), spec(group // 4)]
        shapes = [shape(group // 2, f32), shape(group // 4, bf16), shape(group // 4, bf16)]
    else:
        outs, shapes = [spec(group)], [shape(group, f32)]
    out = pl.pallas_call(
        functools.partial(outer_rows_kernel, group, keep),
        grid_spec=pltpu.PrefetchScalarGridSpec(
            num_scalar_prefetch=1, grid=(rest,), in_specs=specs, out_specs=outs,
            scratch_shapes=[
                pltpu.VMEM((group * each, width), f32),
                pltpu.VMEM((final.shape[1] // (2 * rest), PROJ), f32),
            ],
        ),
        out_shape=shapes,
        compiler_params=params(62),
        cost_estimate=cost(tokens_here * rows * width, (20 if keep else 15) * MIB),
        name="outer_rows",
    )(order, *args)
    out = [o.reshape(-1, tall, width) for o in out]
    return out if keep else out[0]


def flips(count):
    bits = [1 << i for i in range(count.bit_length() - 1)]
    third = {16: 1, 64: 2}[count]
    swapped = bits[third : 2 * third] + bits[:third] + bits[2 * third :][::-1]
    return bits, swapped


def slot_of(rel, order):
    slot = jnp.zeros_like(rel)
    for i, flip in enumerate(order):
        slot = slot + ((rel // flip) % 2) * (1 << (len(order) - 1 - i))
    return slot


def rel_of(slot, order):
    rel = jnp.zeros_like(slot)
    for i, flip in enumerate(order):
        rel = rel + ((slot >> (len(order) - 1 - i)) % 2) * flip
    return rel


def hop(values, stage, count):
    pairs = []
    for stream, order in enumerate(flips(count)):
        pairs += [(stream * count + i, stream * count + (i ^ order[stage])) for i in range(count)]
    return lax.ppermute(values, ("stream", "dp"), pairs)


def swap(values):
    return lax.ppermute(values, "stream", [(0, 1), (1, 0)])


def after(value, *others):
    return lax.optimization_barrier((value, *others))[0]


def gather_rows(values, count):
    for stage in reversed(range(count.bit_length() - 1)):
        values = jnp.concatenate([values, hop(values, stage, count)], 0)
    return values


def take_in(keep, got):
    half = keep.shape[0] // 2
    if half == 0:
        return keep[0] + got[0].astype(f32), None
    return keep[:half] + got[:half].astype(f32), (keep[half:] + got[half:].astype(f32)).astype(bf16)


def scatter_sum(keep, send, stage, count, got=None):
    if got is not None:
        keep, send = take_in(keep, got)
    while send is not None:
        keep, send = take_in(keep, hop(send, stage, count))
        stage += 1
    return keep


def total_sum(values, stage, count):
    for later in range(stage, count.bit_length() - 1):
        values = values + hop(values, later, count)
    return values


def body(
    tokens, doc_lengths, cand_docs, group_sizes, w_qkv, b_qkv, w_attn_out, b_attn_out, gain_one, bias_one,
    w_up, b_up, w_down, b_down, gain_two, bias_two, w_proj,
):
    stream = lax.axis_index("stream")
    me = lax.axis_index("dp")
    count = lax.axis_size("dp")
    hidden = tokens[0]
    rows, width = hidden.shape
    half = rows // 2
    first_lengths = lax.dynamic_slice_in_dim(doc_lengths, me, 1, 0)[0].reshape(-1, 2)[:, 0]
    info = jnp.concatenate([stream[None], first_lengths]).astype(jnp.int32)
    cosine, sine = tables_here(stream, first_lengths)
    vectors = jnp.concatenate([b_qkv, b_attn_out, gain_one, bias_one, b_down, gain_two, bias_two, b_up])[None, :]
    orders = flips(count)
    group = {16: 4, 64: 16}[count]
    rest = count // group
    index = jnp.arange(count, dtype=jnp.int32)
    core = jnp.arange(2, dtype=jnp.int32)[:, None]
    slots = jnp.stack([slot_of(index ^ me, order) for order in orders])
    places = (((core ^ stream) * count + slots) * 2).reshape(-1)
    owners = jnp.stack([me ^ rel_of(index, order) for order in orders])
    owners_send, owners_keep = jnp.where(stream == 0, owners[::-1], owners)
    cols_orders, rows_orders = [], []
    for target, owner in ((1 - stream, owners_send), (stream, owners_keep)):
        grid = owner.reshape(group, rest)
        cols_orders.append(jnp.concatenate([target[None], owner]))
        rows_orders.append(jnp.concatenate([target[None], (grid % group).T.reshape(-1), grid[0] // group]))

    qkv, attended, hat1, rstd1, normed = attend(info, hidden, w_qkv, cosine, sine, w_attn_out, vectors)
    active, der, hat2, rstd2, final, projected, vecs = feed(normed, w_up, w_down, hat1, w_proj, vectors)

    on_docs = stream == 1
    other = swap(jnp.where(on_docs, vecs[:half], vecs[half:]))
    own_docs = jnp.where(on_docs, vecs[half:], other)
    queries = jnp.where(on_docs, other, vecs[:half]).reshape(QH, QLEN, PROJ)
    near = gather_rows(own_docs, count)
    far = swap(near)
    loss, dqueries, keep, send = score(
        cand_docs.reshape(-1), group_sizes.reshape(-1), doc_lengths.reshape(-1), places, queries, near, far
    )
    keep = keep.reshape(count, half, PROJ).astype(f32)
    keep, send = take_in(keep, swap(send).reshape(count, half, PROJ))
    ddocs = scatter_sum(keep, send, 0, count)
    dqueries = dqueries.reshape(half, PROJ)
    back = swap(jnp.where(on_docs, dqueries, ddocs))
    grad_vectors = jnp.where(
        on_docs, jnp.concatenate([back, ddocs], 0), jnp.concatenate([dqueries, back], 0)
    )

    hold = lax.optimization_barrier

    def wide(sums):
        return [b.reshape(2 * count, -1) for b in sums]

    def add_first(keep, got):
        half = keep.shape[0] // 2
        return (keep[half:] + got.astype(f32)).astype(bf16)

    def add_second(keep, got):
        half = keep.shape[0] // 2
        return keep[:half] + got.astype(f32)

    dproj, dresid2, dffn, sums2 = head_back(grad_vectors, projected, w_proj, hat2, rstd2, vectors)
    down = lambda side, left, received=None: outer_rows(
        rows_orders[side], left, dffn, final, dproj, count, group, received
    )
    up = lambda side, left, received=None: outer_cols(cols_orders[side], [(left, dup)], received)
    mix = lambda side, left, received=None: outer_cols(
        cols_orders[side], [(left, dmixed), (attended, dbranch)], received
    )

    d_out = down(0, active)
    d_got = swap(d_out)
    dffn_, d_out = hold((dffn, d_out))
    dup, sum_up = active_back(dffn_, w_down, der)
    active_, d_got, dup = hold((active, d_got, dup))
    d_keep, d_low, d_high = down(1, active_, d_got)
    d_high, d_low, normed_, d_keep = hold((d_high, d_low, normed, d_keep))
    d_high_got, d_low_got = hop(d_high, 0, count), hop(d_low, 0, count)
    u_out = up(0, normed_)
    d_keep, d_high_got, u_out = hold((d_keep, d_high_got, u_out))
    d_send = add_first(d_keep, d_high_got)
    d_send, u_out, dup_ = hold((d_send, u_out, dup))
    d_got, u_got = hop(d_send, 1, count), swap(u_out)
    dresid1, dbranch, dattended, sums1 = feed_back(dup_, w_up, dresid2, hat1, rstd1, w_attn_out, vectors)
    d_keep, d_low_got, d_got, dbranch = hold((d_keep, d_low_got, d_got, dbranch))
    d_keep, d_send = take_in(add_second(d_keep, d_low_got), d_got)
    early = [sums1[2], sums1[0], sums1[1], sum_up[0], sums2[2], sums2[0], sums2[1]]
    table = jnp.concatenate(wide(early), 1)
    d_keep, d_send, table, normed_, u_got = hold((d_keep, d_send, table, normed, u_got))
    d_got, t_got = hop(d_send, 2, count), swap(table)
    u_keep, u_low, u_high = up(1, normed_, u_got)
    d_keep, d_got, table, t_got, u_keep = hold((d_keep, d_got, table, t_got, u_keep))
    d_keep, d_send = take_in(d_keep, d_got)
    table = table + t_got
    u_high, u_low, d_keep, d_send, table, dattended = hold((u_high, u_low, d_keep, d_send, table, dattended))
    u_high_got, u_low_got = hop(u_high, 0, count), hop(u_low, 0, count)
    d_got, t_got = hop(d_send, 3, count), hop(table, 0, count)
    dmixed, sum_qkv = attend_back(info, qkv, dattended, cosine, sine)
    d_keep, d_got, table, t_got, u_keep, u_high_got, u_low_got, dmixed = hold(
        (d_keep, d_got, table, t_got, u_keep, u_high_got, u_low_got, dmixed)
    )
    g_down = scatter_sum(d_keep, d_send, 4, count, d_got)
    u_send = add_first(u_keep, u_high_got)
    u_keep = add_second(u_keep, u_low_got)
    table = table + t_got
    late = wide([sum_qkv[0]])[0]
    g_down, u_send, u_keep, table, late, hidden_ = hold((g_down, u_send, u_keep, table, late, hidden))
    u_got, t_got, l_got = hop(u_send, 1, count), hop(table, 1, count), swap(late)
    m_out = mix(0, hidden_)
    u_keep, u_got, table, t_got, late, l_got, m_out = hold((u_keep, u_got, table, t_got, late, l_got, m_out))
    u_keep, u_send = take_in(u_keep, u_got)
    table, late = table + t_got, late + l_got
    u_keep, u_send, table, late, m_out, dmixed_ = hold((u_keep, u_send, table, late, m_out, dmixed))
    m_got, u_got, t_got, l_got = swap(m_out), hop(u_send, 2, count), hop(table, 2, count), hop(late, 0, count)
    grad_hidden = input_grad(dmixed_, w_qkv, dresid1)
    u_keep, u_got, table, t_got, late, l_got, grad_hidden = hold(
        (u_keep, u_got, table, t_got, late, l_got, grad_hidden)
    )
    u_keep, u_send = take_in(u_keep, u_got)
    table, late = table + t_got, late + l_got
    u_keep, u_send, table, late, hidden_, m_got = hold((u_keep, u_send, table, late, hidden, m_got))
    u_got, t_got, l_got = hop(u_send, 3, count), hop(table, 3, count), hop(late, 1, count)
    m_keep, m_low, m_high = mix(1, hidden_, m_got)
    u_keep, u_got, table, t_got, late, l_got, m_keep = hold((u_keep, u_got, table, t_got, late, l_got, m_keep))
    late = late + l_got
    m_high, m_low, late = hold((m_high, m_low, late))
    m_high_got, m_low_got, l_got = hop(m_high, 0, count), hop(m_low, 0, count), hop(late, 2, count)
    g_up = scatter_sum(u_keep, u_send, 4, count, u_got)
    table = total_sum(table + t_got, 4, count)
    late = total_sum(late + l_got, 3, count)
    m_send = add_first(m_keep, m_high_got)
    m_keep, m_low_got, m_send = hold((m_keep, m_low_got, m_send))
    m_got = hop(m_send, 1, count)
    m_keep, m_send = take_in(add_second(m_keep, m_low_got), m_got)
    g_mix = scatter_sum(m_keep, m_send, 2, count)

    me_all = stream * count + me
    mine = lax.dynamic_slice_in_dim(table, me_all, 1, 0)[0]
    parts, at = [], 0
    for b in early:
        size = b.shape[0] // (2 * count)
        parts.append(mine[at : at + size])
        at += size
    g_bout, g_gain1, g_bias1, g_bup, g_bdown, g_gain2, g_bias2 = parts
    g_bqkv = lax.dynamic_slice_in_dim(late, me_all, 1, 0)[0]
    tall = w_down.shape[0] // (2 * count)
    short = width // (2 * count)
    pieces = width // PROJ
    fold = max(short // pieces, 1)
    g_proj = g_down[tall : tall + fold].reshape(fold, pieces, PROJ).transpose(1, 0, 2)[: short // fold].reshape(short, PROJ)
    return (
        loss[:, 0][None, None, :],
        grad_hidden[None],
        g_mix[:, : 3 * width],
        g_bqkv,
        g_mix[:, 3 * width :],
        g_bout,
        g_gain1,
        g_bias1,
        g_up,
        g_bup,
        g_down[:tall],
        g_bdown,
        g_gain2,
        g_bias2,
        g_proj,
    )


def solution(mesh):
    every = P(("stream", "dp"))
    rows = P(("stream", "dp"), None)
    return jax.shard_map(
        body,
        mesh=mesh,
        in_specs=(P("stream", "dp", None), P(), P("dp", "stream", None, None), P("dp", "stream", None)) + (P(),) * 13,
        out_specs=(
            P("dp", "stream", None), P("stream", "dp", None), rows, every, rows, every, every, every, rows, every,
            rows, every, every, every, rows,
        ),
        check_vma=False,
    )
```

```python
import functools
import math

import jax
import jax.numpy as jnp
import numpy as np
from jax import lax
from jax.experimental import pallas as pl
from jax.experimental.pallas import tpu as pltpu
from jax.sharding import PartitionSpec as P

HD = 64
PROJ = 128
QLEN = 32
CAND = 8
QH = 16
PAIR = 256

score_scale = 0.125
sim_temp = 0.05
loss_temp = 0.08
masked_value = -1e30
norm_eps = 1e-05
vector_eps = 1e-06

f32 = jnp.float32
bf16 = jnp.bfloat16
MIB = 1 << 20

NN = (((1,), (0,)), ((), ()))
NT = (((1,), (1,)), ((), ()))
TN = (((0,), (0,)), ((), ()))


def mm(left, right, dims=NN):
    return lax.dot_general(left, right, dims, preferred_element_type=f32)


def params(mib):
    return pltpu.CompilerParams(vmem_limit_bytes=mib * MIB)


def cost(flops, moved):
    return pl.CostEstimate(flops=int(flops), bytes_accessed=int(moved), transcendentals=0)


def whole(shape):
    return pl.BlockSpec(shape, lambda *_: (0,) * len(shape))


def vector(length):
    return pl.BlockSpec((length,), lambda *_: (0,), pipeline_mode=pl.Buffered(1))


def line(ref):
    return ref[...].astype(f32)[None, :]


def once(shape):
    return pl.BlockSpec(shape, lambda *_: (0,) * len(shape), pipeline_mode=pl.Buffered(1))


def rotation_tables():
    freq = np.exp(np.arange(HD // 2) * (-2.0 * math.log(10000.0) / HD))
    lane = np.arange(2 * HD)
    place = np.concatenate([np.arange(PAIR) % QLEN, np.arange(PAIR), np.arange(PAIR)])
    angle = place[:, None] * freq[lane % (HD // 2)][None, :]
    sign = np.where(lane % HD < HD // 2, -1.0, 1.0)[None, :]
    return np.cos(angle).astype(np.float32), (np.sin(angle) * sign).astype(np.float32)


def first_length(ids_ref, lengths_ref, block):
    return lengths_ref[ids_ref[1], 2 * block]


def table_here(ids_ref, lengths_ref, table_ref, block):
    first = first_length(ids_ref, lengths_ref, block)
    row = lax.broadcasted_iota(jnp.int32, (PAIR, 2 * HD), 0)
    moved = table_ref[pl.ds(2 * PAIR - first, PAIR), :]
    doc = jnp.where(row < first, table_ref[PAIR : 2 * PAIR, :], moved)
    return jnp.where(ids_ref[0] == 1, doc, table_ref[:PAIR, :])


def partner(values):
    lane = lax.broadcasted_iota(jnp.int32, values.shape, 1)
    ahead = pltpu.roll(values, 2 * HD - HD // 2, 1)
    behind = pltpu.roll(values, HD // 2, 1)
    return jnp.where(lane % HD < HD // 2, ahead, behind)


def same_segment(ids_ref, lengths_ref, block):
    is_doc = ids_ref[0] == 1
    first = first_length(ids_ref, lengths_ref, block)
    row = lax.broadcasted_iota(jnp.int32, (PAIR, PAIR), 0)
    col = lax.broadcasted_iota(jnp.int32, (PAIR, PAIR), 1)
    doc = ((row >= first) ^ (col >= first)).astype(jnp.int32)
    query = ((row // QLEN) ^ (col // QLEN)).astype(jnp.int32)
    return jnp.where(is_doc, doc, query) == 0


def normalise(values):
    mean = jnp.mean(values, -1, keepdims=True)
    center = values - mean
    rstd = lax.rsqrt(jnp.mean(center * center, -1, keepdims=True) + norm_eps)
    return center * rstd, rstd


def norm_back(grad, hat, rstd, gain):
    scaled = grad * gain
    return (
        scaled - jnp.mean(scaled, -1, keepdims=True) - hat * jnp.mean(scaled * hat, -1, keepdims=True)
    ) * rstd


def column_sum(values):
    return jnp.sum(values, 0, keepdims=True)


def attend_kernel(
    ids_ref, lengths_ref, x_ref, wqkv_ref, bqkv_ref, cos_ref, sin_ref, wo_ref, bo_ref, g_ref, c_ref,
    qkv_ref, att_ref, hat_ref, rstd_ref, normb_ref, mask_ref,
):
    width = x_ref.shape[1]
    x = x_ref[...]
    block = pl.program_id(0)
    cosine = table_here(ids_ref, lengths_ref, cos_ref, block)
    sine = table_here(ids_ref, lengths_ref, sin_ref, block)
    step = 256
    for start in range(0, 3 * width, step):
        mixed = mm(x, wqkv_ref[:, start : start + step]) + bqkv_ref[start : start + step].astype(f32)[None, :]
        if start < 2 * width:
            parts = []
            for off in range(0, step, 2 * HD):
                one = mixed[:, off : off + 2 * HD]
                one = one * cosine + partner(one) * sine
                parts.append(one.astype(bf16))
            mixed = jnp.concatenate(parts, 1)
            if start < width:
                mixed = mixed * jnp.asarray(score_scale, bf16)
        qkv_ref[:, start : start + step] = mixed.astype(bf16)
    mask_ref[...] = jnp.where(same_segment(ids_ref, lengths_ref, pl.program_id(0)), 0.0, masked_value)
    lane = lax.broadcasted_iota(jnp.int32, (PAIR, 2 * HD), 1)
    for pair in range(width // (2 * HD)):
        at = pair * 2 * HD
        query = qkv_ref[:, at : at + 2 * HD]
        key = qkv_ref[:, width + at : width + at + 2 * HD]
        value = qkv_ref[:, 2 * width + at : 2 * width + at + 2 * HD]
        total = None
        for head in range(2):
            mine = (lane < HD) if head == 0 else (lane >= HD)
            zero = jnp.zeros_like(key)
            scores = mm(query, jnp.where(mine, key, zero), NT) + mask_ref[...]
            highest = jnp.max(scores, -1, keepdims=True)
            terms = jnp.exp(scores - highest)
            weights = (terms * (1.0 / jnp.sum(terms, -1, keepdims=True))).astype(bf16)
            part = mm(weights, jnp.where(mine, value, zero))
            total = part if total is None else total + part
        att_ref[:, at : at + 2 * HD] = total.astype(bf16)
    branch = mm(att_ref[...], wo_ref[...]) + line(bo_ref)
    hat, rstd = normalise(x.astype(f32) + branch)
    hat_ref[...] = hat
    rstd_ref[...] = jnp.broadcast_to(rstd, rstd_ref.shape)
    normb_ref[...] = (hat * line(g_ref) + line(c_ref)).astype(bf16)


def attend(ids, lengths, x, w_qkv, b_qkv, tables, w_out, b_out, gain, bias):
    rows, width = x.shape
    block = lambda cols: pl.BlockSpec((PAIR, cols), lambda i, *_: (i, 0))
    return pl.pallas_call(
        attend_kernel,
        grid_spec=pltpu.PrefetchScalarGridSpec(
            num_scalar_prefetch=2,
            grid=(rows // PAIR,),
            in_specs=[
                block(width), once((width, 3 * width)), vector(3 * width), once(tables[0].shape),
                once(tables[0].shape), once((width, width)), vector(width), vector(width), vector(width),
            ],
            out_specs=[block(3 * width), block(width), block(width), block(128), block(width)],
            scratch_shapes=[pltpu.VMEM((PAIR, PAIR), f32)],
        ),
        out_shape=[
            jax.ShapeDtypeStruct((rows, 3 * width), bf16),
            jax.ShapeDtypeStruct((rows, width), bf16),
            jax.ShapeDtypeStruct((rows, width), f32),
            jax.ShapeDtypeStruct((rows, 128), f32),
            jax.ShapeDtypeStruct((rows, width), bf16),
        ],
        compiler_params=params(62),
        cost_estimate=cost(2 * rows * width * 4 * width, 30 * MIB),
        name="attend",
    )(ids, lengths, x, w_qkv, b_qkv, *tables, w_out, b_out, gain, bias)


def feed_kernel(
    x_ref, wup_ref, bup_ref, wdown_ref, bdown_ref, hat1_ref, g1_ref, c1_ref, g2_ref, c2_ref, wproj_ref,
    act_ref, der_ref, hat2_ref, rstd2_ref, final_ref, proj_ref, vec_ref, acc_ref,
):
    step = pl.program_id(0)
    upward = mm(x_ref[...], wup_ref[...]) + line(bup_ref)
    below = 0.5 + 0.5 * lax.erf(upward * (2.0**-0.5))
    density = jnp.exp(-0.5 * upward * upward) * ((2.0 * math.pi) ** -0.5)
    active = (upward * below).astype(bf16)
    act_ref[...] = active
    der_ref[...] = (below + upward * density).astype(bf16)
    part = mm(active, wdown_ref[...])

    @pl.when(step == 0)
    def _():
        acc_ref[...] = part

    @pl.when(step > 0)
    def _():
        acc_ref[...] += part

    @pl.when(step == pl.num_programs(0) - 1)
    def _():
        for at in range(0, acc_ref.shape[0], PAIR):
            span = slice(at, at + PAIR)
            normed = hat1_ref[span, :] * line(g1_ref) + line(c1_ref)
            hat, rstd = normalise(normed + acc_ref[span, :] + line(bdown_ref))
            hat2_ref[span, :] = hat
            rstd2_ref[span, :] = jnp.broadcast_to(rstd, (PAIR, 128))
            final = (hat * line(g2_ref) + line(c2_ref)).astype(bf16)
            final_ref[span, :] = final
            projected = mm(final, wproj_ref[...])
            proj_ref[span, :] = projected
            inverse = lax.rsqrt(jnp.sum(projected * projected, -1, keepdims=True) + vector_eps)
            vec_ref[span, :] = (projected * inverse).astype(bf16)


def feed(x, w_up, b_up, w_down, b_down, hat1, g1, c1, g2, c2, w_proj):
    rows, width = x.shape
    units = w_up.shape[1]
    step = 512
    cols = pl.BlockSpec((rows, step), lambda i: (0, i))
    return pl.pallas_call(
        feed_kernel,
        grid=(units // step,),
        in_specs=[
            once((rows, width)),
            pl.BlockSpec((width, step), lambda i: (0, i)),
            pl.BlockSpec((step,), lambda i: (i,)),
            pl.BlockSpec((step, width), lambda i: (i, 0)),
            vector(width), once((rows, width)), vector(width), vector(width), vector(width), vector(width),
            once((width, PROJ)),
        ],
        out_specs=[cols, cols, whole((rows, width)), whole((rows, 128)), whole((rows, width)),
                   whole((rows, PROJ)), whole((rows, PROJ))],
        out_shape=[
            jax.ShapeDtypeStruct((rows, units), bf16),
            jax.ShapeDtypeStruct((rows, units), bf16),
            jax.ShapeDtypeStruct((rows, width), f32),
            jax.ShapeDtypeStruct((rows, 128), f32),
            jax.ShapeDtypeStruct((rows, width), bf16),
            jax.ShapeDtypeStruct((rows, PROJ), f32),
            jax.ShapeDtypeStruct((rows, PROJ), bf16),
        ],
        scratch_shapes=[pltpu.VMEM((rows, width), f32)],
        compiler_params=params(62),
        cost_estimate=cost(4 * rows * width * units, 50 * MIB),
        name="feed",
    )(x, w_up, b_up, w_down, b_down, hat1, g1, c1, g2, c2, w_proj)


UNROLL = 8


def load_docs(near_ref, far_ref, docs_ref, sem):
    half_rows = near_ref.shape[0]
    copies = [
        pltpu.make_async_copy(near_ref, docs_ref.at[pl.ds(0, half_rows)], sem.at[0]),
        pltpu.make_async_copy(far_ref, docs_ref.at[pl.ds(half_rows, half_rows)], sem.at[1]),
    ]
    for copy in copies:
        copy.start()
    return copies


def pair_scores(ids_ref, info_ref, length_ref, q_ref, docs_ref, entry, shape):
    count, levels = shape
    lane = lax.broadcasted_iota(jnp.int32, (QLEN, PAIR), 1)
    index = jnp.minimum(entry >> 3, q_ref.shape[0] - 1)
    doc = info_ref[index, entry & 7]
    row = doc >> 3
    pair = (doc >> 1) & 3
    first = length_ref[row, 2 * pair]
    odd = (doc & 1) == 1
    low = jnp.where(odd, first, 0)
    high = jnp.where(odd, PAIR, first)
    core = pair >> 1
    plane = 1 << levels
    rel = (row ^ ids_ref[1]) & (plane - 1)
    slot = choose(core, lambda order: slot_of(rel, order[:levels]), count)
    start = pl.multiple_of((((core ^ ids_ref[0]) * plane + slot) * 2 + (pair & 1)) * PAIR, PAIR)
    scaled = mm(q_ref[index], docs_ref[pl.ds(start, PAIR), :], NT) * (1.0 / sim_temp)
    return start, jnp.where((lane >= low) & (lane < high), scaled, masked_value)


def natural_row(ids_ref, entry, shape):
    count, levels = shape
    slot = entry >> (3 + QH.bit_length() - 1)
    rel = choose(ids_ref[0], lambda order: rel_of(slot, order[levels:]), count)
    z = (ids_ref[1] ^ rel) >> levels
    return z * QH + ((entry >> 3) & (QH - 1))


def score_kernel(
    shape, ids_ref, info_ref, length_ref, q_ref, near_ref, far_ref, score_ref, list_ref, docs_ref, sem,
):
    copies = load_docs(near_ref, far_ref, docs_ref, sem)
    count, levels = shape
    queries = q_ref.shape[0]
    score_ref[...] = jnp.zeros_like(score_ref)
    lane = lax.broadcasted_iota(jnp.int32, (1, 128), 1)
    z = ids_ref[1] >> levels

    def scan(q, found):
        size = info_ref[q, CAND]
        for c in range(CAND):
            here = ((info_ref[q, c] >> (3 + levels)) == z) & (c < size)
            list_ref[1 + found] = q * CAND + c
            found = found + here.astype(jnp.int32)
        return found

    found = lax.fori_loop(0, queries, scan, 0)
    list_ref[0] = found
    for u in range(UNROLL):
        list_ref[1 + found + u] = queries * CAND
    for j in range(QH):
        row = z * QH + j
        score_ref[pl.ds(row, 1), :] = jnp.where(lane == CAND, info_ref[j, CAND].astype(f32), 0.0)
    for copy in copies:
        copy.wait()

    @pl.loop(0, (found + UNROLL - 1) // UNROLL)
    def _(i):
        results = []
        for u in range(UNROLL):
            entry = list_ref[1 + i * UNROLL + u]
            _, scaled = pair_scores(ids_ref, info_ref, length_ref, q_ref, docs_ref, entry, shape)
            highest = jnp.max(scaled, -1, keepdims=True)
            total = jnp.sum(jnp.exp(scaled - highest), -1, keepdims=True)
            best = sim_temp * (highest + jnp.log(total))
            results.append((entry, jnp.sum(best, 0, keepdims=True)))
        for entry, result in results:
            row = jnp.where(entry >= queries * CAND, queries, natural_row(ids_ref, entry, shape))
            score_ref[pl.ds(row, 1), :] = jnp.where(lane == (entry & 7), result, score_ref[pl.ds(row, 1), :])


def score(ids, info, lengths, queries, near, far, shape):
    total = queries.shape[0]
    anywhere = pl.BlockSpec(memory_space=pl.ANY)
    return pl.pallas_call(
        functools.partial(score_kernel, shape),
        grid_spec=pltpu.PrefetchScalarGridSpec(
            num_scalar_prefetch=3,
            grid=(1,),
            in_specs=[whole(queries.shape), anywhere, anywhere],
            out_specs=[whole((total + 8, 128)), pl.BlockSpec(memory_space=pltpu.SMEM)],
            scratch_shapes=[pltpu.VMEM((2 * near.shape[0], PROJ), bf16), pltpu.SemaphoreType.DMA((2,))],
        ),
        out_shape=[
            jax.ShapeDtypeStruct((total + 8, 128), f32),
            jax.ShapeDtypeStruct((total * CAND + 2 * UNROLL,), jnp.int32),
        ],
        compiler_params=params(62),
        cost_estimate=cost(1e10, 4 * MIB),
        name="score",
    )(ids, info, lengths, queries, near, far)


def score_back_kernel(
    shape, ids_ref, info_ref, length_ref, list_ref, score_ref, q_ref, near_ref, far_ref,
    loss_ref, dq_keep_ref, dq_send_ref, keep_ref, send_ref, docs_ref, acc_ref, pull_ref, dq_ref, sem,
):
    copies = load_docs(near_ref, far_ref, docs_ref, sem)
    count, levels = shape
    queries = q_ref.shape[0]
    half_rows = near_ref.shape[0]
    scores = score_ref[:queries, :]
    lane = lax.broadcasted_iota(jnp.int32, (queries, 128), 1)
    size = jnp.sum(jnp.where(lane == CAND, scores, 0.0), -1, keepdims=True)
    counted = lane.astype(f32) < jnp.where(lane < CAND, size, 0.0)
    logits = jnp.where(counted, scores * (1.0 / loss_temp), masked_value)
    top = jnp.max(logits, -1, keepdims=True)
    norm = top + jnp.log(jnp.sum(jnp.exp(logits - top), -1, keepdims=True))
    positive = (lane == 0).astype(f32)
    pull_ref[:queries, :] = (jnp.exp(logits - norm) - positive) * (1.0 / loss_temp)
    pull_ref[queries:, :] = jnp.zeros((8, 128), f32)
    loss = norm - jnp.sum(logits * positive, -1, keepdims=True)
    loss_ref[...] = jnp.broadcast_to(loss, loss_ref.shape)
    dq_ref[...] = jnp.zeros_like(dq_ref)
    chunk = 512

    @pl.loop(0, 2 * half_rows // chunk)
    def _(i):
        acc_ref[pl.ds(pl.multiple_of(i * chunk, chunk), chunk), :] = jnp.zeros((chunk, PROJ), f32)

    for copy in copies:
        copy.wait()
    one = lax.broadcasted_iota(jnp.int32, (1, 128), 1)

    @pl.loop(0, (list_ref[0] + UNROLL - 1) // UNROLL)
    def _(i):
        results = []
        for u in range(UNROLL):
            entry = list_ref[1 + i * UNROLL + u]
            start, scaled = pair_scores(ids_ref, info_ref, length_ref, q_ref, docs_ref, entry, shape)
            terms = jnp.exp(scaled - jnp.max(scaled, -1, keepdims=True))
            row = jnp.where(entry >= queries * CAND, queries, natural_row(ids_ref, entry, shape))
            pull = jnp.sum(jnp.where(one == (entry & 7), pull_ref[pl.ds(row, 1), :], 0.0), -1, keepdims=True)
            dsim = (pull * (terms * (1.0 / jnp.sum(terms, -1, keepdims=True)))).astype(bf16)
            results.append((entry >> 3, start, dsim))
        for index, start, dsim in results:
            acc_ref[pl.ds(start, PAIR), :] += mm(dsim, q_ref[jnp.minimum(index, queries - 1)], TN)
            dq_ref[index] += mm(dsim, docs_ref[pl.ds(start, PAIR), :])

    near_q = dq_keep_ref.shape[0]
    dq_keep_ref[...] = dq_ref[:near_q]
    dq_send_ref[...] = dq_ref[near_q:queries].astype(bf16)

    @pl.loop(0, half_rows // chunk)
    def _(i):
        at = pl.multiple_of(i * chunk, chunk)
        keep_ref[pl.ds(at, chunk), :] = acc_ref[pl.ds(at, chunk), :]
        send_ref[pl.ds(at, chunk), :] = acc_ref[pl.ds(half_rows + at, chunk), :].astype(bf16)


def score_back(ids, info, lengths, entries, scores, queries, near, far, shape):
    total = queries.shape[0]
    half_rows = near.shape[0]
    anywhere = pl.BlockSpec(memory_space=pl.ANY)
    half = (total // 2, QLEN, PROJ)
    return pl.pallas_call(
        functools.partial(score_back_kernel, shape),
        grid_spec=pltpu.PrefetchScalarGridSpec(
            num_scalar_prefetch=4,
            grid=(1,),
            in_specs=[whole(scores.shape), whole(queries.shape), anywhere, anywhere],
            out_specs=[whole((total, 128)), whole(half), whole(half), whole((half_rows, PROJ)), whole((half_rows, PROJ))],
            scratch_shapes=[
                pltpu.VMEM((2 * half_rows, PROJ), bf16),
                pltpu.VMEM((2 * half_rows, PROJ), f32),
                pltpu.VMEM((total + 8, 128), f32),
                pltpu.VMEM((total + 1, QLEN, PROJ), f32),
                pltpu.SemaphoreType.DMA((2,)),
            ],
        ),
        out_shape=[
            jax.ShapeDtypeStruct((total, 128), f32),
            jax.ShapeDtypeStruct(half, f32),
            jax.ShapeDtypeStruct(half, bf16),
            jax.ShapeDtypeStruct((half_rows, PROJ), f32),
            jax.ShapeDtypeStruct((half_rows, PROJ), bf16),
        ],
        compiler_params=params(62),
        cost_estimate=cost(1e10, 8 * MIB),
        name="score_back",
    )(ids, info, lengths, entries, scores, queries, near, far)


def head_kernel(
    grad_ref, proj_ref, wproj_ref, hat_ref, rstd_ref, gain_ref,
    dproj_ref, dresid_ref, dffn_ref, sums_ref,
):
    projected = proj_ref[...]
    grad = grad_ref[...]
    inverse = lax.rsqrt(jnp.sum(projected * projected, -1, keepdims=True) + vector_eps)
    inner = jnp.sum(projected * grad, -1, keepdims=True)
    dproj = (grad * inverse - projected * (inner * inverse * inverse * inverse)).astype(bf16)
    dproj_ref[...] = dproj
    dfinal = mm(dproj, wproj_ref[...], NT)
    hat = hat_ref[...]
    dresid = norm_back(dfinal, hat, rstd_ref[:, :1], line(gain_ref))
    dresid_ref[...] = dresid
    dffn = dresid.astype(bf16)
    dffn_ref[...] = dffn

    @pl.when(pl.program_id(0) == 0)
    def _():
        sums_ref[...] = jnp.zeros_like(sums_ref)

    sums_ref[0:1, :] += column_sum(dfinal * hat)
    sums_ref[1:2, :] += column_sum(dfinal)
    sums_ref[2:3, :] += column_sum(dffn.astype(f32))


def head_back(grad, projected, w_proj, hat, rstd, gain):
    rows, width = hat.shape
    block = lambda cols: pl.BlockSpec((PAIR, cols), lambda i: (i, 0))
    return pl.pallas_call(
        head_kernel,
        grid=(rows // PAIR,),
        in_specs=[block(PROJ), block(PROJ), once((width, PROJ)), block(width), block(128),
                  vector(width)],
        out_specs=[block(PROJ), block(width), block(width), whole((8, width))],
        out_shape=[
            jax.ShapeDtypeStruct((rows, PROJ), bf16),
            jax.ShapeDtypeStruct((rows, width), f32),
            jax.ShapeDtypeStruct((rows, width), bf16),
            jax.ShapeDtypeStruct((8, width), f32),
        ],
        compiler_params=params(62),
        cost_estimate=cost(2 * rows * width * PROJ, 12 * MIB),
        name="head_back",
    )(grad, projected, w_proj, hat, rstd, gain)


def active_back_kernel(dffn_ref, wdown_ref, der_ref, dup_ref, bup_ref):
    dactive = mm(dffn_ref[...], wdown_ref[...], NT)
    dup = (dactive * der_ref[...].astype(f32)).astype(bf16)
    dup_ref[...] = dup
    bup_ref[...] = column_sum(dup.astype(f32))


def active_back(dffn, w_down, der):
    rows, width = dffn.shape
    units = w_down.shape[0]
    step = 512
    cols = pl.BlockSpec((rows, step), lambda i: (0, i))
    return pl.pallas_call(
        active_back_kernel,
        grid=(units // step,),
        in_specs=[once((rows, width)), pl.BlockSpec((step, width), lambda i: (i, 0)), cols],
        out_specs=[cols, pl.BlockSpec((1, step), lambda i: (0, i))],
        out_shape=[jax.ShapeDtypeStruct((rows, units), bf16), jax.ShapeDtypeStruct((1, units), f32)],
        compiler_params=params(62),
        cost_estimate=cost(2 * rows * width * units, 27 * MIB),
        name="active_back",
    )(dffn, w_down, der)


def feed_back_kernel(
    dup_ref, wup_ref, dresid2_ref, hat_ref, rstd_ref, gain_ref, wo_ref,
    dresid1_ref, dbranch_ref, datt_ref, sums_ref, acc_ref,
):
    step = pl.program_id(0)
    part = mm(dup_ref[...], wup_ref[...], NT)

    @pl.when(step == 0)
    def _():
        acc_ref[...] = part

    @pl.when(step > 0)
    def _():
        acc_ref[...] += part

    @pl.when(step == pl.num_programs(0) - 1)
    def _():
        sums = [0.0, 0.0, 0.0]
        for at in range(0, acc_ref.shape[0], PAIR):
            span = slice(at, at + PAIR)
            dnormed = acc_ref[span, :] + dresid2_ref[span, :]
            hat = hat_ref[span, :]
            dresid = norm_back(dnormed, hat, rstd_ref[span, :1], line(gain_ref))
            dresid1_ref[span, :] = dresid
            dbranch = dresid.astype(bf16)
            dbranch_ref[span, :] = dbranch
            datt_ref[span, :] = mm(dbranch, wo_ref[...], NT).astype(bf16)
            sums[0] += column_sum(dnormed * hat)
            sums[1] += column_sum(dnormed)
            sums[2] += column_sum(dbranch.astype(f32))
        for i in range(3):
            sums_ref[i : i + 1, :] = sums[i]


def feed_back(dup, w_up, dresid2, hat, rstd, w_out, gain):
    rows, width = hat.shape
    units = w_up.shape[1]
    step = 1024
    return pl.pallas_call(
        feed_back_kernel,
        grid=(units // step,),
        in_specs=[
            pl.BlockSpec((rows, step), lambda i: (0, i)),
            pl.BlockSpec((width, step), lambda i: (0, i)),
            once((rows, width)), once((rows, width)), once((rows, 128)), vector(width),
            once((width, width)),
        ],
        out_specs=[whole((rows, width)), whole((rows, width)), whole((rows, width)), whole((8, width))],
        out_shape=[
            jax.ShapeDtypeStruct((rows, width), f32),
            jax.ShapeDtypeStruct((rows, width), bf16),
            jax.ShapeDtypeStruct((rows, width), bf16),
            jax.ShapeDtypeStruct((8, width), f32),
        ],
        scratch_shapes=[pltpu.VMEM((rows, width), f32)],
        compiler_params=params(62),
        cost_estimate=cost(2 * rows * width * units, 36 * MIB),
        name="feed_back",
    )(dup, w_up, dresid2, hat, rstd, gain, w_out)


def attend_back_kernel(ids_ref, lengths_ref, qkv_ref, datt_ref, cos_ref, sin_ref, dmixed_ref, sums_ref, mask_ref):
    width = datt_ref.shape[1]
    block = pl.program_id(0)
    cosine = table_here(ids_ref, lengths_ref, cos_ref, block)
    sine = table_here(ids_ref, lengths_ref, sin_ref, block)
    mask_ref[...] = jnp.where(same_segment(ids_ref, lengths_ref, pl.program_id(0)), 0.0, masked_value)
    lane = lax.broadcasted_iota(jnp.int32, (PAIR, 2 * HD), 1)

    @pl.when(pl.program_id(0) == 0)
    def _():
        sums_ref[...] = jnp.zeros_like(sums_ref)

    for pair in range(width // (2 * HD)):
        at = pair * 2 * HD
        query = qkv_ref[:, at : at + 2 * HD]
        key = qkv_ref[:, width + at : width + at + 2 * HD]
        value = qkv_ref[:, 2 * width + at : 2 * width + at + 2 * HD]
        datt = datt_ref[:, at : at + 2 * HD]
        dquery = dkey = dvalue = None
        for head in range(2):
            mine = (lane < HD) if head == 0 else (lane >= HD)
            zero = jnp.zeros_like(key)
            query_h = jnp.where(mine, query, zero)
            key_h = jnp.where(mine, key, zero)
            datt_h = jnp.where(mine, datt, zero)
            scores = mm(key, query_h, NT) + mask_ref[...]
            terms = jnp.exp(scores - jnp.max(scores, 0, keepdims=True))
            weights = terms * (1.0 / jnp.sum(terms, 0, keepdims=True))
            dweights = mm(value, datt_h, NT)
            inner = jnp.sum(weights * dweights, 0, keepdims=True)
            dscores = (weights * (dweights - inner)).astype(bf16)
            dv = mm(weights.astype(bf16), datt_h)
            dk = mm(dscores, query_h)
            dq = mm(dscores, key_h, TN)
            dquery = dq if head == 0 else dquery + dq
            dkey = dk if head == 0 else dkey + dk
            dvalue = dv if head == 0 else dvalue + dv
        dquery = dquery * score_scale
        dquery = dquery * cosine - partner(dquery) * sine
        dkey = dkey * cosine - partner(dkey) * sine
        for i, grad in enumerate((dquery, dkey, dvalue)):
            low = grad.astype(bf16)
            dmixed_ref[:, i * width + at : i * width + at + 2 * HD] = low
            sums_ref[:, i * width + at : i * width + at + 2 * HD] += column_sum(low.astype(f32))


def attend_back(ids, lengths, qkv, datt, tables):
    rows, width = datt.shape
    block = lambda cols: pl.BlockSpec((PAIR, cols), lambda i, *_: (i, 0))
    return pl.pallas_call(
        attend_back_kernel,
        grid_spec=pltpu.PrefetchScalarGridSpec(
            num_scalar_prefetch=2,
            grid=(rows // PAIR,),
            in_specs=[block(3 * width), block(width), once(tables[0].shape), once(tables[0].shape)],
            out_specs=[block(3 * width), whole((1, 3 * width))],
            scratch_shapes=[pltpu.VMEM((PAIR, PAIR), f32)],
        ),
        out_shape=[jax.ShapeDtypeStruct((rows, 3 * width), bf16), jax.ShapeDtypeStruct((1, 3 * width), f32)],
        compiler_params=params(62),
        cost_estimate=cost(2e10, 16 * MIB),
        name="attend_back",
    )(ids, lengths, qkv, datt, *tables)


def input_grad_kernel(dmixed_ref, w_ref, dresid_ref, out_ref):
    out_ref[...] = dresid_ref[...] + mm(dmixed_ref[...], w_ref[...], NT)


def input_grad(dmixed, w_qkv, dresid):
    rows, width = dresid.shape
    block = lambda cols: pl.BlockSpec((PAIR, cols), lambda i: (i, 0))
    return pl.pallas_call(
        input_grad_kernel,
        grid=(rows // PAIR,),
        in_specs=[block(3 * width), once((width, 3 * width)), block(width)],
        out_specs=block(width),
        out_shape=jax.ShapeDtypeStruct((rows, width), f32),
        compiler_params=params(62),
        cost_estimate=cost(6 * rows * width * width, 20 * MIB),
        name="input_grad",
    )(dmixed, w_qkv, dresid)


def place_blocks(value_ref, slots, received, out_refs):
    for slot, block in slots:
        each = out_refs[0].shape[-2]
        value = value_ref[pl.ds(pl.multiple_of(block * each, each), each), :]
        if received is None:
            out_refs[0][slot] = value
        else:
            value = value + received[slot]
            half = out_refs[0].shape[0]
            if slot < half:
                out_refs[0][slot] = value
            else:
                out_refs[1][slot - half] = value.astype(bf16)


def target_of(ids_ref, keep):
    return ids_ref[0] if keep else 1 - ids_ref[0]


def outer_cols_kernel(counts, keep, ids_ref, *refs):
    used = 2 * len(counts)
    received = refs[used] if keep else None
    out_refs, value_ref = refs[used + 1 if keep else used : -1], refs[-1]
    step = pl.program_id(0)
    slots = (received if keep else out_refs[0]).shape[0]
    done = 0
    for i, count in enumerate(counts):

        @pl.when((step >= done) & (step < done + count))
        def _(left_ref=refs[2 * i], right_ref=refs[2 * i + 1]):
            value_ref[...] = mm(left_ref[...], right_ref[...], TN)

        done += count
    target = target_of(ids_ref, keep)
    owners = [choose(target, lambda order: rel_of(k, order), slots) ^ ids_ref[1] for k in range(slots)]
    place_blocks(value_ref, list(enumerate(owners)), received, out_refs)


def outer_cols(ids, pairs, slots, received=None, step=512):
    rows = pairs[0][0].shape[1] // 2
    each = rows // slots
    keep = received is not None
    specs, args, counts = [], [], []
    for left, right, begin, number in pairs:
        count = number // step
        first = sum(counts)
        specs.append(
            pl.BlockSpec((left.shape[0], rows), lambda i, ids: (0, target_of(ids, keep)), pipeline_mode=pl.Buffered(1))
        )
        specs.append(
            pl.BlockSpec(
                (right.shape[0], step),
                lambda i, *_, first=first, count=count, at=begin // step: (0, at + jnp.clip(i - first, 0, count - 1)),
            )
        )
        args += [left, right]
        counts.append(count)
    cols = sum(counts) * step
    spec = lambda count: pl.BlockSpec((count, each, step), lambda i, *_: (0, 0, i))
    shape = lambda count, kind: jax.ShapeDtypeStruct((count, each, cols), kind)
    if keep:
        specs.append(spec(slots))
        args.append(received)
        outs = [spec(slots // 2)] * 2
        shapes = [shape(slots // 2, f32), shape(slots // 2, bf16)]
    else:
        outs, shapes = [spec(slots)], [shape(slots, f32)]
    out = pl.pallas_call(
        functools.partial(outer_cols_kernel, counts, keep),
        grid_spec=pltpu.PrefetchScalarGridSpec(
            num_scalar_prefetch=1, grid=(sum(counts),), in_specs=specs, out_specs=outs,
            scratch_shapes=[pltpu.VMEM((rows, step), f32)],
        ),
        out_shape=shapes,
        compiler_params=params(62),
        cost_estimate=cost(2 * args[0].shape[0] * rows * cols, (20 if keep else 15) * MIB),
        name="outer_cols",
    )(ids, *args)
    return out if keep else out[0]


def outer_rows_kernel(group, slots_apart, keep, ids_ref, left_ref, right_ref, final_ref, dproj_ref, *refs):
    received = refs[0] if keep else None
    out_refs, value_ref, proj_ref = refs[1 if keep else 0 : -2], refs[-2], refs[-1]
    value_ref[...] = mm(left_ref[...], right_ref[...], TN)
    proj_ref[...] = mm(final_ref[...], dproj_ref[...], TN)
    _, tall, width = value_ref.shape[0], out_refs[0].shape[-2], value_ref.shape[1]
    each = value_ref.shape[0] // group
    short = proj_ref.shape[0] // group
    pieces = width // PROJ
    half = group // 2
    target = target_of(ids_ref, keep)
    for j in range(group):
        slot = j * slots_apart + pl.program_id(0)
        block = (choose(target, lambda order: rel_of(slot, order), group * slots_apart) ^ ids_ref[1]) % group
        value = value_ref[pl.ds(pl.multiple_of(block * each, each), each), :]
        small = proj_ref[pl.ds(pl.multiple_of(block * short, short), short), :]
        fold = short // pieces if short >= pieces else 1
        low = [small[i * fold : (i + 1) * fold, :] for i in range(short // fold)]
        if keep:
            value = value + received[j, 0, :each, :]
            low = [
                part + received[j, 0, each : each + fold, i * PROJ : (i + 1) * PROJ] for i, part in enumerate(low)
            ]
            out_ref, at = (out_refs[0], j) if j < half else (out_refs[1 + 2 * (j - half) // half], j % (half // 2))
        else:
            out_ref, at = out_refs[0], j
        kind = out_ref.dtype
        out_ref[at, 0, :each, :] = value.astype(kind)
        out_ref[at, 0, each:, :] = jnp.zeros((tall - each, width), kind)
        for i, part in enumerate(low):
            out_ref[at, 0, each : each + fold, i * PROJ : (i + 1) * PROJ] = part.astype(kind)


def outer_rows(ids, left, right, final, dproj, slots, group, received=None):
    tokens_here, rows = left.shape
    width = right.shape[1]
    rest = slots // group
    each = rows // (2 * slots)
    tall = each + 16
    keep = received is not None
    spec = lambda count: pl.BlockSpec((count, 1, tall, width), lambda i, *_: (0, i, 0, 0))
    shape = lambda count, kind: jax.ShapeDtypeStruct((count, rest, tall, width), kind)
    def cols(i, ids):
        target = target_of(ids, keep)
        return 0, target * rest + (choose(target, lambda order: rel_of(i, order), slots) ^ ids[1]) // group

    specs = [
        pl.BlockSpec((tokens_here, group * each), cols),
        once((tokens_here, width)),
        pl.BlockSpec((tokens_here, final.shape[1] // (2 * rest)), cols),
        once((tokens_here, PROJ)),
    ]
    args = [left, right, final, dproj]
    if keep:
        specs.append(spec(group))
        args.append(received.reshape(group, rest, tall, width))
        outs = [spec(group // 2), spec(group // 4), spec(group // 4)]
        shapes = [shape(group // 2, f32), shape(group // 4, bf16), shape(group // 4, bf16)]
    else:
        outs, shapes = [spec(group)], [shape(group, f32)]
    out = pl.pallas_call(
        functools.partial(outer_rows_kernel, group, rest, keep),
        grid_spec=pltpu.PrefetchScalarGridSpec(
            num_scalar_prefetch=1, grid=(rest,), in_specs=specs, out_specs=outs,
            scratch_shapes=[
                pltpu.VMEM((group * each, width), f32),
                pltpu.VMEM((final.shape[1] // (2 * rest), PROJ), f32),
            ],
        ),
        out_shape=shapes,
        compiler_params=params(62),
        cost_estimate=cost(tokens_here * rows * width, (20 if keep else 15) * MIB),
        name="outer_rows",
    )(ids, *args)
    out = [o.reshape(-1, tall, width) for o in out]
    return out if keep else out[0]


def flips(count):
    bits = [1 << i for i in range(count.bit_length() - 1)]
    third = {16: 1, 64: 2}[count]
    swapped = bits[third : 2 * third] + bits[:third] + bits[2 * third :][::-1]
    return bits, swapped


def slot_of(rel, order):
    return sum(
        ((rel >> (flip.bit_length() - 1)) & 1) << (len(order) - 1 - i) for i, flip in enumerate(order)
    )


def rel_of(slot, order):
    return sum(
        ((slot >> (len(order) - 1 - i)) & 1) << (flip.bit_length() - 1) for i, flip in enumerate(order)
    )


def choose(core, function, count):
    first, second = (function(order) for order in flips(count))
    return jnp.where(core == 0, first, second)


def hop(values, stage, count):
    pairs = []
    for stream, order in enumerate(flips(count)):
        pairs += [(stream * count + i, stream * count + (i ^ order[stage])) for i in range(count)]
    return lax.ppermute(values, ("stream", "dp"), pairs)


def swap(values):
    return lax.ppermute(values, "stream", [(0, 1), (1, 0)])


def after(value, *others):
    return lax.optimization_barrier((value, *others))[0]


def gather_both(first, first_stages, second, second_stages, count):
    pending = [(first, list(first_stages)), (second, list(second_stages))]
    while any(stages for _, stages in pending):
        got = [hop(values, stages[-1], count) if stages else None for values, stages in pending]
        values = lax.optimization_barrier([x for pair in zip(pending, got) for x in (pair[0][0], pair[1]) if x is not None])
        joined = []
        for (_, stages), arrived in zip(pending, got):
            value = values.pop(0)
            if arrived is not None:
                value = jnp.concatenate([value, values.pop(0)], 0)
            joined.append((value, stages[:-1]))
        held = lax.optimization_barrier([value for value, _ in joined])
        pending = [(value, stages) for value, (_, stages) in zip(held, joined)]
    return [value for value, _ in pending]


def take_in(keep, got):
    half = keep.shape[0] // 2
    if half == 0:
        return keep[0] + got[0].astype(f32), None
    return keep[:half] + got[:half].astype(f32), (keep[half:] + got[half:].astype(f32)).astype(bf16)


def scatter_sum(keep, send, stage, count, got=None):
    if got is not None:
        keep, send = take_in(keep, got)
    while send is not None:
        keep, send = take_in(keep, hop(send, stage, count))
        stage += 1
    return keep


def total_sum(values, stage, count):
    for later in range(stage, count.bit_length() - 1):
        values = values + hop(values, later, count)
    return values


def body(
    tokens, doc_lengths, cand_docs, group_sizes, w_qkv, b_qkv, w_attn_out, b_attn_out, gain_one, bias_one,
    w_up, b_up, w_down, b_down, gain_two, bias_two, w_proj,
):
    stream = lax.axis_index("stream")
    me = lax.axis_index("dp")
    count = lax.axis_size("dp")
    hidden = tokens[0]
    rows, width = hidden.shape
    half = rows // 2
    ids = jnp.stack([stream, me]).astype(jnp.int32)
    tables = [jnp.asarray(table) for table in rotation_tables()]
    group = {16: 4, 64: 16}[count]

    hold = lax.optimization_barrier
    levels = {16: 2, 64: 4}[count]
    last_stage = count.bit_length() - 1
    shape = (count, levels)
    info = jnp.concatenate([cand_docs.reshape(QH, CAND), group_sizes.reshape(QH, 1)], 1).astype(jnp.int32)
    hidden_, info = hold((hidden, info))
    info_got = hop(info, last_stage - 1, count)
    qkv, attended, hat1, rstd1, normed = attend(
        ids, doc_lengths, hidden_, w_qkv, b_qkv, tables, w_attn_out, b_attn_out, gain_one, bias_one
    )
    info, info_got, normed = hold((info, info_got, normed))
    info = jnp.concatenate([info, info_got], 0)
    info, normed = hold((info, normed))
    info_got = hop(info, last_stage - 2, count)
    active, der, hat2, rstd2, final, projected, vecs = feed(
        normed, w_up, b_up, w_down, b_down, hat1, gain_one, bias_one, gain_two, bias_two, w_proj
    )
    info, info_got, vecs = hold((info, info_got, vecs))
    info = jnp.concatenate([info, info_got], 0)

    on_docs = stream == 1
    other = swap(jnp.where(on_docs, vecs[:half], vecs[half:]))
    own_docs = jnp.where(on_docs, vecs[half:], other)
    queries = jnp.where(on_docs, other, vecs[:half])
    queries, near = gather_both(queries, range(levels, last_stage), own_docs, range(levels), count)
    queries = queries.reshape(-1, QLEN, PROJ)
    far = swap(near)
    scores, entries = score(ids, info, doc_lengths, queries, near, far, shape)
    scores = total_sum(scores, levels, count)
    loss, dq_keep, dq_send, keep, send = score_back(
        ids, info, doc_lengths, entries, scores, queries, near, far, shape
    )
    loss = lax.dynamic_slice_in_dim(loss, (me >> levels) * QH, QH, 0)
    by_row = (-1, half, PROJ)
    keep, q_keep = keep.reshape(by_row), dq_keep.reshape(by_row)
    got, q_got = swap(send).reshape(by_row), hop(dq_send.reshape(by_row), levels, count)
    keep, got, q_keep, q_got = hold((keep, got, q_keep, q_got))
    keep, send = take_in(keep, got)
    q_keep, q_send = take_in(q_keep, q_got)
    keep, send, q_keep, q_send = hold((keep, send, q_keep, q_send))
    got, q_got = hop(send, 0, count), hop(q_send, levels + 1, count)
    keep, got, q_keep, q_got = hold((keep, got, q_keep, q_got))
    keep, send = take_in(keep, got)
    dqueries = scatter_sum(q_keep, None, last_stage, count, q_got)
    ddocs = scatter_sum(keep, send, 1, count)
    back = swap(jnp.where(on_docs, dqueries, ddocs))
    grad_vectors = jnp.where(
        on_docs, jnp.concatenate([back, ddocs], 0), jnp.concatenate([dqueries, back], 0)
    )

    def add_first(keep, got):
        half = keep.shape[0] // 2
        return (keep[half:] + got.astype(f32)).astype(bf16)

    def add_second(keep, got):
        half = keep.shape[0] // 2
        return keep[:half] + got.astype(f32)

    dproj, dresid2, dffn, sums2 = head_back(grad_vectors, projected, w_proj, hat2, rstd2, gain_two)
    down = lambda left, received=None: outer_rows(
        ids, left, dffn, final, dproj, count, group, received
    )
    units = w_up.shape[1]
    up = lambda left, received=None: outer_cols(ids, [(left, dup, 0, units)], count, received)
    mix_a = lambda left, received=None: outer_cols(ids, [(left, dmixed, 0, 2 * width)], count, received)
    mix_b = lambda left, received=None: outer_cols(
        ids, [(left, dmixed, 2 * width, width), (attended, dbranch, 0, width)], count, received
    )

    d_out = down(active)
    d_got = swap(d_out)
    dffn_, d_out = hold((dffn, d_out))
    dup, sum_up = active_back(dffn_, w_down, der)
    active_, d_got, dup = hold((active, d_got, dup))
    d_keep, d_low, d_high = down(active_, d_got)
    d_high, d_low, normed_, d_keep = hold((d_high, d_low, normed, d_keep))
    d_high_got, d_low_got = hop(d_high, 0, count), hop(d_low, 0, count)
    u_out = up(normed_)
    d_keep, d_high_got, u_out = hold((d_keep, d_high_got, u_out))
    d_send = add_first(d_keep, d_high_got)
    d_send, u_out, dup_ = hold((d_send, u_out, dup))
    d_got, u_got = hop(d_send, 1, count), swap(u_out)
    dresid1, dbranch, dattended, sums1 = feed_back(dup_, w_up, dresid2, hat1, rstd1, w_attn_out, gain_one)
    d_keep, d_low_got, d_got, dbranch = hold((d_keep, d_low_got, d_got, dbranch))
    d_keep, d_send = take_in(add_second(d_keep, d_low_got), d_got)
    d_keep, d_send, normed_, u_got = hold((d_keep, d_send, normed, u_got))
    d_got = hop(d_send, 2, count)
    u_keep, u_send = up(normed_, u_got)
    d_keep, d_got, u_keep = hold((d_keep, d_got, u_keep))
    d_keep, d_send = take_in(d_keep, d_got)
    u_send, d_keep, d_send, dattended = hold((u_send, d_keep, d_send, dattended))
    u_got, d_got = hop(u_send, 0, count), hop(d_send, 3, count)
    dmixed, sum_qkv = attend_back(ids, doc_lengths, qkv, dattended, tables)
    d_keep, d_got, u_keep, u_got, dmixed = hold((d_keep, d_got, u_keep, u_got, dmixed))
    u_keep, u_send = take_in(u_keep, u_got)
    g_down = scatter_sum(d_keep, d_send, 4, count, d_got)
    sums = [sum_qkv[0], sums1[2], sums1[0], sums1[1], sum_up[0], sums2[2], sums2[0], sums2[1]]
    late = jnp.concatenate([v.reshape(2 * count, -1) for v in sums], 1)
    g_down, u_send, u_keep, hidden_, late = hold((g_down, u_send, u_keep, hidden, late))
    u_got, l_got = hop(u_send, 1, count), swap(late)
    a_out = mix_a(hidden_)
    a_out, hidden_, late, l_got = hold((a_out, hidden, late, l_got))
    late = late + l_got
    a_out, hidden_, late = hold((a_out, hidden_, late))
    a_got, l_got = swap(a_out), hop(late, 0, count)
    b_out = mix_b(hidden_)
    u_keep, u_got, b_out, late, l_got = hold((u_keep, u_got, b_out, late, l_got))
    u_keep, u_send = take_in(u_keep, u_got)
    late = late + l_got
    u_keep, u_send, b_out, hidden_, a_got, late = hold((u_keep, u_send, b_out, hidden, a_got, late))
    b_got, u_got, l_got = swap(b_out), hop(u_send, 2, count), hop(late, 1, count)
    a_keep, a_send = mix_a(hidden_, a_got)
    a_send, b_got, hidden_ = hold((a_send, b_got, hidden))
    a_got = hop(a_send, 0, count)
    b_keep, b_send = mix_b(hidden_, b_got)
    u_keep, u_got, b_keep, late, l_got = hold((u_keep, u_got, b_keep, late, l_got))
    u_keep, u_send = take_in(u_keep, u_got)
    late = late + l_got
    a_keep, a_got, u_send, b_send, late = hold((a_keep, a_got, u_send, b_send, late))
    a_keep, a_send = take_in(a_keep, a_got)
    a_keep, a_send, u_send, b_send, dmixed_, late = hold((a_keep, a_send, u_send, b_send, dmixed, late))
    a_got, b_got, u_got = hop(a_send, 1, count), hop(b_send, 0, count), hop(u_send, 3, count)
    l_got = hop(late, 2, count)
    grad_hidden = input_grad(dmixed_, w_qkv, dresid1)
    a_keep, a_got, u_keep, u_got, grad_hidden, b_got = hold((a_keep, a_got, u_keep, u_got, grad_hidden, b_got))
    b_keep, b_send = take_in(b_keep, b_got)
    b_got = hop(b_send, 1, count)
    a_keep, a_send = take_in(a_keep, a_got)
    g_a = scatter_sum(a_keep, a_send, 2, count)
    b_keep, b_send = take_in(b_keep, b_got)
    g_b = scatter_sum(b_keep, b_send, 2, count)
    g_up = scatter_sum(u_keep, u_send, 4, count, u_got)

    late = total_sum(late + l_got, 3, count)
    mine = lax.dynamic_slice_in_dim(late, stream * count + me, 1, 0)[0]
    sizes = [v.shape[0] // (2 * count) for v in sums]
    parts = [mine[end - size : end] for end, size in zip(np.cumsum(sizes), sizes)]
    g_bqkv, g_bout, g_gain1, g_bias1, g_bup, g_bdown, g_gain2, g_bias2 = parts
    tall = w_down.shape[0] // (2 * count)
    short = width // (2 * count)
    pieces = width // PROJ
    fold = max(short // pieces, 1)
    g_proj = g_down[tall : tall + fold].reshape(fold, pieces, PROJ).transpose(1, 0, 2)[: short // fold].reshape(short, PROJ)
    return (
        loss[:, 0][None, None, :],
        grad_hidden[None],
        jnp.concatenate([g_a, g_b[:, :width]], 1),
        g_bqkv,
        g_b[:, width:],
        g_bout,
        g_gain1,
        g_bias1,
        g_up,
        g_bup,
        g_down[:tall],
        g_bdown,
        g_gain2,
        g_bias2,
        g_proj,
    )


def solution(mesh):
    every = P(("stream", "dp"))
    rows = P(("stream", "dp"), None)
    return jax.shard_map(
        body,
        mesh=mesh,
        in_specs=(P("stream", "dp", None), P(), P("dp", "stream", None, None), P("dp", "stream", None)) + (P(),) * 13,
        out_specs=(
            P("dp", "stream", None), P("stream", "dp", None), rows, every, rows, every, every, every, rows, every,
            rows, every, every, every, rows,
        ),
        check_vma=False,
    )
```

```python
import functools
import math

import jax
import jax.numpy as jnp
import numpy as np
from jax import lax
from jax.experimental import pallas as pl
from jax.experimental.pallas import tpu as pltpu
from jax.sharding import PartitionSpec as P

HD = 64
PROJ = 128
QLEN = 32
CAND = 8
QH = 16
PAIR = 256

score_scale = 0.125
sim_temp = 0.05
loss_temp = 0.08
masked_value = -1e30
norm_eps = 1e-05
vector_eps = 1e-06

f32 = jnp.float32
bf16 = jnp.bfloat16
MIB = 1 << 20

NN = (((1,), (0,)), ((), ()))
NT = (((1,), (1,)), ((), ()))
TN = (((0,), (0,)), ((), ()))


def mm(left, right, dims=NN):
    return lax.dot_general(left, right, dims, preferred_element_type=f32)


def params(mib):
    return pltpu.CompilerParams(vmem_limit_bytes=mib * MIB)


def cost(flops, moved):
    return pl.CostEstimate(flops=int(flops), bytes_accessed=int(moved), transcendentals=0)


def whole(shape):
    return pl.BlockSpec(shape, lambda *_: (0,) * len(shape))


def vector(length):
    return pl.BlockSpec((length,), lambda *_: (0,), pipeline_mode=pl.Buffered(1))


def line(ref):
    return ref[...].astype(f32)[None, :]


def once(shape):
    return pl.BlockSpec(shape, lambda *_: (0,) * len(shape), pipeline_mode=pl.Buffered(1))


def rotation_tables():
    freq = np.exp(np.arange(HD // 2) * (-2.0 * math.log(10000.0) / HD))
    lane = np.arange(2 * HD)
    place = np.concatenate([np.arange(PAIR) % QLEN, np.arange(PAIR), np.arange(PAIR)])
    angle = place[:, None] * freq[lane % (HD // 2)][None, :]
    sign = np.where(lane % HD < HD // 2, -1.0, 1.0)[None, :]
    return np.cos(angle).astype(np.float32), (np.sin(angle) * sign).astype(np.float32)


def first_length(ids_ref, lengths_ref, block):
    return lengths_ref[ids_ref[1], 2 * block]


def table_here(ids_ref, lengths_ref, table_ref, block):
    first = first_length(ids_ref, lengths_ref, block)
    row = lax.broadcasted_iota(jnp.int32, (PAIR, 2 * HD), 0)
    moved = table_ref[pl.ds(2 * PAIR - first, PAIR), :]
    doc = jnp.where(row < first, table_ref[PAIR : 2 * PAIR, :], moved)
    return jnp.where(ids_ref[0] == 1, doc, table_ref[:PAIR, :])


def partner(values):
    lane = lax.broadcasted_iota(jnp.int32, values.shape, 1)
    ahead = pltpu.roll(values, 2 * HD - HD // 2, 1)
    behind = pltpu.roll(values, HD // 2, 1)
    return jnp.where(lane % HD < HD // 2, ahead, behind)


def same_segment(ids_ref, lengths_ref, block):
    is_doc = ids_ref[0] == 1
    first = first_length(ids_ref, lengths_ref, block)
    row = lax.broadcasted_iota(jnp.int32, (PAIR, PAIR), 0)
    col = lax.broadcasted_iota(jnp.int32, (PAIR, PAIR), 1)
    doc = ((row >= first) ^ (col >= first)).astype(jnp.int32)
    query = ((row // QLEN) ^ (col // QLEN)).astype(jnp.int32)
    return jnp.where(is_doc, doc, query) == 0


def normalise(values):
    mean = jnp.mean(values, -1, keepdims=True)
    center = values - mean
    rstd = lax.rsqrt(jnp.mean(center * center, -1, keepdims=True) + norm_eps)
    return center * rstd, rstd


def norm_back(grad, hat, rstd, gain):
    scaled = grad * gain
    return (
        scaled - jnp.mean(scaled, -1, keepdims=True) - hat * jnp.mean(scaled * hat, -1, keepdims=True)
    ) * rstd


def column_sum(values):
    return jnp.sum(values, 0, keepdims=True)


def attend_kernel(
    ids_ref, lengths_ref, x_ref, wqkv_ref, bqkv_ref, cos_ref, sin_ref, wo_ref, bo_ref, g_ref, c_ref,
    qkv_ref, att_ref, hat_ref, rstd_ref, normb_ref, mask_ref,
):
    width = x_ref.shape[1]
    x = x_ref[...]
    block = pl.program_id(0)
    cosine = table_here(ids_ref, lengths_ref, cos_ref, block)
    sine = table_here(ids_ref, lengths_ref, sin_ref, block)
    step = 256
    for start in range(0, 3 * width, step):
        mixed = mm(x, wqkv_ref[:, start : start + step]) + bqkv_ref[start : start + step].astype(f32)[None, :]
        if start < 2 * width:
            parts = []
            for off in range(0, step, 2 * HD):
                one = mixed[:, off : off + 2 * HD]
                one = one * cosine + partner(one) * sine
                parts.append(one.astype(bf16))
            mixed = jnp.concatenate(parts, 1)
            if start < width:
                mixed = mixed * jnp.asarray(score_scale, bf16)
        qkv_ref[:, start : start + step] = mixed.astype(bf16)
    mask_ref[...] = jnp.where(same_segment(ids_ref, lengths_ref, pl.program_id(0)), 0.0, masked_value)
    lane = lax.broadcasted_iota(jnp.int32, (PAIR, 2 * HD), 1)
    for pair in range(width // (2 * HD)):
        at = pair * 2 * HD
        query = qkv_ref[:, at : at + 2 * HD]
        key = qkv_ref[:, width + at : width + at + 2 * HD]
        value = qkv_ref[:, 2 * width + at : 2 * width + at + 2 * HD]
        total = None
        for head in range(2):
            mine = (lane < HD) if head == 0 else (lane >= HD)
            zero = jnp.zeros_like(key)
            scores = mm(query, jnp.where(mine, key, zero), NT) + mask_ref[...]
            highest = jnp.max(scores, -1, keepdims=True)
            terms = jnp.exp(scores - highest)
            weights = (terms * (1.0 / jnp.sum(terms, -1, keepdims=True))).astype(bf16)
            part = mm(weights, jnp.where(mine, value, zero))
            total = part if total is None else total + part
        att_ref[:, at : at + 2 * HD] = total.astype(bf16)
    branch = mm(att_ref[...], wo_ref[...]) + line(bo_ref)
    hat, rstd = normalise(x.astype(f32) + branch)
    hat_ref[...] = hat
    rstd_ref[...] = jnp.broadcast_to(rstd, rstd_ref.shape)
    normb_ref[...] = (hat * line(g_ref) + line(c_ref)).astype(bf16)


def attend(ids, lengths, x, w_qkv, b_qkv, tables, w_out, b_out, gain, bias):
    rows, width = x.shape
    block = lambda cols: pl.BlockSpec((PAIR, cols), lambda i, *_: (i, 0))
    return pl.pallas_call(
        attend_kernel,
        grid_spec=pltpu.PrefetchScalarGridSpec(
            num_scalar_prefetch=2,
            grid=(rows // PAIR,),
            in_specs=[
                block(width), once((width, 3 * width)), vector(3 * width), once(tables[0].shape),
                once(tables[0].shape), once((width, width)), vector(width), vector(width), vector(width),
            ],
            out_specs=[block(3 * width), block(width), block(width), block(128), block(width)],
            scratch_shapes=[pltpu.VMEM((PAIR, PAIR), f32)],
        ),
        out_shape=[
            jax.ShapeDtypeStruct((rows, 3 * width), bf16),
            jax.ShapeDtypeStruct((rows, width), bf16),
            jax.ShapeDtypeStruct((rows, width), f32),
            jax.ShapeDtypeStruct((rows, 128), f32),
            jax.ShapeDtypeStruct((rows, width), bf16),
        ],
        compiler_params=params(62),
        cost_estimate=cost(2 * rows * width * 4 * width, 30 * MIB),
        name="attend",
    )(ids, lengths, x, w_qkv, b_qkv, *tables, w_out, b_out, gain, bias)


def stream_out(i, at, pairs, sem):
    copies = [
        pltpu.make_async_copy(ref.at[pl.ds(at, PAIR)], hbm.at[pl.ds(at, PAIR)], sem.at[j, i])
        for j, (ref, hbm) in enumerate(pairs)
    ]
    for copy in copies:
        copy.start()
    return copies


def feed_kernel(
    x_ref, wup_ref, bup_ref, wdown_ref, bdown_ref, hat1_ref, g1_ref, c1_ref, g2_ref, c2_ref, wproj_ref,
    act_ref, der_ref, hat2_hbm, rstd2_ref, final_hbm, proj_ref, vec_ref,
    acc_ref, hat_ref, final_ref, in_sem, out_sem,
):
    step = pl.program_id(0)
    load = pltpu.make_async_copy(hat1_ref, hat_ref, in_sem)

    @pl.when(step == 0)
    def _():
        load.start()

    upward = mm(x_ref[...], wup_ref[...]) + line(bup_ref)
    below = 0.5 + 0.5 * lax.erf(upward * (2.0**-0.5))
    density = jnp.exp(-0.5 * upward * upward) * ((2.0 * math.pi) ** -0.5)
    active = (upward * below).astype(bf16)
    act_ref[...] = active
    der_ref[...] = (below + upward * density).astype(bf16)
    part = mm(active, wdown_ref[...])

    @pl.when(step == 0)
    def _():
        acc_ref[...] = part

    @pl.when(step > 0)
    def _():
        acc_ref[...] += part

    @pl.when(step == pl.num_programs(0) - 1)
    def _():
        load.wait()
        copies = []
        for i, at in enumerate(range(0, acc_ref.shape[0], PAIR)):
            span = slice(at, at + PAIR)
            normed = hat_ref[span, :] * line(g1_ref) + line(c1_ref)
            hat, rstd = normalise(normed + acc_ref[span, :] + line(bdown_ref))
            hat_ref[span, :] = hat
            rstd2_ref[span, :] = jnp.broadcast_to(rstd, (PAIR, 128))
            final = (hat * line(g2_ref) + line(c2_ref)).astype(bf16)
            final_ref[span, :] = final
            copies += stream_out(i, at, ((hat_ref, hat2_hbm), (final_ref, final_hbm)), out_sem)
            projected = mm(final, wproj_ref[...])
            proj_ref[span, :] = projected
            inverse = lax.rsqrt(jnp.sum(projected * projected, -1, keepdims=True) + vector_eps)
            vec_ref[span, :] = (projected * inverse).astype(bf16)
        for copy in copies:
            copy.wait()


def feed(x, w_up, b_up, w_down, b_down, hat1, g1, c1, g2, c2, w_proj):
    rows, width = x.shape
    units = w_up.shape[1]
    step = 512
    cols = pl.BlockSpec((rows, step), lambda i: (0, i))
    anywhere = pl.BlockSpec(memory_space=pl.ANY)
    return pl.pallas_call(
        feed_kernel,
        grid=(units // step,),
        in_specs=[
            once((rows, width)),
            pl.BlockSpec((width, step), lambda i: (0, i)),
            pl.BlockSpec((step,), lambda i: (i,)),
            pl.BlockSpec((step, width), lambda i: (i, 0)),
            vector(width), anywhere, vector(width), vector(width), vector(width), vector(width),
            once((width, PROJ)),
        ],
        out_specs=[cols, cols, anywhere, whole((rows, 128)), anywhere, whole((rows, PROJ)), whole((rows, PROJ))],
        out_shape=[
            jax.ShapeDtypeStruct((rows, units), bf16),
            jax.ShapeDtypeStruct((rows, units), bf16),
            jax.ShapeDtypeStruct((rows, width), f32),
            jax.ShapeDtypeStruct((rows, 128), f32),
            jax.ShapeDtypeStruct((rows, width), bf16),
            jax.ShapeDtypeStruct((rows, PROJ), f32),
            jax.ShapeDtypeStruct((rows, PROJ), bf16),
        ],
        scratch_shapes=[
            pltpu.VMEM((rows, width), f32),
            pltpu.VMEM((rows, width), f32),
            pltpu.VMEM((rows, width), bf16),
            pltpu.SemaphoreType.DMA,
            pltpu.SemaphoreType.DMA((2, rows // PAIR)),
        ],
        compiler_params=params(62),
        cost_estimate=cost(4 * rows * width * units, 50 * MIB),
        name="feed",
    )(x, w_up, b_up, w_down, b_down, hat1, g1, c1, g2, c2, w_proj)


UNROLL = 8


def load_docs(near_ref, far_ref, docs_ref, sem):
    half_rows = near_ref.shape[0]
    copies = [
        pltpu.make_async_copy(near_ref, docs_ref.at[pl.ds(0, half_rows)], sem.at[0]),
        pltpu.make_async_copy(far_ref, docs_ref.at[pl.ds(half_rows, half_rows)], sem.at[1]),
    ]
    for copy in copies:
        copy.start()
    return copies


def pair_scores(ids_ref, info_ref, length_ref, q_ref, docs_ref, entry, shape):
    count, levels = shape
    lane = lax.broadcasted_iota(jnp.int32, (QLEN, PAIR), 1)
    index = jnp.minimum(entry >> 3, q_ref.shape[0] - 1)
    doc = info_ref[index, entry & 7]
    row = doc >> 3
    pair = (doc >> 1) & 3
    first = length_ref[row, 2 * pair]
    odd = (doc & 1) == 1
    low = jnp.where(odd, first, 0)
    high = jnp.where(odd, PAIR, first)
    core = pair >> 1
    plane = 1 << levels
    rel = (row ^ ids_ref[1]) & (plane - 1)
    slot = choose(core, lambda order: slot_of(rel, order[:levels]), count)
    start = pl.multiple_of((((core ^ ids_ref[0]) * plane + slot) * 2 + (pair & 1)) * PAIR, PAIR)
    scaled = mm(q_ref[index], docs_ref[pl.ds(start, PAIR), :], NT) * (1.0 / sim_temp)
    return start, jnp.where((lane >= low) & (lane < high), scaled, masked_value)


def natural_row(ids_ref, entry, shape):
    count, levels = shape
    slot = entry >> (3 + QH.bit_length() - 1)
    rel = choose(ids_ref[0], lambda order: rel_of(slot, order[levels:]), count)
    z = (ids_ref[1] ^ rel) >> levels
    return z * QH + ((entry >> 3) & (QH - 1))


def score_kernel(
    shape, ids_ref, info_ref, length_ref, q_ref, near_ref, far_ref, score_ref, list_ref, docs_ref, sem,
):
    copies = load_docs(near_ref, far_ref, docs_ref, sem)
    count, levels = shape
    queries = q_ref.shape[0]
    score_ref[...] = jnp.zeros_like(score_ref)
    lane = lax.broadcasted_iota(jnp.int32, (1, 128), 1)
    z = ids_ref[1] >> levels

    def scan(q, found):
        size = info_ref[q, CAND]
        for c in range(CAND):
            here = ((info_ref[q, c] >> (3 + levels)) == z) & (c < size)
            list_ref[1 + found] = q * CAND + c
            found = found + here.astype(jnp.int32)
        return found

    found = lax.fori_loop(0, queries, scan, 0)
    list_ref[0] = found
    for u in range(UNROLL):
        list_ref[1 + found + u] = queries * CAND
    for j in range(QH):
        row = z * QH + j
        score_ref[pl.ds(row, 1), :] = jnp.where(lane == CAND, info_ref[j, CAND].astype(f32), 0.0)
    for copy in copies:
        copy.wait()

    @pl.loop(0, (found + UNROLL - 1) // UNROLL)
    def _(i):
        results = []
        for u in range(UNROLL):
            entry = list_ref[1 + i * UNROLL + u]
            _, scaled = pair_scores(ids_ref, info_ref, length_ref, q_ref, docs_ref, entry, shape)
            highest = jnp.max(scaled, -1, keepdims=True)
            total = jnp.sum(jnp.exp(scaled - highest), -1, keepdims=True)
            best = sim_temp * (highest + jnp.log(total))
            results.append((entry, jnp.sum(best, 0, keepdims=True)))
        for entry, result in results:
            row = jnp.where(entry >= queries * CAND, queries, natural_row(ids_ref, entry, shape))
            score_ref[pl.ds(row, 1), :] = jnp.where(lane == (entry & 7), result, score_ref[pl.ds(row, 1), :])


def score(ids, info, lengths, queries, near, far, shape):
    total = queries.shape[0]
    anywhere = pl.BlockSpec(memory_space=pl.ANY)
    return pl.pallas_call(
        functools.partial(score_kernel, shape),
        grid_spec=pltpu.PrefetchScalarGridSpec(
            num_scalar_prefetch=3,
            grid=(1,),
            in_specs=[whole(queries.shape), anywhere, anywhere],
            out_specs=[whole((total + 8, 128)), pl.BlockSpec(memory_space=pltpu.SMEM)],
            scratch_shapes=[pltpu.VMEM((2 * near.shape[0], PROJ), bf16), pltpu.SemaphoreType.DMA((2,))],
        ),
        out_shape=[
            jax.ShapeDtypeStruct((total + 8, 128), f32),
            jax.ShapeDtypeStruct((total * CAND + 2 * UNROLL,), jnp.int32),
        ],
        compiler_params=params(62),
        cost_estimate=cost(1e10, 4 * MIB),
        name="score",
    )(ids, info, lengths, queries, near, far)


def score_back_kernel(
    shape, ids_ref, info_ref, length_ref, list_ref, score_ref, q_ref, near_ref, far_ref,
    loss_ref, dq_keep_ref, dq_send_ref, keep_ref, send_ref, docs_ref, acc_ref, pull_ref, dq_ref, sem,
):
    copies = load_docs(near_ref, far_ref, docs_ref, sem)
    count, levels = shape
    queries = q_ref.shape[0]
    half_rows = near_ref.shape[0]
    scores = score_ref[:queries, :]
    lane = lax.broadcasted_iota(jnp.int32, (queries, 128), 1)
    size = jnp.sum(jnp.where(lane == CAND, scores, 0.0), -1, keepdims=True)
    counted = lane.astype(f32) < jnp.where(lane < CAND, size, 0.0)
    logits = jnp.where(counted, scores * (1.0 / loss_temp), masked_value)
    top = jnp.max(logits, -1, keepdims=True)
    norm = top + jnp.log(jnp.sum(jnp.exp(logits - top), -1, keepdims=True))
    positive = (lane == 0).astype(f32)
    pull_ref[:queries, :] = (jnp.exp(logits - norm) - positive) * (1.0 / loss_temp)
    pull_ref[queries:, :] = jnp.zeros((8, 128), f32)
    loss = norm - jnp.sum(logits * positive, -1, keepdims=True)
    loss_ref[...] = jnp.broadcast_to(loss, loss_ref.shape)
    dq_ref[...] = jnp.zeros_like(dq_ref)
    chunk = 512

    @pl.loop(0, 2 * half_rows // chunk)
    def _(i):
        acc_ref[pl.ds(pl.multiple_of(i * chunk, chunk), chunk), :] = jnp.zeros((chunk, PROJ), f32)

    for copy in copies:
        copy.wait()
    one = lax.broadcasted_iota(jnp.int32, (1, 128), 1)

    @pl.loop(0, (list_ref[0] + UNROLL - 1) // UNROLL)
    def _(i):
        results = []
        for u in range(UNROLL):
            entry = list_ref[1 + i * UNROLL + u]
            start, scaled = pair_scores(ids_ref, info_ref, length_ref, q_ref, docs_ref, entry, shape)
            terms = jnp.exp(scaled - jnp.max(scaled, -1, keepdims=True))
            row = jnp.where(entry >= queries * CAND, queries, natural_row(ids_ref, entry, shape))
            pull = jnp.sum(jnp.where(one == (entry & 7), pull_ref[pl.ds(row, 1), :], 0.0), -1, keepdims=True)
            dsim = (pull * (terms * (1.0 / jnp.sum(terms, -1, keepdims=True)))).astype(bf16)
            results.append((entry >> 3, start, dsim))
        for index, start, dsim in results:
            acc_ref[pl.ds(start, PAIR), :] += mm(dsim, q_ref[jnp.minimum(index, queries - 1)], TN)
            dq_ref[index] += mm(dsim, docs_ref[pl.ds(start, PAIR), :])

    near_q = dq_keep_ref.shape[0]
    dq_keep_ref[...] = dq_ref[:near_q]
    dq_send_ref[...] = dq_ref[near_q:queries].astype(bf16)

    @pl.loop(0, half_rows // chunk)
    def _(i):
        at = pl.multiple_of(i * chunk, chunk)
        keep_ref[pl.ds(at, chunk), :] = acc_ref[pl.ds(at, chunk), :]
        send_ref[pl.ds(at, chunk), :] = acc_ref[pl.ds(half_rows + at, chunk), :].astype(bf16)


def score_back(ids, info, lengths, entries, scores, queries, near, far, shape):
    total = queries.shape[0]
    half_rows = near.shape[0]
    anywhere = pl.BlockSpec(memory_space=pl.ANY)
    half = (total // 2, QLEN, PROJ)
    return pl.pallas_call(
        functools.partial(score_back_kernel, shape),
        grid_spec=pltpu.PrefetchScalarGridSpec(
            num_scalar_prefetch=4,
            grid=(1,),
            in_specs=[whole(scores.shape), whole(queries.shape), anywhere, anywhere],
            out_specs=[whole((total, 128)), whole(half), whole(half), whole((half_rows, PROJ)), whole((half_rows, PROJ))],
            scratch_shapes=[
                pltpu.VMEM((2 * half_rows, PROJ), bf16),
                pltpu.VMEM((2 * half_rows, PROJ), f32),
                pltpu.VMEM((total + 8, 128), f32),
                pltpu.VMEM((total + 1, QLEN, PROJ), f32),
                pltpu.SemaphoreType.DMA((2,)),
            ],
        ),
        out_shape=[
            jax.ShapeDtypeStruct((total, 128), f32),
            jax.ShapeDtypeStruct(half, f32),
            jax.ShapeDtypeStruct(half, bf16),
            jax.ShapeDtypeStruct((half_rows, PROJ), f32),
            jax.ShapeDtypeStruct((half_rows, PROJ), bf16),
        ],
        compiler_params=params(62),
        cost_estimate=cost(1e10, 8 * MIB),
        name="score_back",
    )(ids, info, lengths, entries, scores, queries, near, far)


def head_kernel(
    grad_ref, proj_ref, wproj_ref, hat_ref, rstd_ref, gain_ref,
    dproj_ref, dresid_ref, dffn_ref, sums_ref,
):
    projected = proj_ref[...]
    grad = grad_ref[...]
    inverse = lax.rsqrt(jnp.sum(projected * projected, -1, keepdims=True) + vector_eps)
    inner = jnp.sum(projected * grad, -1, keepdims=True)
    dproj = (grad * inverse - projected * (inner * inverse * inverse * inverse)).astype(bf16)
    dproj_ref[...] = dproj
    dfinal = mm(dproj, wproj_ref[...], NT)
    hat = hat_ref[...]
    dresid = norm_back(dfinal, hat, rstd_ref[:, :1], line(gain_ref))
    dresid_ref[...] = dresid
    dffn = dresid.astype(bf16)
    dffn_ref[...] = dffn

    @pl.when(pl.program_id(0) == 0)
    def _():
        sums_ref[...] = jnp.zeros_like(sums_ref)

    sums_ref[0:1, :] += column_sum(dfinal * hat)
    sums_ref[1:2, :] += column_sum(dfinal)
    sums_ref[2:3, :] += column_sum(dffn.astype(f32))


def head_back(grad, projected, w_proj, hat, rstd, gain):
    rows, width = hat.shape
    block = lambda cols: pl.BlockSpec((PAIR, cols), lambda i: (i, 0))
    return pl.pallas_call(
        head_kernel,
        grid=(rows // PAIR,),
        in_specs=[block(PROJ), block(PROJ), once((width, PROJ)), block(width), block(128),
                  vector(width)],
        out_specs=[block(PROJ), block(width), block(width), whole((8, width))],
        out_shape=[
            jax.ShapeDtypeStruct((rows, PROJ), bf16),
            jax.ShapeDtypeStruct((rows, width), f32),
            jax.ShapeDtypeStruct((rows, width), bf16),
            jax.ShapeDtypeStruct((8, width), f32),
        ],
        compiler_params=params(62),
        cost_estimate=cost(2 * rows * width * PROJ, 12 * MIB),
        name="head_back",
    )(grad, projected, w_proj, hat, rstd, gain)


def active_back_kernel(dffn_ref, wdown_ref, der_ref, dup_ref, bup_ref):
    dactive = mm(dffn_ref[...], wdown_ref[...], NT)
    dup = (dactive * der_ref[...].astype(f32)).astype(bf16)
    dup_ref[...] = dup
    bup_ref[...] = column_sum(dup.astype(f32))


def active_back(dffn, w_down, der):
    rows, width = dffn.shape
    units = w_down.shape[0]
    step = 512
    cols = pl.BlockSpec((rows, step), lambda i: (0, i))
    return pl.pallas_call(
        active_back_kernel,
        grid=(units // step,),
        in_specs=[once((rows, width)), pl.BlockSpec((step, width), lambda i: (i, 0)), cols],
        out_specs=[cols, pl.BlockSpec((1, step), lambda i: (0, i))],
        out_shape=[jax.ShapeDtypeStruct((rows, units), bf16), jax.ShapeDtypeStruct((1, units), f32)],
        compiler_params=params(62),
        cost_estimate=cost(2 * rows * width * units, 27 * MIB),
        name="active_back",
    )(dffn, w_down, der)


def feed_back_kernel(
    dup_ref, wup_ref, dresid2_hbm, hat_hbm, rstd_hbm, gain_ref, wo_hbm,
    dresid1_hbm, dbranch_hbm, datt_hbm, sums_ref,
    acc_ref, dresid_ref, hat_ref, rstd_ref, wo_ref, dbranch_ref, datt_ref, in_sem, out_sem,
):
    step = pl.program_id(0)
    loads = [
        pltpu.make_async_copy(hbm, ref, in_sem.at[i])
        for i, (hbm, ref) in enumerate(
            ((dresid2_hbm, dresid_ref), (hat_hbm, hat_ref), (rstd_hbm, rstd_ref), (wo_hbm, wo_ref))
        )
    ]

    @pl.when(step == 0)
    def _():
        for load in loads:
            load.start()

    part = mm(dup_ref[...], wup_ref[...], NT)

    @pl.when(step == 0)
    def _():
        acc_ref[...] = part

    @pl.when(step > 0)
    def _():
        acc_ref[...] += part

    @pl.when(step == pl.num_programs(0) - 1)
    def _():
        for load in loads:
            load.wait()
        sums = [0.0, 0.0, 0.0]
        copies = []
        for i, at in enumerate(range(0, acc_ref.shape[0], PAIR)):
            span = slice(at, at + PAIR)
            dnormed = acc_ref[span, :] + dresid_ref[span, :]
            hat = hat_ref[span, :]
            dresid = norm_back(dnormed, hat, rstd_ref[span, :1], line(gain_ref))
            dresid_ref[span, :] = dresid
            dbranch = dresid.astype(bf16)
            dbranch_ref[span, :] = dbranch
            datt_ref[span, :] = mm(dbranch, wo_ref[...], NT).astype(bf16)
            sums[0] += column_sum(dnormed * hat)
            sums[1] += column_sum(dnormed)
            sums[2] += column_sum(dbranch.astype(f32))
            outs = ((dresid_ref, dresid1_hbm), (dbranch_ref, dbranch_hbm), (datt_ref, datt_hbm))
            copies += stream_out(i, at, outs, out_sem)
        for i in range(3):
            sums_ref[i : i + 1, :] = sums[i]
        for copy in copies:
            copy.wait()


def feed_back(dup, w_up, dresid2, hat, rstd, w_out, gain):
    rows, width = hat.shape
    units = w_up.shape[1]
    step = 1024
    anywhere = pl.BlockSpec(memory_space=pl.ANY)
    return pl.pallas_call(
        feed_back_kernel,
        grid=(units // step,),
        in_specs=[
            pl.BlockSpec((rows, step), lambda i: (0, i)),
            pl.BlockSpec((width, step), lambda i: (0, i)),
            anywhere, anywhere, anywhere, vector(width), anywhere,
        ],
        out_specs=[anywhere, anywhere, anywhere, whole((8, width))],
        out_shape=[
            jax.ShapeDtypeStruct((rows, width), f32),
            jax.ShapeDtypeStruct((rows, width), bf16),
            jax.ShapeDtypeStruct((rows, width), bf16),
            jax.ShapeDtypeStruct((8, width), f32),
        ],
        scratch_shapes=[
            pltpu.VMEM((rows, width), f32),
            pltpu.VMEM((rows, width), f32),
            pltpu.VMEM((rows, width), f32),
            pltpu.VMEM((rows, 128), f32),
            pltpu.VMEM((width, width), bf16),
            pltpu.VMEM((rows, width), bf16),
            pltpu.VMEM((rows, width), bf16),
            pltpu.SemaphoreType.DMA((4,)),
            pltpu.SemaphoreType.DMA((3, rows // PAIR)),
        ],
        compiler_params=params(62),
        cost_estimate=cost(2 * rows * width * units, 36 * MIB),
        name="feed_back",
    )(dup, w_up, dresid2, hat, rstd, gain, w_out)


def attend_back_kernel(ids_ref, lengths_ref, qkv_ref, datt_ref, cos_ref, sin_ref, dmixed_ref, sums_ref, mask_ref):
    width = datt_ref.shape[1]
    block = pl.program_id(0)
    cosine = table_here(ids_ref, lengths_ref, cos_ref, block)
    sine = table_here(ids_ref, lengths_ref, sin_ref, block)
    mask_ref[...] = jnp.where(same_segment(ids_ref, lengths_ref, pl.program_id(0)), 0.0, masked_value)
    lane = lax.broadcasted_iota(jnp.int32, (PAIR, 2 * HD), 1)

    @pl.when(pl.program_id(0) == 0)
    def _():
        sums_ref[...] = jnp.zeros_like(sums_ref)

    for pair in range(width // (2 * HD)):
        at = pair * 2 * HD
        query = qkv_ref[:, at : at + 2 * HD]
        key = qkv_ref[:, width + at : width + at + 2 * HD]
        value = qkv_ref[:, 2 * width + at : 2 * width + at + 2 * HD]
        datt = datt_ref[:, at : at + 2 * HD]
        dquery = dkey = dvalue = None
        for head in range(2):
            mine = (lane < HD) if head == 0 else (lane >= HD)
            zero = jnp.zeros_like(key)
            query_h = jnp.where(mine, query, zero)
            key_h = jnp.where(mine, key, zero)
            datt_h = jnp.where(mine, datt, zero)
            scores = mm(key, query_h, NT) + mask_ref[...]
            terms = jnp.exp(scores - jnp.max(scores, 0, keepdims=True))
            weights = terms * (1.0 / jnp.sum(terms, 0, keepdims=True))
            dweights = mm(value, datt_h, NT)
            inner = jnp.sum(weights * dweights, 0, keepdims=True)
            dscores = (weights * (dweights - inner)).astype(bf16)
            dv = mm(weights.astype(bf16), datt_h)
            dk = mm(dscores, query_h)
            dq = mm(dscores, key_h, TN)
            dquery = dq if head == 0 else dquery + dq
            dkey = dk if head == 0 else dkey + dk
            dvalue = dv if head == 0 else dvalue + dv
        dquery = dquery * score_scale
        dquery = dquery * cosine - partner(dquery) * sine
        dkey = dkey * cosine - partner(dkey) * sine
        for i, grad in enumerate((dquery, dkey, dvalue)):
            low = grad.astype(bf16)
            dmixed_ref[:, i * width + at : i * width + at + 2 * HD] = low
            sums_ref[:, i * width + at : i * width + at + 2 * HD] += column_sum(low.astype(f32))


def attend_back(ids, lengths, qkv, datt, tables):
    rows, width = datt.shape
    block = lambda cols: pl.BlockSpec((PAIR, cols), lambda i, *_: (i, 0))
    return pl.pallas_call(
        attend_back_kernel,
        grid_spec=pltpu.PrefetchScalarGridSpec(
            num_scalar_prefetch=2,
            grid=(rows // PAIR,),
            in_specs=[block(3 * width), block(width), once(tables[0].shape), once(tables[0].shape)],
            out_specs=[block(3 * width), whole((1, 3 * width))],
            scratch_shapes=[pltpu.VMEM((PAIR, PAIR), f32)],
        ),
        out_shape=[jax.ShapeDtypeStruct((rows, 3 * width), bf16), jax.ShapeDtypeStruct((1, 3 * width), f32)],
        compiler_params=params(62),
        cost_estimate=cost(2e10, 16 * MIB),
        name="attend_back",
    )(ids, lengths, qkv, datt, *tables)


def input_grad_kernel(dmixed_ref, w_ref, dresid_ref, out_ref):
    out_ref[...] = dresid_ref[...] + mm(dmixed_ref[...], w_ref[...], NT)


def input_grad(dmixed, w_qkv, dresid):
    rows, width = dresid.shape
    block = lambda cols: pl.BlockSpec((PAIR, cols), lambda i: (i, 0))
    return pl.pallas_call(
        input_grad_kernel,
        grid=(rows // PAIR,),
        in_specs=[block(3 * width), once((width, 3 * width)), block(width)],
        out_specs=block(width),
        out_shape=jax.ShapeDtypeStruct((rows, width), f32),
        compiler_params=params(62),
        cost_estimate=cost(6 * rows * width * width, 20 * MIB),
        name="input_grad",
    )(dmixed, w_qkv, dresid)


def target_of(ids_ref, keep):
    return ids_ref[0] if keep else 1 - ids_ref[0]


def put(value, received, out_refs):
    if received is None:
        out_refs[0][...] = value.reshape(out_refs[0].shape).astype(bf16)
        return
    each, at = out_refs[0].shape[1], 0
    for out_ref in out_refs:
        count = out_ref.shape[0]
        part = value[at * each : (at + count) * each].reshape(out_ref.shape) + received[at : at + count].astype(f32)
        out_ref[...] = part.astype(out_ref.dtype)
        at += count


def outer_cols_kernel(counts, keep, slots, ids_ref, *refs):
    number = len(counts)
    received = refs[2 * number] if keep else None
    out_refs = refs[2 * number + 1 : -number] if keep else refs[2 * number : 2 * number + 1]
    turned_refs = refs[-number:]
    step = pl.program_id(0)
    each = turned_refs[0].shape[0] // slots
    target = target_of(ids_ref, keep)

    @pl.when(step == 0)
    def _():
        for left_ref, turned_ref in zip(refs[0 : 2 * number : 2], turned_refs):
            for at in range(0, left_ref.shape[1], 128):
                turned = left_ref[:, at : at + 128].T.astype(turned_ref.dtype)
                for k in range(128 // each):
                    rel = (at // each + k) ^ ids_ref[1]
                    slot = choose(target, lambda order: slot_of(rel, order), slots)
                    turned_ref[pl.ds(pl.multiple_of(slot * each, each), each), :] = turned[k * each : (k + 1) * each]

    done = 0
    for i, count in enumerate(counts):

        @pl.when((step >= done) & (step < done + count))
        def _(right_ref=refs[2 * i + 1], turned_ref=turned_refs[i]):
            put(mm(turned_ref[...].astype(bf16), right_ref[...]), received, out_refs)

        done += count


def outer_cols(ids, pairs, slots, received=None, parts=1, begin_at=0):
    rows = pairs[0][0].shape[1] // 2
    each = rows // slots
    keep = received is not None
    step = 1024
    specs, args, counts = [], [], []
    for left, right, begin, number in pairs:
        count = number // step
        first = sum(counts)
        specs.append(
            pl.BlockSpec((left.shape[0], rows), lambda i, ids: (0, target_of(ids, keep)), pipeline_mode=pl.Buffered(1))
        )
        specs.append(
            pl.BlockSpec(
                (right.shape[0], step),
                lambda i, *_, first=first, count=count, at=begin // step: (0, at + jnp.clip(i - first, 0, count - 1)),
            )
        )
        args += [left, right]
        counts.append(count)
    cols = sum(counts) * step
    spec = lambda count: pl.BlockSpec((count, each, step), lambda i, *_: (0, 0, i))
    shape = lambda count, kind: jax.ShapeDtypeStruct((count, each, cols), kind)
    if keep:
        specs.append(pl.BlockSpec((slots, each, step), lambda i, *_: (0, 0, begin_at // step + i)))
        args.append(received)
        outs = [spec(slots // 2)] + [spec(slots // 2 // parts)] * parts
        shapes = [shape(slots // 2, f32)] + [shape(slots // 2 // parts, bf16)] * parts
    else:
        outs, shapes = [spec(slots)], [shape(slots, bf16)]
    kind = bf16 if each % 16 == 0 else f32
    out = pl.pallas_call(
        functools.partial(outer_cols_kernel, counts, keep, slots),
        grid_spec=pltpu.PrefetchScalarGridSpec(
            num_scalar_prefetch=1, grid=(sum(counts),), in_specs=specs, out_specs=outs,
            scratch_shapes=[pltpu.VMEM((rows, left.shape[0]), kind) for left, *_ in pairs],
        ),
        out_shape=shapes,
        compiler_params=params(62),
        cost_estimate=cost(2 * args[0].shape[0] * rows * cols, (20 if keep else 15) * MIB),
        name="outer_cols",
    )(ids, *args)
    return out if keep else out[0]


def outer_rows_kernel(group, slots_apart, keep, ids_ref, *refs):
    left_refs, (right_ref, final_ref, dproj_ref) = refs[:group], refs[group : group + 3]
    received = refs[group + 3] if keep else None
    out_refs, proj_ref = refs[group + (4 if keep else 3) : -1], refs[-1]
    left = jnp.concatenate([ref[...].reshape(ref.shape[-2:]) for ref in left_refs], 1)
    value = mm(left, right_ref[...], TN)
    proj_ref[...] = mm(final_ref[...], dproj_ref[...], TN)
    tall, width = out_refs[0].shape[-2], value.shape[1]
    each = value.shape[0] // group
    short = proj_ref.shape[0] // group
    pieces = width // PROJ
    half = group // 2
    target = target_of(ids_ref, keep)
    for j in range(group):
        slot = j * slots_apart + pl.program_id(0)
        block = (choose(target, lambda order: rel_of(slot, order), group * slots_apart) ^ ids_ref[1]) & (group - 1)
        part = value[j * each : (j + 1) * each, :]
        small = proj_ref[pl.ds(pl.multiple_of(block * short, short), short), :]
        fold = short // pieces if short >= pieces else 1
        low = [small[i * fold : (i + 1) * fold, :] for i in range(short // fold)]
        if keep:
            part = part + received[j, 0, :each, :].astype(f32)
            low = [
                x + received[j, 0, each : each + fold, i * PROJ : (i + 1) * PROJ].astype(f32) for i, x in enumerate(low)
            ]
            out_ref, at = (out_refs[0], j) if j < half else (out_refs[1 + 2 * (j - half) // half], j % (half // 2))
        else:
            out_ref, at = out_refs[0], j
        kind = out_ref.dtype
        out_ref[at, 0, :each, :] = part.astype(kind)
        out_ref[at, 0, each:, :] = jnp.zeros((tall - each, width), kind)
        for i, x in enumerate(low):
            out_ref[at, 0, each : each + fold, i * PROJ : (i + 1) * PROJ] = x.astype(kind)


def outer_rows(ids, left, right, final, dproj, slots, group, received=None):
    tokens_here, rows = left.shape
    width = right.shape[1]
    rest = slots // group
    each = rows // (2 * slots)
    tall = each + 8
    keep = received is not None
    spec = lambda count: pl.BlockSpec((count, 1, tall, width), lambda i, *_: (0, i, 0, 0))
    shape = lambda count, kind: jax.ShapeDtypeStruct((count, rest, tall, width), kind)

    def owner(slot, ids):
        target = target_of(ids, keep)
        return target * slots + (choose(target, lambda order: rel_of(slot, order), slots) ^ ids[1])

    specs = [
        pl.BlockSpec((tokens_here, each), lambda i, ids, j=j: (0, owner(j * rest + i, ids))) for j in range(group)
    ]
    lefts = [left] * group
    if each < 128:
        specs = [
            pl.BlockSpec((1, tokens_here, each), lambda i, ids, j=j: (owner(j * rest + i, ids), 0, 0)) for j in range(group)
        ]
        lefts = [left.reshape(tokens_here, -1, each).transpose(1, 0, 2)] * group
    specs += [
        once((tokens_here, width)),
        pl.BlockSpec((tokens_here, final.shape[1] // (2 * rest)), lambda i, ids: (0, owner(i, ids) // group)),
        once((tokens_here, PROJ)),
    ]
    args = lefts + [right, final, dproj]
    if keep:
        specs.append(spec(group))
        args.append(received.reshape(group, rest, tall, width))
        outs = [spec(group // 2), spec(group // 4), spec(group // 4)]
        shapes = [shape(group // 2, f32), shape(group // 4, bf16), shape(group // 4, bf16)]
    else:
        outs, shapes = [spec(group)], [shape(group, bf16)]
    out = pl.pallas_call(
        functools.partial(outer_rows_kernel, group, rest, keep),
        grid_spec=pltpu.PrefetchScalarGridSpec(
            num_scalar_prefetch=1, grid=(rest,), in_specs=specs, out_specs=outs,
            scratch_shapes=[pltpu.VMEM((final.shape[1] // (2 * rest), PROJ), f32)],
        ),
        out_shape=shapes,
        compiler_params=params(62),
        cost_estimate=cost(tokens_here * rows * width, (20 if keep else 15) * MIB),
        name="outer_rows",
    )(ids, *args)
    out = [o.reshape(-1, tall, width) for o in out]
    return out if keep else out[0]


def flips(count):
    bits = [1 << i for i in range(count.bit_length() - 1)]
    third = {16: 1, 64: 2}[count]
    swapped = bits[third : 2 * third] + bits[:third] + bits[2 * third :][::-1]
    return bits, swapped


def slot_of(rel, order):
    return sum(
        ((rel >> (flip.bit_length() - 1)) & 1) << (len(order) - 1 - i) for i, flip in enumerate(order)
    )


def rel_of(slot, order):
    return sum(
        ((slot >> (len(order) - 1 - i)) & 1) << (flip.bit_length() - 1) for i, flip in enumerate(order)
    )


def choose(core, function, count):
    first, second = (function(order) for order in flips(count))
    return jnp.where(core == 0, first, second)


def hop(values, stage, count):
    pairs = []
    for stream, order in enumerate(flips(count)):
        pairs += [(stream * count + i, stream * count + (i ^ order[stage])) for i in range(count)]
    return lax.ppermute(values, ("stream", "dp"), pairs)


def swap(values):
    return lax.ppermute(values, "stream", [(0, 1), (1, 0)])


def after(value, *others):
    return lax.optimization_barrier((value, *others))[0]


def gather_both(first, first_stages, second, second_stages, count):
    pending = [(first, list(first_stages)), (second, list(second_stages))]
    while any(stages for _, stages in pending):
        got = [hop(values, stages[-1], count) if stages else None for values, stages in pending]
        values = lax.optimization_barrier([x for pair in zip(pending, got) for x in (pair[0][0], pair[1]) if x is not None])
        joined = []
        for (_, stages), arrived in zip(pending, got):
            value = values.pop(0)
            if arrived is not None:
                value = jnp.concatenate([value, values.pop(0)], 0)
            joined.append((value, stages[:-1]))
        held = lax.optimization_barrier([value for value, _ in joined])
        pending = [(value, stages) for value, (_, stages) in zip(held, joined)]
    return [value for value, _ in pending]


def take_in(keep, got):
    half = keep.shape[0] // 2
    if half == 0:
        return keep[0] + got[0].astype(f32), None
    return keep[:half] + got[:half].astype(f32), (keep[half:] + got[half:].astype(f32)).astype(bf16)


def scatter_sum(keep, send, stage, count, got=None):
    if got is not None:
        keep, send = take_in(keep, got)
    while send is not None:
        keep, send = take_in(keep, hop(send, stage, count))
        stage += 1
    return keep


def total_sum(values, stage, count):
    for later in range(stage, count.bit_length() - 1):
        values = values + hop(values, later, count)
    return values


def body(
    tokens, doc_lengths, cand_docs, group_sizes, w_qkv, b_qkv, w_attn_out, b_attn_out, gain_one, bias_one,
    w_up, b_up, w_down, b_down, gain_two, bias_two, w_proj,
):
    stream = lax.axis_index("stream")
    me = lax.axis_index("dp")
    count = lax.axis_size("dp")
    hidden = tokens[0]
    rows, width = hidden.shape
    half = rows // 2
    ids = jnp.stack([stream, me]).astype(jnp.int32)
    tables = [jnp.asarray(table) for table in rotation_tables()]
    group = {16: 4, 64: 16}[count]

    hold = lax.optimization_barrier
    levels = {16: 2, 64: 4}[count]
    last_stage = count.bit_length() - 1
    shape = (count, levels)
    info = jnp.concatenate([cand_docs.reshape(QH, CAND), group_sizes.reshape(QH, 1)], 1).astype(jnp.int32)
    hidden_, info = hold((hidden, info))
    info_got = hop(info, last_stage - 1, count)
    qkv, attended, hat1, rstd1, normed = attend(
        ids, doc_lengths, hidden_, w_qkv, b_qkv, tables, w_attn_out, b_attn_out, gain_one, bias_one
    )
    info, info_got, normed = hold((info, info_got, normed))
    info = jnp.concatenate([info, info_got], 0)
    info, normed = hold((info, normed))
    info_got = hop(info, last_stage - 2, count)
    active, der, hat2, rstd2, final, projected, vecs = feed(
        normed, w_up, b_up, w_down, b_down, hat1, gain_one, bias_one, gain_two, bias_two, w_proj
    )
    info, info_got, vecs = hold((info, info_got, vecs))
    info = jnp.concatenate([info, info_got], 0)

    on_docs = stream == 1
    other = swap(jnp.where(on_docs, vecs[:half], vecs[half:]))
    own_docs = jnp.where(on_docs, vecs[half:], other)
    queries = jnp.where(on_docs, other, vecs[:half])
    queries, near = gather_both(queries, range(levels, last_stage), own_docs, range(levels), count)
    queries = queries.reshape(-1, QLEN, PROJ)
    far = swap(near)
    scores, entries = score(ids, info, doc_lengths, queries, near, far, shape)
    scores = total_sum(scores, levels, count)
    loss, dq_keep, dq_send, keep, send = score_back(
        ids, info, doc_lengths, entries, scores, queries, near, far, shape
    )
    loss = lax.dynamic_slice_in_dim(loss, (me >> levels) * QH, QH, 0)
    by_row = (-1, half, PROJ)
    keep, q_keep = keep.reshape(by_row), dq_keep.reshape(by_row)
    got, q_got = swap(send).reshape(by_row), hop(dq_send.reshape(by_row), levels, count)
    keep, got, q_keep, q_got = hold((keep, got, q_keep, q_got))
    keep, send = take_in(keep, got)
    q_keep, q_send = take_in(q_keep, q_got)
    keep, send, q_keep, q_send = hold((keep, send, q_keep, q_send))
    got, q_got = hop(send, 0, count), hop(q_send, levels + 1, count)
    keep, got, q_keep, q_got = hold((keep, got, q_keep, q_got))
    keep, send = take_in(keep, got)
    dqueries = scatter_sum(q_keep, None, last_stage, count, q_got)
    ddocs = scatter_sum(keep, send, 1, count)
    back = swap(jnp.where(on_docs, dqueries, ddocs))
    grad_vectors = jnp.where(
        on_docs, jnp.concatenate([back, ddocs], 0), jnp.concatenate([dqueries, back], 0)
    )

    def add_first(keep, got):
        half = keep.shape[0] // 2
        return (keep[half:] + got.astype(f32)).astype(bf16)

    def add_second(keep, got):
        half = keep.shape[0] // 2
        return keep[:half] + got.astype(f32)

    dproj, dresid2, dffn, sums2 = head_back(grad_vectors, projected, w_proj, hat2, rstd2, gain_two)
    down = lambda left, received=None: outer_rows(
        ids, left, dffn, final, dproj, count, group, received
    )
    units = w_up.shape[1]
    up = lambda left, received=None: outer_cols(ids, [(left, dup, 0, units)], count, received)
    mix_out = lambda left: outer_cols(ids, [(left, dmixed, 0, 3 * width), (attended, dbranch, 0, width)], count)
    mix_a = lambda left, received: outer_cols(ids, [(left, dmixed, 0, 2 * width)], count, received)
    mix_b = lambda left, received: outer_cols(
        ids, [(left, dmixed, 2 * width, width), (attended, dbranch, 0, width)], count, received, 1, 2 * width
    )

    d_out = down(active)
    d_got = swap(d_out)
    dffn_, d_out = hold((dffn, d_out))
    dup, sum_up = active_back(dffn_, w_down, der)
    active_, d_got, dup = hold((active, d_got, dup))
    d_keep, d_low, d_high = down(active_, d_got)
    d_high, d_low, normed_, d_keep = hold((d_high, d_low, normed, d_keep))
    u_out = up(normed_)
    d_high, d_low, u_out, dup_ = hold((d_high, d_low, u_out, dup))
    d_high_got, d_low_got, u_got = hop(d_high, 0, count), hop(d_low, 0, count), swap(u_out)
    dresid1, dbranch, dattended, sums1 = feed_back(dup_, w_up, dresid2, hat1, rstd1, w_attn_out, gain_one)
    d_keep, d_high_got, d_low_got, dbranch = hold((d_keep, d_high_got, d_low_got, dbranch))
    d_send = add_first(d_keep, d_high_got)
    d_keep = add_second(d_keep, d_low_got)
    d_keep, d_send, normed_, u_got = hold((d_keep, d_send, normed, u_got))
    d_got = hop(d_send, 1, count)
    u_keep, u_send = up(normed_, u_got)
    d_keep, d_got, u_keep = hold((d_keep, d_got, u_keep))
    d_keep, d_send = take_in(d_keep, d_got)
    u_send, d_keep, d_send, dattended = hold((u_send, d_keep, d_send, dattended))
    u_got, d_got = hop(u_send, 0, count), hop(d_send, 2, count)
    dmixed, sum_qkv = attend_back(ids, doc_lengths, qkv, dattended, tables)
    d_keep, d_got, u_keep, u_got, dmixed = hold((d_keep, d_got, u_keep, u_got, dmixed))
    u_keep, u_send = take_in(u_keep, u_got)
    d_keep, d_send = take_in(d_keep, d_got)
    sums = [sum_qkv[0], sums1[2], sums1[0], sums1[1], sum_up[0], sums2[2], sums2[0], sums2[1]]
    late = jnp.concatenate([v.reshape(2 * count, -1) for v in sums], 1)
    u_send, u_keep, hidden_, late, d_keep, d_send = hold((u_send, u_keep, hidden, late, d_keep, d_send))
    u_got, l_got, d_got = hop(u_send, 1, count), swap(late), hop(d_send, 3, count)
    m_out = mix_out(hidden_)
    m_out, late, l_got, u_keep, u_got, d_keep, d_got = hold((m_out, late, l_got, u_keep, u_got, d_keep, d_got))
    g_down = scatter_sum(d_keep, d_send, 4, count, d_got)
    u_keep, u_send = take_in(u_keep, u_got)
    late = late + l_got
    m_out, hidden_, late, g_down, u_send, u_keep = hold((m_out, hidden_, late, g_down, u_send, u_keep))
    m_got, l_got, u_got = swap(m_out), hop(late, 0, count), hop(u_send, 2, count)
    a_keep, a_send = mix_a(hidden_, m_got)
    u_keep, u_got, a_send, late, l_got = hold((u_keep, u_got, a_send, late, l_got))
    u_keep, u_send = take_in(u_keep, u_got)
    late = late + l_got
    u_keep, u_send, a_send, hidden_, late = hold((u_keep, u_send, a_send, hidden_, late))
    a_got, u_got, l_got = hop(a_send, 0, count), hop(u_send, 3, count), hop(late, 1, count)
    b_keep, b_send = mix_b(hidden_, m_got)
    u_keep, u_got, b_keep, late, l_got = hold((u_keep, u_got, b_keep, late, l_got))
    g_up = scatter_sum(u_keep, u_send, 4, count, u_got)
    late = late + l_got
    a_keep, a_got, g_up, b_send, late = hold((a_keep, a_got, g_up, b_send, late))
    a_keep, a_send = take_in(a_keep, a_got)
    a_keep, a_send, b_send, dmixed_, late = hold((a_keep, a_send, b_send, dmixed, late))
    a_got, b_got = hop(a_send, 1, count), hop(b_send, 0, count)
    l_got = hop(late, 2, count)
    grad_hidden = input_grad(dmixed_, w_qkv, dresid1)
    a_keep, a_got, grad_hidden, b_got = hold((a_keep, a_got, grad_hidden, b_got))
    b_keep, b_send = take_in(b_keep, b_got)
    b_got = hop(b_send, 1, count)
    a_keep, a_send = take_in(a_keep, a_got)
    g_a = scatter_sum(a_keep, a_send, 2, count)
    b_keep, b_send = take_in(b_keep, b_got)
    g_b = scatter_sum(b_keep, b_send, 2, count)

    late = total_sum(late + l_got, 3, count)
    mine = lax.dynamic_slice_in_dim(late, stream * count + me, 1, 0)[0]
    sizes = [v.shape[0] // (2 * count) for v in sums]
    parts = [mine[end - size : end] for end, size in zip(np.cumsum(sizes), sizes)]
    g_bqkv, g_bout, g_gain1, g_bias1, g_bup, g_bdown, g_gain2, g_bias2 = parts
    tall = w_down.shape[0] // (2 * count)
    short = width // (2 * count)
    pieces = width // PROJ
    fold = max(short // pieces, 1)
    g_proj = g_down[tall : tall + fold].reshape(fold, pieces, PROJ).transpose(1, 0, 2)[: short // fold].reshape(short, PROJ)
    return (
        loss[:, 0][None, None, :],
        grad_hidden[None],
        jnp.concatenate([g_a, g_b[:, :width]], 1),
        g_bqkv,
        g_b[:, width:],
        g_bout,
        g_gain1,
        g_bias1,
        g_up,
        g_bup,
        g_down[:tall],
        g_bdown,
        g_gain2,
        g_bias2,
        g_proj,
    )


def solution(mesh):
    every = P(("stream", "dp"))
    rows = P(("stream", "dp"), None)
    return jax.shard_map(
        body,
        mesh=mesh,
        in_specs=(P("stream", "dp", None), P(), P("dp", "stream", None, None), P("dp", "stream", None)) + (P(),) * 13,
        out_specs=(
            P("dp", "stream", None), P("stream", "dp", None), rows, every, rows, every, every, every, rows, every,
            rows, every, every, every, rows,
        ),
        check_vma=False,
    )
```

```python
import functools
import math

import jax
import jax.numpy as jnp
import numpy as np
from jax import lax
from jax.experimental import pallas as pl
from jax.experimental.pallas import tpu as pltpu
from jax.sharding import PartitionSpec as P

HD = 64
PROJ = 128
QLEN = 32
CAND = 8
QH = 16
PAIR = 256

score_scale = 0.125
sim_temp = 0.05
loss_temp = 0.08
masked_value = -1e30
norm_eps = 1e-05
vector_eps = 1e-06

f32 = jnp.float32
bf16 = jnp.bfloat16
MIB = 1 << 20

NN = (((1,), (0,)), ((), ()))
NT = (((1,), (1,)), ((), ()))
TN = (((0,), (0,)), ((), ()))


def mm(left, right, dims=NN):
    return lax.dot_general(left, right, dims, preferred_element_type=f32)


def params(mib):
    return pltpu.CompilerParams(vmem_limit_bytes=mib * MIB)


def cost(flops, moved):
    return pl.CostEstimate(flops=int(flops), bytes_accessed=int(moved), transcendentals=0)


def whole(shape):
    return pl.BlockSpec(shape, lambda *_: (0,) * len(shape))


def vector(length):
    return pl.BlockSpec((length,), lambda *_: (0,), pipeline_mode=pl.Buffered(1))


def line(ref):
    return ref[...].astype(f32)[None, :]


def once(shape):
    return pl.BlockSpec(shape, lambda *_: (0,) * len(shape), pipeline_mode=pl.Buffered(1))


def rotation_tables():
    freq = np.exp(np.arange(HD // 2) * (-2.0 * math.log(10000.0) / HD))
    lane = np.arange(2 * HD)
    place = np.concatenate([np.arange(PAIR) % QLEN, np.arange(PAIR), np.arange(PAIR)])
    angle = place[:, None] * freq[lane % (HD // 2)][None, :]
    sign = np.where(lane % HD < HD // 2, -1.0, 1.0)[None, :]
    return np.cos(angle).astype(np.float32), (np.sin(angle) * sign).astype(np.float32)


def first_length(ids_ref, lengths_ref, block):
    return lengths_ref[ids_ref[1], 2 * block]


def table_here(ids_ref, lengths_ref, table_ref, block):
    first = first_length(ids_ref, lengths_ref, block)
    row = lax.broadcasted_iota(jnp.int32, (PAIR, 2 * HD), 0)
    moved = table_ref[pl.ds(2 * PAIR - first, PAIR), :]
    doc = jnp.where(row < first, table_ref[PAIR : 2 * PAIR, :], moved)
    return jnp.where(ids_ref[0] == 1, doc, table_ref[:PAIR, :])


def partner(values):
    lane = lax.broadcasted_iota(jnp.int32, values.shape, 1)
    ahead = pltpu.roll(values, 2 * HD - HD // 2, 1)
    behind = pltpu.roll(values, HD // 2, 1)
    return jnp.where(lane % HD < HD // 2, ahead, behind)


def same_segment(ids_ref, lengths_ref, block):
    is_doc = ids_ref[0] == 1
    first = first_length(ids_ref, lengths_ref, block)
    row = lax.broadcasted_iota(jnp.int32, (PAIR, PAIR), 0)
    col = lax.broadcasted_iota(jnp.int32, (PAIR, PAIR), 1)
    doc = ((row >= first) ^ (col >= first)).astype(jnp.int32)
    query = ((row // QLEN) ^ (col // QLEN)).astype(jnp.int32)
    return jnp.where(is_doc, doc, query) == 0


def normalise(values):
    mean = jnp.mean(values, -1, keepdims=True)
    center = values - mean
    rstd = lax.rsqrt(jnp.mean(center * center, -1, keepdims=True) + norm_eps)
    return center * rstd, rstd


def norm_back(grad, hat, rstd, gain):
    scaled = grad * gain
    return (
        scaled - jnp.mean(scaled, -1, keepdims=True) - hat * jnp.mean(scaled * hat, -1, keepdims=True)
    ) * rstd


def column_sum(values):
    return jnp.sum(values, 0, keepdims=True)


def attend_kernel(
    ids_ref, lengths_ref, x_ref, wqkv_ref, bqkv_ref, cos_ref, sin_ref, wo_ref, bo_ref, g_ref, c_ref,
    qkv_ref, att_ref, hat_ref, rstd_ref, normb_ref, mask_ref,
):
    width = x_ref.shape[1]
    x = x_ref[...]
    block = pl.program_id(0)
    cosine = table_here(ids_ref, lengths_ref, cos_ref, block)
    sine = table_here(ids_ref, lengths_ref, sin_ref, block)
    step = 512
    for start in range(0, 3 * width, step):
        mixed = mm(x, wqkv_ref[:, start : start + step]) + bqkv_ref[start : start + step].astype(f32)[None, :]
        if start < 2 * width:
            parts = []
            for off in range(0, step, 2 * HD):
                one = mixed[:, off : off + 2 * HD]
                one = one * cosine + partner(one) * sine
                parts.append(one.astype(bf16))
            mixed = jnp.concatenate(parts, 1)
            if start < width:
                mixed = mixed * jnp.asarray(score_scale, bf16)
        qkv_ref[:, start : start + step] = mixed.astype(bf16)
    mask_ref[...] = jnp.where(same_segment(ids_ref, lengths_ref, pl.program_id(0)), 0.0, masked_value)
    lane = lax.broadcasted_iota(jnp.int32, (PAIR, 2 * HD), 1)
    mask = mask_ref[...]
    group = 4
    for begin in range(0, width // (2 * HD), group):
        heads = [(pair * 2 * HD, head) for pair in range(begin, begin + group) for head in range(2)]
        mine = lambda head: (lane < HD) if head == 0 else (lane >= HD)
        pick = lambda at, head: jnp.where(mine(head), qkv_ref[:, at : at + 2 * HD], jnp.zeros((PAIR, 2 * HD), bf16))
        scores = [mm(qkv_ref[:, at : at + 2 * HD], pick(width + at, head), NT) + mask for at, head in heads]
        terms = [jnp.exp(s - jnp.max(s, -1, keepdims=True)) for s in scores]
        weights = [(t * (1.0 / jnp.sum(t, -1, keepdims=True))).astype(bf16) for t in terms]
        parts = [mm(w, pick(2 * width + at, head)) for w, (at, head) in zip(weights, heads)]
        for k in range(group):
            at = heads[2 * k][0]
            att_ref[:, at : at + 2 * HD] = (parts[2 * k] + parts[2 * k + 1]).astype(bf16)
    branch = mm(att_ref[...], wo_ref[...]) + line(bo_ref)
    hat, rstd = normalise(x.astype(f32) + branch)
    hat_ref[...] = hat
    rstd_ref[...] = jnp.broadcast_to(rstd, rstd_ref.shape)
    normb_ref[...] = (hat * line(g_ref) + line(c_ref)).astype(bf16)


def attend(ids, lengths, x, w_qkv, b_qkv, tables, w_out, b_out, gain, bias):
    rows, width = x.shape
    block = lambda cols: pl.BlockSpec((PAIR, cols), lambda i, *_: (i, 0))
    return pl.pallas_call(
        attend_kernel,
        grid_spec=pltpu.PrefetchScalarGridSpec(
            num_scalar_prefetch=2,
            grid=(rows // PAIR,),
            in_specs=[
                block(width), once((width, 3 * width)), vector(3 * width), once(tables[0].shape),
                once(tables[0].shape), once((width, width)), vector(width), vector(width), vector(width),
            ],
            out_specs=[block(3 * width), block(width), block(width), block(128), block(width)],
            scratch_shapes=[pltpu.VMEM((PAIR, PAIR), f32)],
        ),
        out_shape=[
            jax.ShapeDtypeStruct((rows, 3 * width), bf16),
            jax.ShapeDtypeStruct((rows, width), bf16),
            jax.ShapeDtypeStruct((rows, width), f32),
            jax.ShapeDtypeStruct((rows, 128), f32),
            jax.ShapeDtypeStruct((rows, width), bf16),
        ],
        compiler_params=params(62),
        cost_estimate=cost(2 * rows * width * 4 * width, 30 * MIB),
        name="attend",
    )(ids, lengths, x, w_qkv, b_qkv, *tables, w_out, b_out, gain, bias)


def stream_out(i, at, pairs, sem):
    copies = [
        pltpu.make_async_copy(ref.at[pl.ds(at, PAIR)], hbm.at[pl.ds(at, PAIR)], sem.at[j, i])
        for j, (ref, hbm) in enumerate(pairs)
    ]
    for copy in copies:
        copy.start()
    return copies


def feed_kernel(
    x_ref, wup_ref, bup_ref, wdown_ref, bdown_ref, hat1_ref, g1_ref, c1_ref, g2_ref, c2_ref, wproj_ref,
    act_ref, der_ref, hat2_hbm, rstd2_ref, final_hbm, proj_ref, vec_ref,
    acc_ref, hat_ref, final_ref, in_sem, out_sem,
):
    step = pl.program_id(0)
    load = pltpu.make_async_copy(hat1_ref, hat_ref, in_sem)

    @pl.when(step == 0)
    def _():
        load.start()

    upward = mm(x_ref[...], wup_ref[...]) + line(bup_ref)
    below = 0.5 + 0.5 * lax.erf(upward * (2.0**-0.5))
    density = jnp.exp(-0.5 * upward * upward) * ((2.0 * math.pi) ** -0.5)
    active = (upward * below).astype(bf16)
    act_ref[...] = active
    der_ref[...] = (below + upward * density).astype(bf16)
    part = mm(active, wdown_ref[...])

    @pl.when(step == 0)
    def _():
        acc_ref[...] = part

    @pl.when(step > 0)
    def _():
        acc_ref[...] += part

    @pl.when(step == pl.num_programs(0) - 1)
    def _():
        load.wait()
        copies = []
        for i, at in enumerate(range(0, acc_ref.shape[0], PAIR)):
            span = slice(at, at + PAIR)
            normed = hat_ref[span, :] * line(g1_ref) + line(c1_ref)
            hat, rstd = normalise(normed + acc_ref[span, :] + line(bdown_ref))
            hat_ref[span, :] = hat
            rstd2_ref[span, :] = jnp.broadcast_to(rstd, (PAIR, 128))
            final = (hat * line(g2_ref) + line(c2_ref)).astype(bf16)
            final_ref[span, :] = final
            copies += stream_out(i, at, ((hat_ref, hat2_hbm), (final_ref, final_hbm)), out_sem)
            projected = mm(final, wproj_ref[...])
            proj_ref[span, :] = projected
            inverse = lax.rsqrt(jnp.sum(projected * projected, -1, keepdims=True) + vector_eps)
            vec_ref[span, :] = (projected * inverse).astype(bf16)
        for copy in copies:
            copy.wait()


def feed(x, w_up, b_up, w_down, b_down, hat1, g1, c1, g2, c2, w_proj):
    rows, width = x.shape
    units = w_up.shape[1]
    step = 512
    cols = pl.BlockSpec((rows, step), lambda i: (0, i))
    anywhere = pl.BlockSpec(memory_space=pl.ANY)
    return pl.pallas_call(
        feed_kernel,
        grid=(units // step,),
        in_specs=[
            once((rows, width)),
            pl.BlockSpec((width, step), lambda i: (0, i)),
            pl.BlockSpec((step,), lambda i: (i,)),
            pl.BlockSpec((step, width), lambda i: (i, 0)),
            vector(width), anywhere, vector(width), vector(width), vector(width), vector(width),
            once((width, PROJ)),
        ],
        out_specs=[cols, cols, anywhere, whole((rows, 128)), anywhere, whole((rows, PROJ)), whole((rows, PROJ))],
        out_shape=[
            jax.ShapeDtypeStruct((rows, units), bf16),
            jax.ShapeDtypeStruct((rows, units), bf16),
            jax.ShapeDtypeStruct((rows, width), f32),
            jax.ShapeDtypeStruct((rows, 128), f32),
            jax.ShapeDtypeStruct((rows, width), bf16),
            jax.ShapeDtypeStruct((rows, PROJ), f32),
            jax.ShapeDtypeStruct((rows, PROJ), bf16),
        ],
        scratch_shapes=[
            pltpu.VMEM((rows, width), f32),
            pltpu.VMEM((rows, width), f32),
            pltpu.VMEM((rows, width), bf16),
            pltpu.SemaphoreType.DMA,
            pltpu.SemaphoreType.DMA((2, rows // PAIR)),
        ],
        compiler_params=params(62),
        cost_estimate=cost(4 * rows * width * units, 50 * MIB),
        name="feed",
    )(x, w_up, b_up, w_down, b_down, hat1, g1, c1, g2, c2, w_proj)


UNROLL = 8


def load_docs(near_ref, far_ref, docs_ref, sem):
    half_rows = near_ref.shape[0]
    copies = [
        pltpu.make_async_copy(near_ref, docs_ref.at[pl.ds(0, half_rows)], sem.at[0]),
        pltpu.make_async_copy(far_ref, docs_ref.at[pl.ds(half_rows, half_rows)], sem.at[1]),
    ]
    for copy in copies:
        copy.start()
    return copies


def pair_scores(ids_ref, info_ref, length_ref, q_ref, docs_ref, entry, shape):
    count, levels = shape
    lane = lax.broadcasted_iota(jnp.int32, (QLEN, PAIR), 1)
    index = jnp.minimum(entry >> 3, q_ref.shape[0] - 1)
    doc = info_ref[index, entry & 7]
    row = doc >> 3
    pair = (doc >> 1) & 3
    first = length_ref[row, 2 * pair]
    odd = (doc & 1) == 1
    low = jnp.where(odd, first, 0)
    high = jnp.where(odd, PAIR, first)
    core = pair >> 1
    plane = 1 << levels
    rel = (row ^ ids_ref[1]) & (plane - 1)
    slot = choose(core, lambda order: slot_of(rel, order[:levels]), count)
    start = pl.multiple_of((((core ^ ids_ref[0]) * plane + slot) * 2 + (pair & 1)) * PAIR, PAIR)
    scaled = mm(q_ref[index], docs_ref[pl.ds(start, PAIR), :], NT) * (1.0 / sim_temp)
    return start, jnp.where((lane >= low) & (lane < high), scaled, masked_value)


def natural_row(ids_ref, entry, shape):
    count, levels = shape
    slot = entry >> (3 + QH.bit_length() - 1)
    rel = choose(ids_ref[0], lambda order: rel_of(slot, order[levels:]), count)
    z = (ids_ref[1] ^ rel) >> levels
    return z * QH + ((entry >> 3) & (QH - 1))


def score_kernel(
    shape, ids_ref, info_ref, length_ref, q_ref, near_ref, far_ref, score_ref, list_ref, docs_ref, sem,
):
    copies = load_docs(near_ref, far_ref, docs_ref, sem)
    count, levels = shape
    queries = q_ref.shape[0]
    score_ref[...] = jnp.zeros_like(score_ref)
    lane = lax.broadcasted_iota(jnp.int32, (1, 128), 1)
    z = ids_ref[1] >> levels

    def scan(q, found):
        size = info_ref[q, CAND]
        for c in range(CAND):
            here = ((info_ref[q, c] >> (3 + levels)) == z) & (c < size)
            list_ref[1 + found] = q * CAND + c
            found = found + here.astype(jnp.int32)
        return found

    found = lax.fori_loop(0, queries, scan, 0)
    list_ref[0] = found
    for u in range(UNROLL):
        list_ref[1 + found + u] = queries * CAND
    for j in range(QH):
        row = z * QH + j
        score_ref[pl.ds(row, 1), :] = jnp.where(lane == CAND, info_ref[j, CAND].astype(f32), 0.0)
    for copy in copies:
        copy.wait()

    @pl.loop(0, (found + UNROLL - 1) // UNROLL)
    def _(i):
        entries = [list_ref[1 + i * UNROLL + u] for u in range(UNROLL)]
        scaled = [pair_scores(ids_ref, info_ref, length_ref, q_ref, docs_ref, entry, shape)[1] for entry in entries]
        highest = [jnp.max(x, -1, keepdims=True) for x in scaled]
        totals = [jnp.sum(jnp.exp(x - m), -1, keepdims=True) for x, m in zip(scaled, highest)]
        results = [
            jnp.sum(sim_temp * (m + jnp.log(total)), 0, keepdims=True) for m, total in zip(highest, totals)
        ]
        for entry, result in zip(entries, results):
            row = jnp.where(entry >= queries * CAND, queries, natural_row(ids_ref, entry, shape))
            score_ref[pl.ds(row, 1), :] = jnp.where(lane == (entry & 7), result, score_ref[pl.ds(row, 1), :])


def score(ids, info, lengths, queries, near, far, shape):
    total = queries.shape[0]
    anywhere = pl.BlockSpec(memory_space=pl.ANY)
    return pl.pallas_call(
        functools.partial(score_kernel, shape),
        grid_spec=pltpu.PrefetchScalarGridSpec(
            num_scalar_prefetch=3,
            grid=(1,),
            in_specs=[whole(queries.shape), anywhere, anywhere],
            out_specs=[whole((total + 8, 128)), pl.BlockSpec(memory_space=pltpu.SMEM)],
            scratch_shapes=[pltpu.VMEM((2 * near.shape[0], PROJ), bf16), pltpu.SemaphoreType.DMA((2,))],
        ),
        out_shape=[
            jax.ShapeDtypeStruct((total + 8, 128), f32),
            jax.ShapeDtypeStruct((total * CAND + 2 * UNROLL,), jnp.int32),
        ],
        compiler_params=params(62),
        cost_estimate=cost(1e10, 4 * MIB),
        name="score",
    )(ids, info, lengths, queries, near, far)


def score_back_kernel(
    shape, ids_ref, info_ref, length_ref, list_ref, score_ref, q_ref, near_ref, far_ref,
    loss_ref, dq_keep_ref, dq_send_ref, keep_ref, send_ref, docs_ref, acc_ref, pull_ref, dq_ref, sem,
):
    copies = load_docs(near_ref, far_ref, docs_ref, sem)
    count, levels = shape
    queries = q_ref.shape[0]
    half_rows = near_ref.shape[0]
    scores = score_ref[:queries, :]
    lane = lax.broadcasted_iota(jnp.int32, (queries, 128), 1)
    size = jnp.sum(jnp.where(lane == CAND, scores, 0.0), -1, keepdims=True)
    counted = lane.astype(f32) < jnp.where(lane < CAND, size, 0.0)
    logits = jnp.where(counted, scores * (1.0 / loss_temp), masked_value)
    top = jnp.max(logits, -1, keepdims=True)
    norm = top + jnp.log(jnp.sum(jnp.exp(logits - top), -1, keepdims=True))
    positive = (lane == 0).astype(f32)
    pull_ref[:queries, :] = (jnp.exp(logits - norm) - positive) * (1.0 / loss_temp)
    pull_ref[queries:, :] = jnp.zeros((8, 128), f32)
    loss = norm - jnp.sum(logits * positive, -1, keepdims=True)
    loss_ref[...] = jnp.broadcast_to(loss, loss_ref.shape)
    dq_ref[...] = jnp.zeros_like(dq_ref)
    chunk = 512

    @pl.loop(0, 2 * half_rows // chunk)
    def _(i):
        acc_ref[pl.ds(pl.multiple_of(i * chunk, chunk), chunk), :] = jnp.zeros((chunk, PROJ), f32)

    for copy in copies:
        copy.wait()
    one = lax.broadcasted_iota(jnp.int32, (1, 128), 1)

    @pl.loop(0, (list_ref[0] + UNROLL - 1) // UNROLL)
    def _(i):
        entries = [list_ref[1 + i * UNROLL + u] for u in range(UNROLL)]
        found = [pair_scores(ids_ref, info_ref, length_ref, q_ref, docs_ref, entry, shape) for entry in entries]
        terms = [jnp.exp(scaled - jnp.max(scaled, -1, keepdims=True)) for _, scaled in found]
        totals = [jnp.sum(x, -1, keepdims=True) for x in terms]
        pulls = []
        for entry in entries:
            row = jnp.where(entry >= queries * CAND, queries, natural_row(ids_ref, entry, shape))
            pulls.append(
                jnp.sum(jnp.where(one == (entry & 7), pull_ref[pl.ds(row, 1), :], 0.0), -1, keepdims=True)
            )
        dsims = [(pull * (x * (1.0 / total))).astype(bf16) for pull, x, total in zip(pulls, terms, totals)]
        for entry, (start, _), dsim in zip(entries, found, dsims):
            index = entry >> 3
            acc_ref[pl.ds(start, PAIR), :] += mm(dsim, q_ref[jnp.minimum(index, queries - 1)], TN)
            dq_ref[index] += mm(dsim, docs_ref[pl.ds(start, PAIR), :])

    near_q = dq_keep_ref.shape[0]
    dq_keep_ref[...] = dq_ref[:near_q]
    dq_send_ref[...] = dq_ref[near_q:queries].astype(bf16)

    @pl.loop(0, half_rows // chunk)
    def _(i):
        at = pl.multiple_of(i * chunk, chunk)
        keep_ref[pl.ds(at, chunk), :] = acc_ref[pl.ds(at, chunk), :]
        send_ref[pl.ds(at, chunk), :] = acc_ref[pl.ds(half_rows + at, chunk), :].astype(bf16)


def score_back(ids, info, lengths, entries, scores, queries, near, far, shape):
    total = queries.shape[0]
    half_rows = near.shape[0]
    anywhere = pl.BlockSpec(memory_space=pl.ANY)
    half = (total // 2, QLEN, PROJ)
    return pl.pallas_call(
        functools.partial(score_back_kernel, shape),
        grid_spec=pltpu.PrefetchScalarGridSpec(
            num_scalar_prefetch=4,
            grid=(1,),
            in_specs=[whole(scores.shape), whole(queries.shape), anywhere, anywhere],
            out_specs=[whole((total, 128)), whole(half), whole(half), whole((half_rows, PROJ)), whole((half_rows, PROJ))],
            scratch_shapes=[
                pltpu.VMEM((2 * half_rows, PROJ), bf16),
                pltpu.VMEM((2 * half_rows, PROJ), f32),
                pltpu.VMEM((total + 8, 128), f32),
                pltpu.VMEM((total + 1, QLEN, PROJ), f32),
                pltpu.SemaphoreType.DMA((2,)),
            ],
        ),
        out_shape=[
            jax.ShapeDtypeStruct((total, 128), f32),
            jax.ShapeDtypeStruct(half, f32),
            jax.ShapeDtypeStruct(half, bf16),
            jax.ShapeDtypeStruct((half_rows, PROJ), f32),
            jax.ShapeDtypeStruct((half_rows, PROJ), bf16),
        ],
        compiler_params=params(62),
        cost_estimate=cost(1e10, 8 * MIB),
        name="score_back",
    )(ids, info, lengths, entries, scores, queries, near, far)


def head_kernel(
    grad_ref, proj_ref, wproj_ref, hat_ref, rstd_ref, gain_ref,
    dproj_ref, dresid_ref, dffn_ref, sums_ref,
):
    projected = proj_ref[...]
    grad = grad_ref[...]
    inverse = lax.rsqrt(jnp.sum(projected * projected, -1, keepdims=True) + vector_eps)
    inner = jnp.sum(projected * grad, -1, keepdims=True)
    dproj = (grad * inverse - projected * (inner * inverse * inverse * inverse)).astype(bf16)
    dproj_ref[...] = dproj
    dfinal = mm(dproj, wproj_ref[...], NT)
    hat = hat_ref[...]
    dresid = norm_back(dfinal, hat, rstd_ref[:, :1], line(gain_ref))
    dresid_ref[...] = dresid
    dffn = dresid.astype(bf16)
    dffn_ref[...] = dffn

    @pl.when(pl.program_id(0) == 0)
    def _():
        sums_ref[...] = jnp.zeros_like(sums_ref)

    sums_ref[0:1, :] += column_sum(dfinal * hat)
    sums_ref[1:2, :] += column_sum(dfinal)
    sums_ref[2:3, :] += column_sum(dffn.astype(f32))


def head_back(grad, projected, w_proj, hat, rstd, gain):
    rows, width = hat.shape
    block = lambda cols: pl.BlockSpec((PAIR, cols), lambda i: (i, 0))
    return pl.pallas_call(
        head_kernel,
        grid=(rows // PAIR,),
        in_specs=[block(PROJ), block(PROJ), once((width, PROJ)), block(width), block(128),
                  vector(width)],
        out_specs=[block(PROJ), block(width), block(width), whole((8, width))],
        out_shape=[
            jax.ShapeDtypeStruct((rows, PROJ), bf16),
            jax.ShapeDtypeStruct((rows, width), f32),
            jax.ShapeDtypeStruct((rows, width), bf16),
            jax.ShapeDtypeStruct((8, width), f32),
        ],
        compiler_params=params(62),
        cost_estimate=cost(2 * rows * width * PROJ, 12 * MIB),
        name="head_back",
    )(grad, projected, w_proj, hat, rstd, gain)


def active_back_kernel(dffn_ref, wdown_ref, der_ref, dup_ref, bup_ref):
    dactive = mm(dffn_ref[...], wdown_ref[...], NT)
    dup = (dactive * der_ref[...].astype(f32)).astype(bf16)
    dup_ref[...] = dup
    bup_ref[...] = column_sum(dup.astype(f32))


def active_back(dffn, w_down, der):
    rows, width = dffn.shape
    units = w_down.shape[0]
    step = 512
    cols = pl.BlockSpec((rows, step), lambda i: (0, i))
    return pl.pallas_call(
        active_back_kernel,
        grid=(units // step,),
        in_specs=[once((rows, width)), pl.BlockSpec((step, width), lambda i: (i, 0)), cols],
        out_specs=[cols, pl.BlockSpec((1, step), lambda i: (0, i))],
        out_shape=[jax.ShapeDtypeStruct((rows, units), bf16), jax.ShapeDtypeStruct((1, units), f32)],
        compiler_params=params(62),
        cost_estimate=cost(2 * rows * width * units, 27 * MIB),
        name="active_back",
    )(dffn, w_down, der)


def feed_back_kernel(
    dup_ref, wup_ref, dresid2_hbm, hat_hbm, rstd_hbm, gain_ref, wo_hbm,
    dresid1_hbm, dbranch_hbm, datt_hbm, sums_ref,
    acc_ref, dresid_ref, hat_ref, rstd_ref, wo_ref, dbranch_ref, datt_ref, in_sem, out_sem,
):
    step = pl.program_id(0)
    loads = [
        pltpu.make_async_copy(hbm, ref, in_sem.at[i])
        for i, (hbm, ref) in enumerate(
            ((dresid2_hbm, dresid_ref), (hat_hbm, hat_ref), (rstd_hbm, rstd_ref), (wo_hbm, wo_ref))
        )
    ]

    @pl.when(step == 0)
    def _():
        for load in loads:
            load.start()

    part = mm(dup_ref[...], wup_ref[...], NT)

    @pl.when(step == 0)
    def _():
        acc_ref[...] = part

    @pl.when(step > 0)
    def _():
        acc_ref[...] += part

    @pl.when(step == pl.num_programs(0) - 1)
    def _():
        for load in loads:
            load.wait()
        sums = [0.0, 0.0, 0.0]
        copies = []
        for i, at in enumerate(range(0, acc_ref.shape[0], PAIR)):
            span = slice(at, at + PAIR)
            dnormed = acc_ref[span, :] + dresid_ref[span, :]
            hat = hat_ref[span, :]
            dresid = norm_back(dnormed, hat, rstd_ref[span, :1], line(gain_ref))
            dresid_ref[span, :] = dresid
            dbranch = dresid.astype(bf16)
            dbranch_ref[span, :] = dbranch
            datt_ref[span, :] = mm(dbranch, wo_ref[...], NT).astype(bf16)
            sums[0] += column_sum(dnormed * hat)
            sums[1] += column_sum(dnormed)
            sums[2] += column_sum(dbranch.astype(f32))
            outs = ((dresid_ref, dresid1_hbm), (dbranch_ref, dbranch_hbm), (datt_ref, datt_hbm))
            copies += stream_out(i, at, outs, out_sem)
        for i in range(3):
            sums_ref[i : i + 1, :] = sums[i]
        for copy in copies:
            copy.wait()


def feed_back(dup, w_up, dresid2, hat, rstd, w_out, gain):
    rows, width = hat.shape
    units = w_up.shape[1]
    step = 1024
    anywhere = pl.BlockSpec(memory_space=pl.ANY)
    return pl.pallas_call(
        feed_back_kernel,
        grid=(units // step,),
        in_specs=[
            pl.BlockSpec((rows, step), lambda i: (0, i)),
            pl.BlockSpec((width, step), lambda i: (0, i)),
            anywhere, anywhere, anywhere, vector(width), anywhere,
        ],
        out_specs=[anywhere, anywhere, anywhere, whole((8, width))],
        out_shape=[
            jax.ShapeDtypeStruct((rows, width), f32),
            jax.ShapeDtypeStruct((rows, width), bf16),
            jax.ShapeDtypeStruct((rows, width), bf16),
            jax.ShapeDtypeStruct((8, width), f32),
        ],
        scratch_shapes=[
            pltpu.VMEM((rows, width), f32),
            pltpu.VMEM((rows, width), f32),
            pltpu.VMEM((rows, width), f32),
            pltpu.VMEM((rows, 128), f32),
            pltpu.VMEM((width, width), bf16),
            pltpu.VMEM((rows, width), bf16),
            pltpu.VMEM((rows, width), bf16),
            pltpu.SemaphoreType.DMA((4,)),
            pltpu.SemaphoreType.DMA((3, rows // PAIR)),
        ],
        compiler_params=params(62),
        cost_estimate=cost(2 * rows * width * units, 36 * MIB),
        name="feed_back",
    )(dup, w_up, dresid2, hat, rstd, gain, w_out)


def attend_back_kernel(ids_ref, lengths_ref, qkv_ref, datt_ref, cos_ref, sin_ref, dmixed_ref, sums_ref, mask_ref):
    width = datt_ref.shape[1]
    block = pl.program_id(0)
    cosine = table_here(ids_ref, lengths_ref, cos_ref, block)
    sine = table_here(ids_ref, lengths_ref, sin_ref, block)
    mask_ref[...] = jnp.where(same_segment(ids_ref, lengths_ref, pl.program_id(0)), 0.0, masked_value)
    lane = lax.broadcasted_iota(jnp.int32, (PAIR, 2 * HD), 1)

    @pl.when(pl.program_id(0) == 0)
    def _():
        sums_ref[...] = jnp.zeros_like(sums_ref)

    mask = mask_ref[...]
    masks = (lane < HD, lane >= HD)
    group = 4
    for begin in range(0, width // (2 * HD), group):
        spots = [pair * 2 * HD for pair in range(begin, begin + group)]
        heads = [(at, m) for at in spots for m in masks]
        read = lambda ref, at: ref[:, at : at + 2 * HD]
        pick = lambda ref, at, m: jnp.where(m, read(ref, at), jnp.zeros((PAIR, 2 * HD), bf16))
        scores = [mm(read(qkv_ref, width + at), pick(qkv_ref, at, m), NT) + mask for at, m in heads]
        terms = [jnp.exp(x - jnp.max(x, 0, keepdims=True)) for x in scores]
        dweights = [mm(read(qkv_ref, 2 * width + at), pick(datt_ref, at, m), NT) for at, m in heads]
        weights = [x * (1.0 / jnp.sum(x, 0, keepdims=True)) for x in terms]
        dvalues = [mm(w.astype(bf16), pick(datt_ref, at, m)) for w, (at, m) in zip(weights, heads)]
        moved = [w * d for w, d in zip(weights, dweights)]
        dscores = [(m - w * jnp.sum(m, 0, keepdims=True)).astype(bf16) for w, m in zip(weights, moved)]
        dkeys = [mm(d, pick(qkv_ref, at, m)) for d, (at, m) in zip(dscores, heads)]
        dqueries = [mm(d, pick(qkv_ref, width + at, m), TN) for d, (at, m) in zip(dscores, heads)]
        for k, at in enumerate(spots):
            dquery, dkey, dvalue = (x[2 * k] + x[2 * k + 1] for x in (dqueries, dkeys, dvalues))
            dquery = dquery * score_scale
            dquery = dquery * cosine - partner(dquery) * sine
            dkey = dkey * cosine - partner(dkey) * sine
            for i, grad in enumerate((dquery, dkey, dvalue)):
                low = grad.astype(bf16)
                dmixed_ref[:, i * width + at : i * width + at + 2 * HD] = low
                sums_ref[:, i * width + at : i * width + at + 2 * HD] += column_sum(low.astype(f32))


def attend_back(ids, lengths, qkv, datt, tables):
    rows, width = datt.shape
    block = lambda cols: pl.BlockSpec((PAIR, cols), lambda i, *_: (i, 0))
    return pl.pallas_call(
        attend_back_kernel,
        grid_spec=pltpu.PrefetchScalarGridSpec(
            num_scalar_prefetch=2,
            grid=(rows // PAIR,),
            in_specs=[block(3 * width), block(width), once(tables[0].shape), once(tables[0].shape)],
            out_specs=[block(3 * width), whole((1, 3 * width))],
            scratch_shapes=[pltpu.VMEM((PAIR, PAIR), f32)],
        ),
        out_shape=[jax.ShapeDtypeStruct((rows, 3 * width), bf16), jax.ShapeDtypeStruct((1, 3 * width), f32)],
        compiler_params=params(62),
        cost_estimate=cost(2e10, 16 * MIB),
        name="attend_back",
    )(ids, lengths, qkv, datt, *tables)


def input_grad_kernel(dmixed_ref, w_ref, dresid_ref, out_ref):
    out_ref[...] = dresid_ref[...] + mm(dmixed_ref[...], w_ref[...], NT)


def input_grad(dmixed, w_qkv, dresid):
    rows, width = dresid.shape
    block = lambda cols: pl.BlockSpec((PAIR, cols), lambda i: (i, 0))
    return pl.pallas_call(
        input_grad_kernel,
        grid=(rows // PAIR,),
        in_specs=[block(3 * width), once((width, 3 * width)), block(width)],
        out_specs=block(width),
        out_shape=jax.ShapeDtypeStruct((rows, width), f32),
        compiler_params=params(62),
        cost_estimate=cost(6 * rows * width * width, 20 * MIB),
        name="input_grad",
    )(dmixed, w_qkv, dresid)


def target_of(ids_ref, keep):
    return ids_ref[0] if keep else 1 - ids_ref[0]


def put(value, received, out_refs):
    if received is None:
        out_refs[0][...] = value.reshape(out_refs[0].shape).astype(bf16)
        return
    each, at = out_refs[0].shape[1], 0
    for out_ref in out_refs:
        count = out_ref.shape[0]
        part = value[at * each : (at + count) * each].reshape(out_ref.shape) + received[at : at + count].astype(f32)
        out_ref[...] = part.astype(out_ref.dtype)
        at += count


def outer_cols_kernel(counts, keep, slots, ids_ref, *refs):
    number = len(counts)
    received = refs[2 * number] if keep else None
    out_refs = refs[2 * number + 1 : -number] if keep else refs[2 * number : 2 * number + 1]
    turned_refs = refs[-number:]
    step = pl.program_id(0)
    each = turned_refs[0].shape[0] // slots
    target = target_of(ids_ref, keep)

    @pl.when(step == 0)
    def _():
        for left_ref, turned_ref in zip(refs[0 : 2 * number : 2], turned_refs):
            for at in range(0, left_ref.shape[1], 128):
                turned = left_ref[:, at : at + 128].T.astype(turned_ref.dtype)
                for k in range(128 // each):
                    rel = (at // each + k) ^ ids_ref[1]
                    slot = choose(target, lambda order: slot_of(rel, order), slots)
                    turned_ref[pl.ds(pl.multiple_of(slot * each, each), each), :] = turned[k * each : (k + 1) * each]

    done = 0
    for i, count in enumerate(counts):

        @pl.when((step >= done) & (step < done + count))
        def _(right_ref=refs[2 * i + 1], turned_ref=turned_refs[i]):
            put(mm(turned_ref[...].astype(bf16), right_ref[...]), received, out_refs)

        done += count


def outer_cols(ids, pairs, slots, received=None, parts=1, begin_at=0):
    rows = pairs[0][0].shape[1] // 2
    each = rows // slots
    keep = received is not None
    step = 1024
    specs, args, counts = [], [], []
    for left, right, begin, number in pairs:
        count = number // step
        first = sum(counts)
        specs.append(
            pl.BlockSpec((left.shape[0], rows), lambda i, ids: (0, target_of(ids, keep)), pipeline_mode=pl.Buffered(1))
        )
        specs.append(
            pl.BlockSpec(
                (right.shape[0], step),
                lambda i, *_, first=first, count=count, at=begin // step: (0, at + jnp.clip(i - first, 0, count - 1)),
            )
        )
        args += [left, right]
        counts.append(count)
    cols = sum(counts) * step
    spec = lambda count: pl.BlockSpec((count, each, step), lambda i, *_: (0, 0, i))
    shape = lambda count, kind: jax.ShapeDtypeStruct((count, each, cols), kind)
    if keep:
        specs.append(pl.BlockSpec((slots, each, step), lambda i, *_: (0, 0, begin_at // step + i)))
        args.append(received)
        outs = [spec(slots // 2)] + [spec(slots // 2 // parts)] * parts
        shapes = [shape(slots // 2, f32)] + [shape(slots // 2 // parts, bf16)] * parts
    else:
        outs, shapes = [spec(slots)], [shape(slots, bf16)]
    kind = bf16 if each % 16 == 0 else f32
    out = pl.pallas_call(
        functools.partial(outer_cols_kernel, counts, keep, slots),
        grid_spec=pltpu.PrefetchScalarGridSpec(
            num_scalar_prefetch=1, grid=(sum(counts),), in_specs=specs, out_specs=outs,
            scratch_shapes=[pltpu.VMEM((rows, left.shape[0]), kind) for left, *_ in pairs],
        ),
        out_shape=shapes,
        compiler_params=params(62),
        cost_estimate=cost(2 * args[0].shape[0] * rows * cols, (20 if keep else 15) * MIB),
        name="outer_cols",
    )(ids, *args)
    return out if keep else out[0]


def outer_rows_kernel(group, slots_apart, keep, ids_ref, *refs):
    left_refs, (right_ref, final_ref, dproj_ref) = refs[:group], refs[group : group + 3]
    received = refs[group + 3] if keep else None
    out_refs, proj_ref = refs[group + (4 if keep else 3) : -1], refs[-1]
    left = jnp.concatenate([ref[...].reshape(ref.shape[-2:]) for ref in left_refs], 1)
    value = mm(left, right_ref[...], TN)
    proj_ref[...] = mm(final_ref[...], dproj_ref[...], TN)
    tall, width = out_refs[0].shape[-2], value.shape[1]
    each = value.shape[0] // group
    short = proj_ref.shape[0] // group
    pieces = width // PROJ
    half = group // 2
    target = target_of(ids_ref, keep)
    for j in range(group):
        slot = j * slots_apart + pl.program_id(0)
        block = (choose(target, lambda order: rel_of(slot, order), group * slots_apart) ^ ids_ref[1]) & (group - 1)
        part = value[j * each : (j + 1) * each, :]
        small = proj_ref[pl.ds(pl.multiple_of(block * short, short), short), :]
        fold = short // pieces if short >= pieces else 1
        low = [small[i * fold : (i + 1) * fold, :] for i in range(short // fold)]
        if keep:
            part = part + received[j, 0, :each, :].astype(f32)
            low = [
                x + received[j, 0, each : each + fold, i * PROJ : (i + 1) * PROJ].astype(f32) for i, x in enumerate(low)
            ]
            out_ref, at = (out_refs[0], j) if j < half else (out_refs[1 + 2 * (j - half) // half], j % (half // 2))
        else:
            out_ref, at = out_refs[0], j
        kind = out_ref.dtype
        out_ref[at, 0, :each, :] = part.astype(kind)
        out_ref[at, 0, each:, :] = jnp.zeros((tall - each, width), kind)
        for i, x in enumerate(low):
            out_ref[at, 0, each : each + fold, i * PROJ : (i + 1) * PROJ] = x.astype(kind)


def outer_rows(ids, left, right, final, dproj, slots, group, received=None):
    tokens_here, rows = left.shape
    width = right.shape[1]
    rest = slots // group
    each = rows // (2 * slots)
    tall = each + 8
    keep = received is not None
    spec = lambda count: pl.BlockSpec((count, 1, tall, width), lambda i, *_: (0, i, 0, 0))
    shape = lambda count, kind: jax.ShapeDtypeStruct((count, rest, tall, width), kind)

    def owner(slot, ids):
        target = target_of(ids, keep)
        return target * slots + (choose(target, lambda order: rel_of(slot, order), slots) ^ ids[1])

    specs = [
        pl.BlockSpec((tokens_here, each), lambda i, ids, j=j: (0, owner(j * rest + i, ids))) for j in range(group)
    ]
    lefts = [left] * group
    if each < 128:
        specs = [
            pl.BlockSpec((1, tokens_here, each), lambda i, ids, j=j: (owner(j * rest + i, ids), 0, 0)) for j in range(group)
        ]
        lefts = [left.reshape(tokens_here, -1, each).transpose(1, 0, 2)] * group
    specs += [
        once((tokens_here, width)),
        pl.BlockSpec((tokens_here, final.shape[1] // (2 * rest)), lambda i, ids: (0, owner(i, ids) // group)),
        once((tokens_here, PROJ)),
    ]
    args = lefts + [right, final, dproj]
    if keep:
        specs.append(spec(group))
        args.append(received.reshape(group, rest, tall, width))
        outs = [spec(group // 2), spec(group // 4), spec(group // 4)]
        shapes = [shape(group // 2, f32), shape(group // 4, bf16), shape(group // 4, bf16)]
    else:
        outs, shapes = [spec(group)], [shape(group, bf16)]
    out = pl.pallas_call(
        functools.partial(outer_rows_kernel, group, rest, keep),
        grid_spec=pltpu.PrefetchScalarGridSpec(
            num_scalar_prefetch=1, grid=(rest,), in_specs=specs, out_specs=outs,
            scratch_shapes=[pltpu.VMEM((final.shape[1] // (2 * rest), PROJ), f32)],
        ),
        out_shape=shapes,
        compiler_params=params(62),
        cost_estimate=cost(tokens_here * rows * width, (20 if keep else 15) * MIB),
        name="outer_rows",
    )(ids, *args)
    out = [o.reshape(-1, tall, width) for o in out]
    return out if keep else out[0]


def flips(count):
    bits = [1 << i for i in range(count.bit_length() - 1)]
    third = {16: 1, 64: 2}[count]
    swapped = bits[third : 2 * third] + bits[:third] + bits[2 * third :][::-1]
    return bits, swapped


def slot_of(rel, order):
    return sum(
        ((rel >> (flip.bit_length() - 1)) & 1) << (len(order) - 1 - i) for i, flip in enumerate(order)
    )


def rel_of(slot, order):
    return sum(
        ((slot >> (len(order) - 1 - i)) & 1) << (flip.bit_length() - 1) for i, flip in enumerate(order)
    )


def choose(core, function, count):
    first, second = (function(order) for order in flips(count))
    return jnp.where(core == 0, first, second)


def hop(values, stage, count):
    pairs = []
    for stream, order in enumerate(flips(count)):
        pairs += [(stream * count + i, stream * count + (i ^ order[stage])) for i in range(count)]
    return lax.ppermute(values, ("stream", "dp"), pairs)


def swap(values):
    return lax.ppermute(values, "stream", [(0, 1), (1, 0)])


def after(value, *others):
    return lax.optimization_barrier((value, *others))[0]


def gather_both(first, first_stages, second, second_stages, count):
    pending = [(first, list(first_stages)), (second, list(second_stages))]
    while any(stages for _, stages in pending):
        got = [hop(values, stages[-1], count) if stages else None for values, stages in pending]
        values = lax.optimization_barrier([x for pair in zip(pending, got) for x in (pair[0][0], pair[1]) if x is not None])
        joined = []
        for (_, stages), arrived in zip(pending, got):
            value = values.pop(0)
            if arrived is not None:
                value = jnp.concatenate([value, values.pop(0)], 0)
            joined.append((value, stages[:-1]))
        held = lax.optimization_barrier([value for value, _ in joined])
        pending = [(value, stages) for value, (_, stages) in zip(held, joined)]
    return [value for value, _ in pending]


def take_in(keep, got):
    half = keep.shape[0] // 2
    if half == 0:
        return keep[0] + got[0].astype(f32), None
    return keep[:half] + got[:half].astype(f32), (keep[half:] + got[half:].astype(f32)).astype(bf16)


def scatter_sum(keep, send, stage, count, got=None):
    if got is not None:
        keep, send = take_in(keep, got)
    while send is not None:
        keep, send = take_in(keep, hop(send, stage, count))
        stage += 1
    return keep


def total_sum(values, stage, count):
    for later in range(stage, count.bit_length() - 1):
        values = values + hop(values, later, count)
    return values


def body(
    tokens, doc_lengths, cand_docs, group_sizes, w_qkv, b_qkv, w_attn_out, b_attn_out, gain_one, bias_one,
    w_up, b_up, w_down, b_down, gain_two, bias_two, w_proj,
):
    stream = lax.axis_index("stream")
    me = lax.axis_index("dp")
    count = lax.axis_size("dp")
    hidden = tokens[0]
    rows, width = hidden.shape
    half = rows // 2
    ids = jnp.stack([stream, me]).astype(jnp.int32)
    tables = [jnp.asarray(table) for table in rotation_tables()]
    group = {16: 4, 64: 16}[count]

    hold = lax.optimization_barrier
    levels = {16: 2, 64: 4}[count]
    last_stage = count.bit_length() - 1
    shape = (count, levels)
    info = jnp.concatenate([cand_docs.reshape(QH, CAND), group_sizes.reshape(QH, 1)], 1).astype(jnp.int32)
    hidden_, info = hold((hidden, info))
    info_got = hop(info, last_stage - 1, count)
    qkv, attended, hat1, rstd1, normed = attend(
        ids, doc_lengths, hidden_, w_qkv, b_qkv, tables, w_attn_out, b_attn_out, gain_one, bias_one
    )
    info, info_got, normed = hold((info, info_got, normed))
    info = jnp.concatenate([info, info_got], 0)
    info, normed = hold((info, normed))
    info_got = hop(info, last_stage - 2, count)
    active, der, hat2, rstd2, final, projected, vecs = feed(
        normed, w_up, b_up, w_down, b_down, hat1, gain_one, bias_one, gain_two, bias_two, w_proj
    )
    info, info_got, vecs = hold((info, info_got, vecs))
    info = jnp.concatenate([info, info_got], 0)

    on_docs = stream == 1
    other = swap(jnp.where(on_docs, vecs[:half], vecs[half:]))
    own_docs = jnp.where(on_docs, vecs[half:], other)
    queries = jnp.where(on_docs, other, vecs[:half])
    queries, near = gather_both(queries, range(levels, last_stage), own_docs, range(levels), count)
    queries = queries.reshape(-1, QLEN, PROJ)
    far = swap(near)
    scores, entries = score(ids, info, doc_lengths, queries, near, far, shape)
    scores = total_sum(scores, levels, count)
    loss, dq_keep, dq_send, keep, send = score_back(
        ids, info, doc_lengths, entries, scores, queries, near, far, shape
    )
    loss = lax.dynamic_slice_in_dim(loss, (me >> levels) * QH, QH, 0)
    by_row = (-1, half, PROJ)
    keep, q_keep = keep.reshape(by_row), dq_keep.reshape(by_row)
    got, q_got = swap(send).reshape(by_row), hop(dq_send.reshape(by_row), levels, count)
    keep, got, q_keep, q_got = hold((keep, got, q_keep, q_got))
    keep, send = take_in(keep, got)
    q_keep, q_send = take_in(q_keep, q_got)
    keep, send, q_keep, q_send = hold((keep, send, q_keep, q_send))
    got, q_got = hop(send, 0, count), hop(q_send, levels + 1, count)
    keep, got, q_keep, q_got = hold((keep, got, q_keep, q_got))
    keep, send = take_in(keep, got)
    dqueries = scatter_sum(q_keep, None, last_stage, count, q_got)
    ddocs = scatter_sum(keep, send, 1, count)
    back = swap(jnp.where(on_docs, dqueries, ddocs))
    grad_vectors = jnp.where(
        on_docs, jnp.concatenate([back, ddocs], 0), jnp.concatenate([dqueries, back], 0)
    )

    def add_first(keep, got):
        half = keep.shape[0] // 2
        return (keep[half:] + got.astype(f32)).astype(bf16)

    def add_second(keep, got):
        half = keep.shape[0] // 2
        return keep[:half] + got.astype(f32)

    dproj, dresid2, dffn, sums2 = head_back(grad_vectors, projected, w_proj, hat2, rstd2, gain_two)
    down = lambda left, received=None: outer_rows(
        ids, left, dffn, final, dproj, count, group, received
    )
    units = w_up.shape[1]
    up = lambda left, received=None: outer_cols(ids, [(left, dup, 0, units)], count, received)
    mix_out = lambda left: outer_cols(ids, [(left, dmixed, 0, 3 * width), (attended, dbranch, 0, width)], count)
    mix_a = lambda left, received: outer_cols(ids, [(left, dmixed, 0, 2 * width)], count, received)
    mix_b = lambda left, received: outer_cols(
        ids, [(left, dmixed, 2 * width, width), (attended, dbranch, 0, width)], count, received, 1, 2 * width
    )

    d_out = down(active)
    d_got = swap(d_out)
    dffn_, d_out = hold((dffn, d_out))
    dup, sum_up = active_back(dffn_, w_down, der)
    active_, d_got, dup = hold((active, d_got, dup))
    d_keep, d_low, d_high = down(active_, d_got)
    d_high, d_low, normed_, d_keep = hold((d_high, d_low, normed, d_keep))
    u_out = up(normed_)
    d_high, d_low, u_out, dup_ = hold((d_high, d_low, u_out, dup))
    d_high_got, d_low_got, u_got = hop(d_high, 0, count), hop(d_low, 0, count), swap(u_out)
    dresid1, dbranch, dattended, sums1 = feed_back(dup_, w_up, dresid2, hat1, rstd1, w_attn_out, gain_one)
    d_keep, d_high_got, d_low_got, dbranch = hold((d_keep, d_high_got, d_low_got, dbranch))
    d_send = add_first(d_keep, d_high_got)
    d_keep = add_second(d_keep, d_low_got)
    d_keep, d_send, normed_, u_got = hold((d_keep, d_send, normed, u_got))
    d_got = hop(d_send, 1, count)
    u_keep, u_send = up(normed_, u_got)
    d_keep, d_got, u_keep = hold((d_keep, d_got, u_keep))
    d_keep, d_send = take_in(d_keep, d_got)
    u_send, d_keep, d_send, dattended = hold((u_send, d_keep, d_send, dattended))
    u_got, d_got = hop(u_send, 0, count), hop(d_send, 2, count)
    dmixed, sum_qkv = attend_back(ids, doc_lengths, qkv, dattended, tables)
    d_keep, d_got, u_keep, u_got, dmixed = hold((d_keep, d_got, u_keep, u_got, dmixed))
    u_keep, u_send = take_in(u_keep, u_got)
    d_keep, d_send = take_in(d_keep, d_got)
    sums = [sum_qkv[0], sums1[2], sums1[0], sums1[1], sum_up[0], sums2[2], sums2[0], sums2[1]]
    late = jnp.concatenate([v.reshape(2 * count, -1) for v in sums], 1)
    u_send, u_keep, hidden_, late, d_keep, d_send = hold((u_send, u_keep, hidden, late, d_keep, d_send))
    u_got, l_got, d_got = hop(u_send, 1, count), swap(late), hop(d_send, 3, count)
    m_out = mix_out(hidden_)
    m_out, late, l_got, u_keep, u_got, d_keep, d_got = hold((m_out, late, l_got, u_keep, u_got, d_keep, d_got))
    g_down = scatter_sum(d_keep, d_send, 4, count, d_got)
    u_keep, u_send = take_in(u_keep, u_got)
    late = late + l_got
    m_out, hidden_, late, g_down, u_send, u_keep = hold((m_out, hidden_, late, g_down, u_send, u_keep))
    m_got, l_got, u_got = swap(m_out), hop(late, 0, count), hop(u_send, 2, count)
    a_keep, a_send = mix_a(hidden_, m_got)
    u_keep, u_got, a_send, late, l_got = hold((u_keep, u_got, a_send, late, l_got))
    u_keep, u_send = take_in(u_keep, u_got)
    late = late + l_got
    u_keep, u_send, a_send, hidden_, late = hold((u_keep, u_send, a_send, hidden_, late))
    a_got, u_got, l_got = hop(a_send, 0, count), hop(u_send, 3, count), hop(late, 1, count)
    b_keep, b_send = mix_b(hidden_, m_got)
    u_keep, u_got, b_keep, late, l_got = hold((u_keep, u_got, b_keep, late, l_got))
    g_up = scatter_sum(u_keep, u_send, 4, count, u_got)
    late = late + l_got
    a_keep, a_got, g_up, b_send, late = hold((a_keep, a_got, g_up, b_send, late))
    a_keep, a_send = take_in(a_keep, a_got)
    a_keep, a_send, b_send, dmixed_, late = hold((a_keep, a_send, b_send, dmixed, late))
    a_got, b_got = hop(a_send, 1, count), hop(b_send, 0, count)
    l_got = hop(late, 2, count)
    grad_hidden = input_grad(dmixed_, w_qkv, dresid1)
    a_keep, a_got, grad_hidden, b_got = hold((a_keep, a_got, grad_hidden, b_got))
    b_keep, b_send = take_in(b_keep, b_got)
    b_got = hop(b_send, 1, count)
    a_keep, a_send = take_in(a_keep, a_got)
    g_a = scatter_sum(a_keep, a_send, 2, count)
    b_keep, b_send = take_in(b_keep, b_got)
    g_b = scatter_sum(b_keep, b_send, 2, count)

    late = total_sum(late + l_got, 3, count)
    mine = lax.dynamic_slice_in_dim(late, stream * count + me, 1, 0)[0]
    sizes = [v.shape[0] // (2 * count) for v in sums]
    parts = [mine[end - size : end] for end, size in zip(np.cumsum(sizes), sizes)]
    g_bqkv, g_bout, g_gain1, g_bias1, g_bup, g_bdown, g_gain2, g_bias2 = parts
    tall = w_down.shape[0] // (2 * count)
    short = width // (2 * count)
    pieces = width // PROJ
    fold = max(short // pieces, 1)
    g_proj = g_down[tall : tall + fold].reshape(fold, pieces, PROJ).transpose(1, 0, 2)[: short // fold].reshape(short, PROJ)
    return (
        loss[:, 0][None, None, :],
        grad_hidden[None],
        jnp.concatenate([g_a, g_b[:, :width]], 1),
        g_bqkv,
        g_b[:, width:],
        g_bout,
        g_gain1,
        g_bias1,
        g_up,
        g_bup,
        g_down[:tall],
        g_bdown,
        g_gain2,
        g_bias2,
        g_proj,
    )


def solution(mesh):
    every = P(("stream", "dp"))
    rows = P(("stream", "dp"), None)
    return jax.shard_map(
        body,
        mesh=mesh,
        in_specs=(P("stream", "dp", None), P(), P("dp", "stream", None, None), P("dp", "stream", None)) + (P(),) * 13,
        out_specs=(
            P("dp", "stream", None), P("stream", "dp", None), rows, every, rows, every, every, every, rows, every,
            rows, every, every, every, rows,
        ),
        check_vma=False,
    )
```

```python
import functools
import math

import jax
import jax.numpy as jnp
import numpy as np
from jax import lax
from jax.experimental import pallas as pl
from jax.experimental.pallas import tpu as pltpu
from jax.sharding import PartitionSpec as P

HD = 64
PROJ = 128
QLEN = 32
CAND = 8
QH = 16
PAIR = 256

score_scale = 0.125
sim_temp = 0.05
loss_temp = 0.08
masked_value = -1e30
norm_eps = 1e-05
vector_eps = 1e-06

f32 = jnp.float32
bf16 = jnp.bfloat16
MIB = 1 << 20

NN = (((1,), (0,)), ((), ()))
NT = (((1,), (1,)), ((), ()))
TN = (((0,), (0,)), ((), ()))


def mm(left, right, dims=NN):
    return lax.dot_general(left, right, dims, preferred_element_type=f32)


def params(mib):
    return pltpu.CompilerParams(vmem_limit_bytes=mib * MIB)


def cost(flops, moved):
    return pl.CostEstimate(flops=int(flops), bytes_accessed=int(moved), transcendentals=0)


def whole(shape):
    return pl.BlockSpec(shape, lambda *_: (0,) * len(shape))


def vector(length):
    return pl.BlockSpec((length,), lambda *_: (0,), pipeline_mode=pl.Buffered(1))


def line(ref):
    return ref[...].astype(f32)[None, :]


def once(shape):
    return pl.BlockSpec(shape, lambda *_: (0,) * len(shape), pipeline_mode=pl.Buffered(1))


def rotation_tables():
    freq = np.exp(np.arange(HD // 2) * (-2.0 * math.log(10000.0) / HD))
    lane = np.arange(2 * HD)
    place = np.concatenate([np.arange(PAIR) % QLEN, np.arange(PAIR), np.arange(PAIR)])
    angle = place[:, None] * freq[lane % (HD // 2)][None, :]
    sign = np.where(lane % HD < HD // 2, -1.0, 1.0)[None, :]
    return np.cos(angle).astype(np.float32), (np.sin(angle) * sign).astype(np.float32)


def first_length(ids_ref, lengths_ref, block):
    return lengths_ref[ids_ref[1], 2 * block]


def table_here(ids_ref, lengths_ref, table_ref, block):
    first = first_length(ids_ref, lengths_ref, block)
    row = lax.broadcasted_iota(jnp.int32, (PAIR, 2 * HD), 0)
    moved = table_ref[pl.ds(2 * PAIR - first, PAIR), :]
    doc = jnp.where(row < first, table_ref[PAIR : 2 * PAIR, :], moved)
    return jnp.where(ids_ref[0] == 1, doc, table_ref[:PAIR, :])


def partner(values):
    lane = lax.broadcasted_iota(jnp.int32, values.shape, 1)
    ahead = pltpu.roll(values, 2 * HD - HD // 2, 1)
    behind = pltpu.roll(values, HD // 2, 1)
    return jnp.where(lane % HD < HD // 2, ahead, behind)


def same_segment(ids_ref, lengths_ref, block):
    is_doc = ids_ref[0] == 1
    first = first_length(ids_ref, lengths_ref, block)
    row = lax.broadcasted_iota(jnp.int32, (PAIR, PAIR), 0)
    col = lax.broadcasted_iota(jnp.int32, (PAIR, PAIR), 1)
    doc = ((row >= first) ^ (col >= first)).astype(jnp.int32)
    query = ((row // QLEN) ^ (col // QLEN)).astype(jnp.int32)
    return jnp.where(is_doc, doc, query) == 0


def normalise(values):
    mean = jnp.mean(values, -1, keepdims=True)
    center = values - mean
    rstd = lax.rsqrt(jnp.mean(center * center, -1, keepdims=True) + norm_eps)
    return center * rstd, rstd


def norm_back(grad, hat, rstd, gain):
    scaled = grad * gain
    return (
        scaled - jnp.mean(scaled, -1, keepdims=True) - hat * jnp.mean(scaled * hat, -1, keepdims=True)
    ) * rstd


def column_sum(values):
    return jnp.sum(values, 0, keepdims=True)


def attend_kernel(
    ids_ref, lengths_ref, x_ref, wqkv_ref, bqkv_ref, cos_ref, sin_ref, wo_ref, bo_ref, g_ref, c_ref,
    qkv_ref, att_ref, hat_ref, rstd_ref, normb_ref, mask_ref,
):
    width = x_ref.shape[1]
    x = x_ref[...]
    block = pl.program_id(0)
    cosine = table_here(ids_ref, lengths_ref, cos_ref, block)
    sine = table_here(ids_ref, lengths_ref, sin_ref, block)
    step = 512
    for start in range(0, 3 * width, step):
        mixed = mm(x, wqkv_ref[:, start : start + step]) + bqkv_ref[start : start + step].astype(f32)[None, :]
        if start < 2 * width:
            parts = []
            for off in range(0, step, 2 * HD):
                one = mixed[:, off : off + 2 * HD]
                one = one * cosine + partner(one) * sine
                parts.append(one.astype(bf16))
            mixed = jnp.concatenate(parts, 1)
            if start < width:
                mixed = mixed * jnp.asarray(score_scale, bf16)
        qkv_ref[:, start : start + step] = mixed.astype(bf16)
    mask_ref[...] = jnp.where(same_segment(ids_ref, lengths_ref, pl.program_id(0)), 0.0, masked_value)
    lane = lax.broadcasted_iota(jnp.int32, (PAIR, 2 * HD), 1)
    mask = mask_ref[...]
    group = 4
    for begin in range(0, width // (2 * HD), group):
        heads = [(pair * 2 * HD, head) for pair in range(begin, begin + group) for head in range(2)]
        mine = lambda head: (lane < HD) if head == 0 else (lane >= HD)
        pick = lambda at, head: jnp.where(mine(head), qkv_ref[:, at : at + 2 * HD], jnp.zeros((PAIR, 2 * HD), bf16))
        scores = [mm(qkv_ref[:, at : at + 2 * HD], pick(width + at, head), NT) + mask for at, head in heads]
        terms = [jnp.exp(s - jnp.max(s, -1, keepdims=True)) for s in scores]
        weights = [(t * (1.0 / jnp.sum(t, -1, keepdims=True))).astype(bf16) for t in terms]
        parts = [mm(w, pick(2 * width + at, head)) for w, (at, head) in zip(weights, heads)]
        for k in range(group):
            at = heads[2 * k][0]
            att_ref[:, at : at + 2 * HD] = (parts[2 * k] + parts[2 * k + 1]).astype(bf16)
    branch = mm(att_ref[...], wo_ref[...]) + line(bo_ref)
    hat, rstd = normalise(x.astype(f32) + branch)
    hat_ref[...] = hat
    rstd_ref[...] = jnp.broadcast_to(rstd, rstd_ref.shape)
    normb_ref[...] = (hat * line(g_ref) + line(c_ref)).astype(bf16)


def attend(ids, lengths, x, w_qkv, b_qkv, tables, w_out, b_out, gain, bias):
    rows, width = x.shape
    block = lambda cols: pl.BlockSpec((PAIR, cols), lambda i, *_: (i, 0))
    return pl.pallas_call(
        attend_kernel,
        grid_spec=pltpu.PrefetchScalarGridSpec(
            num_scalar_prefetch=2,
            grid=(rows // PAIR,),
            in_specs=[
                block(width), once((width, 3 * width)), vector(3 * width), once(tables[0].shape),
                once(tables[0].shape), once((width, width)), vector(width), vector(width), vector(width),
            ],
            out_specs=[block(3 * width), block(width), block(width), block(128), block(width)],
            scratch_shapes=[pltpu.VMEM((PAIR, PAIR), f32)],
        ),
        out_shape=[
            jax.ShapeDtypeStruct((rows, 3 * width), bf16),
            jax.ShapeDtypeStruct((rows, width), bf16),
            jax.ShapeDtypeStruct((rows, width), f32),
            jax.ShapeDtypeStruct((rows, 128), f32),
            jax.ShapeDtypeStruct((rows, width), bf16),
        ],
        compiler_params=params(62),
        cost_estimate=cost(2 * rows * width * 4 * width, 30 * MIB),
        name="attend",
    )(ids, lengths, x, w_qkv, b_qkv, *tables, w_out, b_out, gain, bias)


def stream_out(i, at, pairs, sem):
    copies = [
        pltpu.make_async_copy(ref.at[pl.ds(at, PAIR)], hbm.at[pl.ds(at, PAIR)], sem.at[j, i])
        for j, (ref, hbm) in enumerate(pairs)
    ]
    for copy in copies:
        copy.start()
    return copies


def feed_kernel(
    x_ref, wup_ref, bup_ref, wdown_ref, bdown_ref, hat1_ref, g1_ref, c1_ref, g2_ref, c2_ref, wproj_ref,
    act_ref, der_ref, hat2_hbm, rstd2_ref, final_hbm, proj_ref, vec_ref,
    acc_ref, hat_ref, final_ref, in_sem, out_sem,
):
    step = pl.program_id(0)
    load = pltpu.make_async_copy(hat1_ref, hat_ref, in_sem)

    @pl.when(step == 0)
    def _():
        load.start()

    upward = mm(x_ref[...], wup_ref[...]) + line(bup_ref)
    below = 0.5 + 0.5 * lax.erf(upward * (2.0**-0.5))
    density = jnp.exp(-0.5 * upward * upward) * ((2.0 * math.pi) ** -0.5)
    active = (upward * below).astype(bf16)
    act_ref[...] = active
    der_ref[...] = (below + upward * density).astype(bf16)
    part = mm(active, wdown_ref[...])

    @pl.when(step == 0)
    def _():
        acc_ref[...] = part

    @pl.when(step > 0)
    def _():
        acc_ref[...] += part

    @pl.when(step == pl.num_programs(0) - 1)
    def _():
        load.wait()
        copies = []
        for i, at in enumerate(range(0, acc_ref.shape[0], PAIR)):
            span = slice(at, at + PAIR)
            normed = hat_ref[span, :] * line(g1_ref) + line(c1_ref)
            hat, rstd = normalise(normed + acc_ref[span, :] + line(bdown_ref))
            hat_ref[span, :] = hat
            rstd2_ref[span, :] = jnp.broadcast_to(rstd, (PAIR, 128))
            final = (hat * line(g2_ref) + line(c2_ref)).astype(bf16)
            final_ref[span, :] = final
            copies += stream_out(i, at, ((hat_ref, hat2_hbm), (final_ref, final_hbm)), out_sem)
            projected = mm(final, wproj_ref[...])
            proj_ref[span, :] = projected
            inverse = lax.rsqrt(jnp.sum(projected * projected, -1, keepdims=True) + vector_eps)
            vec_ref[span, :] = (projected * inverse).astype(bf16)
        for copy in copies:
            copy.wait()


def feed(x, w_up, b_up, w_down, b_down, hat1, g1, c1, g2, c2, w_proj):
    rows, width = x.shape
    units = w_up.shape[1]
    step = 1024
    cols = pl.BlockSpec((rows, step), lambda i: (0, i))
    anywhere = pl.BlockSpec(memory_space=pl.ANY)
    return pl.pallas_call(
        feed_kernel,
        grid=(units // step,),
        in_specs=[
            once((rows, width)),
            pl.BlockSpec((width, step), lambda i: (0, i)),
            pl.BlockSpec((step,), lambda i: (i,)),
            pl.BlockSpec((step, width), lambda i: (i, 0)),
            vector(width), anywhere, vector(width), vector(width), vector(width), vector(width),
            once((width, PROJ)),
        ],
        out_specs=[cols, cols, anywhere, whole((rows, 128)), anywhere, whole((rows, PROJ)), whole((rows, PROJ))],
        out_shape=[
            jax.ShapeDtypeStruct((rows, units), bf16),
            jax.ShapeDtypeStruct((rows, units), bf16),
            jax.ShapeDtypeStruct((rows, width), f32),
            jax.ShapeDtypeStruct((rows, 128), f32),
            jax.ShapeDtypeStruct((rows, width), bf16),
            jax.ShapeDtypeStruct((rows, PROJ), f32),
            jax.ShapeDtypeStruct((rows, PROJ), bf16),
        ],
        scratch_shapes=[
            pltpu.VMEM((rows, width), f32),
            pltpu.VMEM((rows, width), f32),
            pltpu.VMEM((rows, width), bf16),
            pltpu.SemaphoreType.DMA,
            pltpu.SemaphoreType.DMA((2, rows // PAIR)),
        ],
        compiler_params=params(62),
        cost_estimate=cost(4 * rows * width * units, 50 * MIB),
        name="feed",
    )(x, w_up, b_up, w_down, b_down, hat1, g1, c1, g2, c2, w_proj)


UNROLL = 8


def load_docs(near_ref, far_ref, docs_ref, sem):
    half_rows = near_ref.shape[0]
    copies = [
        pltpu.make_async_copy(near_ref, docs_ref.at[pl.ds(0, half_rows)], sem.at[0]),
        pltpu.make_async_copy(far_ref, docs_ref.at[pl.ds(half_rows, half_rows)], sem.at[1]),
    ]
    for copy in copies:
        copy.start()
    return copies


def pair_scores(ids_ref, info_ref, length_ref, q_ref, docs_ref, entry, shape):
    count, levels = shape
    lane = lax.broadcasted_iota(jnp.int32, (QLEN, PAIR), 1)
    index = jnp.minimum(entry >> 3, q_ref.shape[0] - 1)
    doc = info_ref[index, entry & 7]
    row = doc >> 3
    pair = (doc >> 1) & 3
    first = length_ref[row, 2 * pair]
    odd = (doc & 1) == 1
    low = jnp.where(odd, first, 0)
    high = jnp.where(odd, PAIR, first)
    core = pair >> 1
    plane = 1 << levels
    rel = (row ^ ids_ref[1]) & (plane - 1)
    slot = choose(core, lambda order: slot_of(rel, order[:levels]), count)
    start = pl.multiple_of((((core ^ ids_ref[0]) * plane + slot) * 2 + (pair & 1)) * PAIR, PAIR)
    scaled = mm(q_ref[index], docs_ref[pl.ds(start, PAIR), :], NT) * (1.0 / sim_temp)
    return start, jnp.where((lane >= low) & (lane < high), scaled, masked_value)


def natural_row(ids_ref, entry, shape):
    count, levels = shape
    slot = entry >> (3 + QH.bit_length() - 1)
    rel = choose(ids_ref[0], lambda order: rel_of(slot, order[levels:]), count)
    z = (ids_ref[1] ^ rel) >> levels
    return z * QH + ((entry >> 3) & (QH - 1))


def score_kernel(
    shape, ids_ref, info_ref, length_ref, q_ref, near_ref, far_ref, score_ref, list_ref, docs_ref, sem,
):
    copies = load_docs(near_ref, far_ref, docs_ref, sem)
    count, levels = shape
    queries = q_ref.shape[0]
    score_ref[...] = jnp.zeros_like(score_ref)
    lane = lax.broadcasted_iota(jnp.int32, (1, 128), 1)
    z = ids_ref[1] >> levels

    def scan(q, found):
        size = info_ref[q, CAND]
        for c in range(CAND):
            here = ((info_ref[q, c] >> (3 + levels)) == z) & (c < size)
            list_ref[1 + found] = q * CAND + c
            found = found + here.astype(jnp.int32)
        return found

    found = lax.fori_loop(0, queries, scan, 0)
    list_ref[0] = found
    for u in range(UNROLL):
        list_ref[1 + found + u] = queries * CAND
    for j in range(QH):
        row = z * QH + j
        score_ref[pl.ds(row, 1), :] = jnp.where(lane == CAND, info_ref[j, CAND].astype(f32), 0.0)
    for copy in copies:
        copy.wait()

    @pl.loop(0, (found + UNROLL - 1) // UNROLL)
    def _(i):
        entries = [list_ref[1 + i * UNROLL + u] for u in range(UNROLL)]
        scaled = [pair_scores(ids_ref, info_ref, length_ref, q_ref, docs_ref, entry, shape)[1] for entry in entries]
        highest = [jnp.max(x, -1, keepdims=True) for x in scaled]
        totals = [jnp.sum(jnp.exp(x - m), -1, keepdims=True) for x, m in zip(scaled, highest)]
        results = [
            jnp.sum(sim_temp * (m + jnp.log(total)), 0, keepdims=True) for m, total in zip(highest, totals)
        ]
        for entry, result in zip(entries, results):
            row = jnp.where(entry >= queries * CAND, queries, natural_row(ids_ref, entry, shape))
            score_ref[pl.ds(row, 1), :] = jnp.where(lane == (entry & 7), result, score_ref[pl.ds(row, 1), :])


def score(ids, info, lengths, queries, near, far, shape):
    total = queries.shape[0]
    anywhere = pl.BlockSpec(memory_space=pl.ANY)
    return pl.pallas_call(
        functools.partial(score_kernel, shape),
        grid_spec=pltpu.PrefetchScalarGridSpec(
            num_scalar_prefetch=3,
            grid=(1,),
            in_specs=[whole(queries.shape), anywhere, anywhere],
            out_specs=[whole((total + 8, 128)), pl.BlockSpec(memory_space=pltpu.SMEM)],
            scratch_shapes=[pltpu.VMEM((2 * near.shape[0], PROJ), bf16), pltpu.SemaphoreType.DMA((2,))],
        ),
        out_shape=[
            jax.ShapeDtypeStruct((total + 8, 128), f32),
            jax.ShapeDtypeStruct((total * CAND + 2 * UNROLL,), jnp.int32),
        ],
        compiler_params=params(62),
        cost_estimate=cost(1e10, 4 * MIB),
        name="score",
    )(ids, info, lengths, queries, near, far)


def score_back_kernel(
    shape, ids_ref, info_ref, length_ref, list_ref, score_ref, q_ref, near_ref, far_ref,
    loss_ref, dq_keep_ref, dq_send_ref, keep_ref, send_ref, docs_ref, acc_ref, pull_ref, dq_ref, sem,
):
    copies = load_docs(near_ref, far_ref, docs_ref, sem)
    count, levels = shape
    queries = q_ref.shape[0]
    half_rows = near_ref.shape[0]
    scores = score_ref[:queries, :]
    lane = lax.broadcasted_iota(jnp.int32, (queries, 128), 1)
    size = jnp.sum(jnp.where(lane == CAND, scores, 0.0), -1, keepdims=True)
    counted = lane.astype(f32) < jnp.where(lane < CAND, size, 0.0)
    logits = jnp.where(counted, scores * (1.0 / loss_temp), masked_value)
    top = jnp.max(logits, -1, keepdims=True)
    norm = top + jnp.log(jnp.sum(jnp.exp(logits - top), -1, keepdims=True))
    positive = (lane == 0).astype(f32)
    pull_ref[:queries, :] = (jnp.exp(logits - norm) - positive) * (1.0 / loss_temp)
    pull_ref[queries:, :] = jnp.zeros((8, 128), f32)
    loss = norm - jnp.sum(logits * positive, -1, keepdims=True)
    loss_ref[...] = jnp.broadcast_to(loss, loss_ref.shape)
    dq_ref[...] = jnp.zeros_like(dq_ref)
    chunk = 512

    @pl.loop(0, 2 * half_rows // chunk)
    def _(i):
        acc_ref[pl.ds(pl.multiple_of(i * chunk, chunk), chunk), :] = jnp.zeros((chunk, PROJ), f32)

    for copy in copies:
        copy.wait()
    one = lax.broadcasted_iota(jnp.int32, (1, 128), 1)

    @pl.loop(0, (list_ref[0] + UNROLL - 1) // UNROLL)
    def _(i):
        entries = [list_ref[1 + i * UNROLL + u] for u in range(UNROLL)]
        found = [pair_scores(ids_ref, info_ref, length_ref, q_ref, docs_ref, entry, shape) for entry in entries]
        terms = [jnp.exp(scaled - jnp.max(scaled, -1, keepdims=True)) for _, scaled in found]
        totals = [jnp.sum(x, -1, keepdims=True) for x in terms]
        pulls = []
        for entry in entries:
            row = jnp.where(entry >= queries * CAND, queries, natural_row(ids_ref, entry, shape))
            pulls.append(
                jnp.sum(jnp.where(one == (entry & 7), pull_ref[pl.ds(row, 1), :], 0.0), -1, keepdims=True)
            )
        dsims = [(pull * (x * (1.0 / total))).astype(bf16) for pull, x, total in zip(pulls, terms, totals)]
        for entry, (start, _), dsim in zip(entries, found, dsims):
            index = entry >> 3
            acc_ref[pl.ds(start, PAIR), :] += mm(dsim, q_ref[jnp.minimum(index, queries - 1)], TN)
            dq_ref[index] += mm(dsim, docs_ref[pl.ds(start, PAIR), :])

    near_q = dq_keep_ref.shape[0]
    dq_keep_ref[...] = dq_ref[:near_q]
    dq_send_ref[...] = dq_ref[near_q:queries].astype(bf16)

    @pl.loop(0, half_rows // chunk)
    def _(i):
        at = pl.multiple_of(i * chunk, chunk)
        keep_ref[pl.ds(at, chunk), :] = acc_ref[pl.ds(at, chunk), :]
        send_ref[pl.ds(at, chunk), :] = acc_ref[pl.ds(half_rows + at, chunk), :].astype(bf16)


def score_back(ids, info, lengths, entries, scores, queries, near, far, shape):
    total = queries.shape[0]
    half_rows = near.shape[0]
    anywhere = pl.BlockSpec(memory_space=pl.ANY)
    half = (total // 2, QLEN, PROJ)
    return pl.pallas_call(
        functools.partial(score_back_kernel, shape),
        grid_spec=pltpu.PrefetchScalarGridSpec(
            num_scalar_prefetch=4,
            grid=(1,),
            in_specs=[whole(scores.shape), whole(queries.shape), anywhere, anywhere],
            out_specs=[whole((total, 128)), whole(half), whole(half), whole((half_rows, PROJ)), whole((half_rows, PROJ))],
            scratch_shapes=[
                pltpu.VMEM((2 * half_rows, PROJ), bf16),
                pltpu.VMEM((2 * half_rows, PROJ), f32),
                pltpu.VMEM((total + 8, 128), f32),
                pltpu.VMEM((total + 1, QLEN, PROJ), f32),
                pltpu.SemaphoreType.DMA((2,)),
            ],
        ),
        out_shape=[
            jax.ShapeDtypeStruct((total, 128), f32),
            jax.ShapeDtypeStruct(half, f32),
            jax.ShapeDtypeStruct(half, bf16),
            jax.ShapeDtypeStruct((half_rows, PROJ), f32),
            jax.ShapeDtypeStruct((half_rows, PROJ), bf16),
        ],
        compiler_params=params(62),
        cost_estimate=cost(1e10, 8 * MIB),
        name="score_back",
    )(ids, info, lengths, entries, scores, queries, near, far)


def head_kernel(
    grad_ref, proj_ref, wproj_ref, hat_ref, rstd_ref, gain_ref,
    dproj_ref, dresid_ref, dffn_ref, sums_ref,
):
    projected = proj_ref[...]
    grad = grad_ref[...]
    inverse = lax.rsqrt(jnp.sum(projected * projected, -1, keepdims=True) + vector_eps)
    inner = jnp.sum(projected * grad, -1, keepdims=True)
    dproj = (grad * inverse - projected * (inner * inverse * inverse * inverse)).astype(bf16)
    dproj_ref[...] = dproj
    dfinal = mm(dproj, wproj_ref[...], NT)
    hat = hat_ref[...]
    dresid = norm_back(dfinal, hat, rstd_ref[:, :1], line(gain_ref))
    dresid_ref[...] = dresid
    dffn = dresid.astype(bf16)
    dffn_ref[...] = dffn

    @pl.when(pl.program_id(0) == 0)
    def _():
        sums_ref[...] = jnp.zeros_like(sums_ref)

    sums_ref[0:1, :] += column_sum(dfinal * hat)
    sums_ref[1:2, :] += column_sum(dfinal)
    sums_ref[2:3, :] += column_sum(dffn.astype(f32))


def head_back(grad, projected, w_proj, hat, rstd, gain):
    rows, width = hat.shape
    block = lambda cols: pl.BlockSpec((PAIR, cols), lambda i: (i, 0))
    return pl.pallas_call(
        head_kernel,
        grid=(rows // PAIR,),
        in_specs=[block(PROJ), block(PROJ), once((width, PROJ)), block(width), block(128),
                  vector(width)],
        out_specs=[block(PROJ), block(width), block(width), whole((8, width))],
        out_shape=[
            jax.ShapeDtypeStruct((rows, PROJ), bf16),
            jax.ShapeDtypeStruct((rows, width), f32),
            jax.ShapeDtypeStruct((rows, width), bf16),
            jax.ShapeDtypeStruct((8, width), f32),
        ],
        compiler_params=params(62),
        cost_estimate=cost(2 * rows * width * PROJ, 12 * MIB),
        name="head_back",
    )(grad, projected, w_proj, hat, rstd, gain)


def active_back_kernel(dffn_ref, wdown_ref, der_ref, dup_ref, bup_ref):
    dactive = mm(dffn_ref[...], wdown_ref[...], NT)
    dup = (dactive * der_ref[...].astype(f32)).astype(bf16)
    dup_ref[...] = dup
    bup_ref[...] = column_sum(dup.astype(f32))


def active_back(dffn, w_down, der):
    rows, width = dffn.shape
    units = w_down.shape[0]
    step = 1024
    cols = pl.BlockSpec((rows, step), lambda i: (0, i))
    return pl.pallas_call(
        active_back_kernel,
        grid=(units // step,),
        in_specs=[once((rows, width)), pl.BlockSpec((step, width), lambda i: (i, 0)), cols],
        out_specs=[cols, pl.BlockSpec((1, step), lambda i: (0, i))],
        out_shape=[jax.ShapeDtypeStruct((rows, units), bf16), jax.ShapeDtypeStruct((1, units), f32)],
        compiler_params=params(62),
        cost_estimate=cost(2 * rows * width * units, 27 * MIB),
        name="active_back",
    )(dffn, w_down, der)


def feed_back_kernel(
    dup_ref, wup_ref, dresid2_hbm, hat_hbm, rstd_hbm, gain_ref, wo_hbm,
    dresid1_hbm, dbranch_hbm, datt_hbm, sums_ref,
    acc_ref, dresid_ref, hat_ref, rstd_ref, wo_ref, dbranch_ref, datt_ref, in_sem, out_sem,
):
    step = pl.program_id(0)
    loads = [
        pltpu.make_async_copy(hbm, ref, in_sem.at[i])
        for i, (hbm, ref) in enumerate(
            ((dresid2_hbm, dresid_ref), (hat_hbm, hat_ref), (rstd_hbm, rstd_ref), (wo_hbm, wo_ref))
        )
    ]

    @pl.when(step == 0)
    def _():
        for load in loads:
            load.start()

    part = mm(dup_ref[...], wup_ref[...], NT)

    @pl.when(step == 0)
    def _():
        acc_ref[...] = part

    @pl.when(step > 0)
    def _():
        acc_ref[...] += part

    @pl.when(step == pl.num_programs(0) - 1)
    def _():
        for load in loads:
            load.wait()
        sums = [0.0, 0.0, 0.0]
        copies = []
        for i, at in enumerate(range(0, acc_ref.shape[0], PAIR)):
            span = slice(at, at + PAIR)
            dnormed = acc_ref[span, :] + dresid_ref[span, :]
            hat = hat_ref[span, :]
            dresid = norm_back(dnormed, hat, rstd_ref[span, :1], line(gain_ref))
            dresid_ref[span, :] = dresid
            dbranch = dresid.astype(bf16)
            dbranch_ref[span, :] = dbranch
            datt_ref[span, :] = mm(dbranch, wo_ref[...], NT).astype(bf16)
            sums[0] += column_sum(dnormed * hat)
            sums[1] += column_sum(dnormed)
            sums[2] += column_sum(dbranch.astype(f32))
            outs = ((dresid_ref, dresid1_hbm), (dbranch_ref, dbranch_hbm), (datt_ref, datt_hbm))
            copies += stream_out(i, at, outs, out_sem)
        for i in range(3):
            sums_ref[i : i + 1, :] = sums[i]
        for copy in copies:
            copy.wait()


def feed_back(dup, w_up, dresid2, hat, rstd, w_out, gain):
    rows, width = hat.shape
    units = w_up.shape[1]
    step = 1024
    anywhere = pl.BlockSpec(memory_space=pl.ANY)
    return pl.pallas_call(
        feed_back_kernel,
        grid=(units // step,),
        in_specs=[
            pl.BlockSpec((rows, step), lambda i: (0, i)),
            pl.BlockSpec((width, step), lambda i: (0, i)),
            anywhere, anywhere, anywhere, vector(width), anywhere,
        ],
        out_specs=[anywhere, anywhere, anywhere, whole((8, width))],
        out_shape=[
            jax.ShapeDtypeStruct((rows, width), f32),
            jax.ShapeDtypeStruct((rows, width), bf16),
            jax.ShapeDtypeStruct((rows, width), bf16),
            jax.ShapeDtypeStruct((8, width), f32),
        ],
        scratch_shapes=[
            pltpu.VMEM((rows, width), f32),
            pltpu.VMEM((rows, width), f32),
            pltpu.VMEM((rows, width), f32),
            pltpu.VMEM((rows, 128), f32),
            pltpu.VMEM((width, width), bf16),
            pltpu.VMEM((rows, width), bf16),
            pltpu.VMEM((rows, width), bf16),
            pltpu.SemaphoreType.DMA((4,)),
            pltpu.SemaphoreType.DMA((3, rows // PAIR)),
        ],
        compiler_params=params(62),
        cost_estimate=cost(2 * rows * width * units, 36 * MIB),
        name="feed_back",
    )(dup, w_up, dresid2, hat, rstd, gain, w_out)


def attend_back_kernel(ids_ref, lengths_ref, qkv_ref, datt_ref, cos_ref, sin_ref, dmixed_ref, sums_ref, mask_ref):
    width = datt_ref.shape[1]
    block = pl.program_id(0)
    cosine = table_here(ids_ref, lengths_ref, cos_ref, block)
    sine = table_here(ids_ref, lengths_ref, sin_ref, block)
    mask_ref[...] = jnp.where(same_segment(ids_ref, lengths_ref, pl.program_id(0)), 0.0, masked_value)
    lane = lax.broadcasted_iota(jnp.int32, (PAIR, 2 * HD), 1)

    @pl.when(pl.program_id(0) == 0)
    def _():
        sums_ref[...] = jnp.zeros_like(sums_ref)

    mask = mask_ref[...]
    masks = (lane < HD, lane >= HD)
    group = 4
    for begin in range(0, width // (2 * HD), group):
        spots = [pair * 2 * HD for pair in range(begin, begin + group)]
        heads = [(at, m) for at in spots for m in masks]
        read = lambda ref, at: ref[:, at : at + 2 * HD]
        pick = lambda ref, at, m: jnp.where(m, read(ref, at), jnp.zeros((PAIR, 2 * HD), bf16))
        scores = [mm(read(qkv_ref, width + at), pick(qkv_ref, at, m), NT) + mask for at, m in heads]
        terms = [jnp.exp(x - jnp.max(x, 0, keepdims=True)) for x in scores]
        dweights = [mm(read(qkv_ref, 2 * width + at), pick(datt_ref, at, m), NT) for at, m in heads]
        weights = [x * (1.0 / jnp.sum(x, 0, keepdims=True)) for x in terms]
        dvalues = [mm(w.astype(bf16), pick(datt_ref, at, m)) for w, (at, m) in zip(weights, heads)]
        moved = [w * d for w, d in zip(weights, dweights)]
        dscores = [(m - w * jnp.sum(m, 0, keepdims=True)).astype(bf16) for w, m in zip(weights, moved)]
        dkeys = [mm(d, pick(qkv_ref, at, m)) for d, (at, m) in zip(dscores, heads)]
        dqueries = [mm(d, pick(qkv_ref, width + at, m), TN) for d, (at, m) in zip(dscores, heads)]
        for k, at in enumerate(spots):
            dquery, dkey, dvalue = (x[2 * k] + x[2 * k + 1] for x in (dqueries, dkeys, dvalues))
            dquery = dquery * score_scale
            dquery = dquery * cosine - partner(dquery) * sine
            dkey = dkey * cosine - partner(dkey) * sine
            for i, grad in enumerate((dquery, dkey, dvalue)):
                low = grad.astype(bf16)
                dmixed_ref[:, i * width + at : i * width + at + 2 * HD] = low
                sums_ref[:, i * width + at : i * width + at + 2 * HD] += column_sum(low.astype(f32))


def attend_back(ids, lengths, qkv, datt, tables):
    rows, width = datt.shape
    block = lambda cols: pl.BlockSpec((PAIR, cols), lambda i, *_: (i, 0))
    return pl.pallas_call(
        attend_back_kernel,
        grid_spec=pltpu.PrefetchScalarGridSpec(
            num_scalar_prefetch=2,
            grid=(rows // PAIR,),
            in_specs=[block(3 * width), block(width), once(tables[0].shape), once(tables[0].shape)],
            out_specs=[block(3 * width), whole((1, 3 * width))],
            scratch_shapes=[pltpu.VMEM((PAIR, PAIR), f32)],
        ),
        out_shape=[jax.ShapeDtypeStruct((rows, 3 * width), bf16), jax.ShapeDtypeStruct((1, 3 * width), f32)],
        compiler_params=params(62),
        cost_estimate=cost(2e10, 16 * MIB),
        name="attend_back",
    )(ids, lengths, qkv, datt, *tables)


def input_grad_kernel(dmixed_ref, w_ref, dresid_ref, out_ref):
    out_ref[...] = dresid_ref[...] + mm(dmixed_ref[...], w_ref[...], NT)


def input_grad(dmixed, w_qkv, dresid):
    rows, width = dresid.shape
    block = lambda cols: pl.BlockSpec((2 * PAIR, cols), lambda i: (i, 0))
    return pl.pallas_call(
        input_grad_kernel,
        grid=(rows // (2 * PAIR),),
        in_specs=[block(3 * width), once((width, 3 * width)), block(width)],
        out_specs=block(width),
        out_shape=jax.ShapeDtypeStruct((rows, width), f32),
        compiler_params=params(62),
        cost_estimate=cost(6 * rows * width * width, 20 * MIB),
        name="input_grad",
    )(dmixed, w_qkv, dresid)


def target_of(ids_ref, keep):
    return ids_ref[0] if keep else 1 - ids_ref[0]


def put(value, received, out_refs):
    if received is None:
        out_refs[0][...] = value.reshape(out_refs[0].shape).astype(bf16)
        return
    each, at = out_refs[0].shape[1], 0
    for out_ref in out_refs:
        count = out_ref.shape[0]
        part = value[at * each : (at + count) * each].reshape(out_ref.shape) + received[at : at + count].astype(f32)
        out_ref[...] = part.astype(out_ref.dtype)
        at += count


def outer_cols_kernel(counts, keep, slots, ids_ref, *refs):
    number = len(counts)
    received = refs[2 * number] if keep else None
    out_refs = refs[2 * number + 1 : -number] if keep else refs[2 * number : 2 * number + 1]
    turned_refs = refs[-number:]
    step = pl.program_id(0)
    each = turned_refs[0].shape[0] // slots
    target = target_of(ids_ref, keep)

    @pl.when(step == 0)
    def _():
        for left_ref, turned_ref in zip(refs[0 : 2 * number : 2], turned_refs):
            for at in range(0, left_ref.shape[1], 128):
                turned = left_ref[:, at : at + 128].T.astype(turned_ref.dtype)
                for k in range(128 // each):
                    rel = (at // each + k) ^ ids_ref[1]
                    slot = choose(target, lambda order: slot_of(rel, order), slots)
                    turned_ref[pl.ds(pl.multiple_of(slot * each, each), each), :] = turned[k * each : (k + 1) * each]

    done = 0
    for i, count in enumerate(counts):

        @pl.when((step >= done) & (step < done + count))
        def _(right_ref=refs[2 * i + 1], turned_ref=turned_refs[i]):
            put(mm(turned_ref[...].astype(bf16), right_ref[...]), received, out_refs)

        done += count


def outer_cols(ids, pairs, slots, received=None, parts=1, begin_at=0):
    rows = pairs[0][0].shape[1] // 2
    each = rows // slots
    keep = received is not None
    step = 1024
    specs, args, counts = [], [], []
    for left, right, begin, number in pairs:
        count = number // step
        first = sum(counts)
        specs.append(
            pl.BlockSpec((left.shape[0], rows), lambda i, ids: (0, target_of(ids, keep)), pipeline_mode=pl.Buffered(1))
        )
        specs.append(
            pl.BlockSpec(
                (right.shape[0], step),
                lambda i, *_, first=first, count=count, at=begin // step: (0, at + jnp.clip(i - first, 0, count - 1)),
            )
        )
        args += [left, right]
        counts.append(count)
    cols = sum(counts) * step
    spec = lambda count: pl.BlockSpec((count, each, step), lambda i, *_: (0, 0, i))
    shape = lambda count, kind: jax.ShapeDtypeStruct((count, each, cols), kind)
    if keep:
        specs.append(pl.BlockSpec((slots, each, step), lambda i, *_: (0, 0, begin_at // step + i)))
        args.append(received)
        outs = [spec(slots // 2)] + [spec(slots // 2 // parts)] * parts
        shapes = [shape(slots // 2, f32)] + [shape(slots // 2 // parts, bf16)] * parts
    else:
        outs, shapes = [spec(slots)], [shape(slots, bf16)]
    kind = bf16 if each % 16 == 0 else f32
    out = pl.pallas_call(
        functools.partial(outer_cols_kernel, counts, keep, slots),
        grid_spec=pltpu.PrefetchScalarGridSpec(
            num_scalar_prefetch=1, grid=(sum(counts),), in_specs=specs, out_specs=outs,
            scratch_shapes=[pltpu.VMEM((rows, left.shape[0]), kind) for left, *_ in pairs],
        ),
        out_shape=shapes,
        compiler_params=params(62),
        cost_estimate=cost(2 * args[0].shape[0] * rows * cols, (20 if keep else 15) * MIB),
        name="outer_cols",
    )(ids, *args)
    return out if keep else out[0]


def outer_rows_kernel(group, slots_apart, keep, ids_ref, *refs):
    left_refs, (right_ref, final_ref, dproj_ref) = refs[:group], refs[group : group + 3]
    received = refs[group + 3] if keep else None
    out_refs, proj_ref = refs[group + (4 if keep else 3) : -1], refs[-1]
    left = jnp.concatenate([ref[...].reshape(ref.shape[-2:]) for ref in left_refs], 1)
    value = mm(left, right_ref[...], TN)
    proj_ref[...] = mm(final_ref[...], dproj_ref[...], TN)
    tall, width = out_refs[0].shape[-2], value.shape[1]
    each = value.shape[0] // group
    short = proj_ref.shape[0] // group
    pieces = width // PROJ
    half = group // 2
    target = target_of(ids_ref, keep)
    for j in range(group):
        slot = j * slots_apart + pl.program_id(0)
        block = (choose(target, lambda order: rel_of(slot, order), group * slots_apart) ^ ids_ref[1]) & (group - 1)
        part = value[j * each : (j + 1) * each, :]
        small = proj_ref[pl.ds(pl.multiple_of(block * short, short), short), :]
        fold = short // pieces if short >= pieces else 1
        low = [small[i * fold : (i + 1) * fold, :] for i in range(short // fold)]
        if keep:
            part = part + received[j, 0, :each, :].astype(f32)
            low = [
                x + received[j, 0, each : each + fold, i * PROJ : (i + 1) * PROJ].astype(f32) for i, x in enumerate(low)
            ]
            out_ref, at = (out_refs[0], j) if j < half else (out_refs[1 + 2 * (j - half) // half], j % (half // 2))
        else:
            out_ref, at = out_refs[0], j
        kind = out_ref.dtype
        out_ref[at, 0, :each, :] = part.astype(kind)
        out_ref[at, 0, each:, :] = jnp.zeros((tall - each, width), kind)
        for i, x in enumerate(low):
            out_ref[at, 0, each : each + fold, i * PROJ : (i + 1) * PROJ] = x.astype(kind)


def outer_rows(ids, left, right, final, dproj, slots, group, received=None):
    tokens_here, rows = left.shape
    width = right.shape[1]
    rest = slots // group
    each = rows // (2 * slots)
    tall = each + 8
    keep = received is not None
    spec = lambda count: pl.BlockSpec((count, 1, tall, width), lambda i, *_: (0, i, 0, 0))
    shape = lambda count, kind: jax.ShapeDtypeStruct((count, rest, tall, width), kind)

    def owner(slot, ids):
        target = target_of(ids, keep)
        return target * slots + (choose(target, lambda order: rel_of(slot, order), slots) ^ ids[1])

    specs = [
        pl.BlockSpec((tokens_here, each), lambda i, ids, j=j: (0, owner(j * rest + i, ids))) for j in range(group)
    ]
    lefts = [left] * group
    if each < 128:
        specs = [
            pl.BlockSpec((1, tokens_here, each), lambda i, ids, j=j: (owner(j * rest + i, ids), 0, 0)) for j in range(group)
        ]
        lefts = [left.reshape(tokens_here, -1, each).transpose(1, 0, 2)] * group
    specs += [
        once((tokens_here, width)),
        pl.BlockSpec((tokens_here, final.shape[1] // (2 * rest)), lambda i, ids: (0, owner(i, ids) // group)),
        once((tokens_here, PROJ)),
    ]
    args = lefts + [right, final, dproj]
    if keep:
        specs.append(spec(group))
        args.append(received.reshape(group, rest, tall, width))
        outs = [spec(group // 2), spec(group // 4), spec(group // 4)]
        shapes = [shape(group // 2, f32), shape(group // 4, bf16), shape(group // 4, bf16)]
    else:
        outs, shapes = [spec(group)], [shape(group, bf16)]
    out = pl.pallas_call(
        functools.partial(outer_rows_kernel, group, rest, keep),
        grid_spec=pltpu.PrefetchScalarGridSpec(
            num_scalar_prefetch=1, grid=(rest,), in_specs=specs, out_specs=outs,
            scratch_shapes=[pltpu.VMEM((final.shape[1] // (2 * rest), PROJ), f32)],
        ),
        out_shape=shapes,
        compiler_params=params(62),
        cost_estimate=cost(tokens_here * rows * width, (20 if keep else 15) * MIB),
        name="outer_rows",
    )(ids, *args)
    out = [o.reshape(-1, tall, width) for o in out]
    return out if keep else out[0]


def flips(count):
    bits = [1 << i for i in range(count.bit_length() - 1)]
    third = {16: 1, 64: 2}[count]
    swapped = bits[third : 2 * third] + bits[:third] + bits[2 * third :][::-1]
    return bits, swapped


def slot_of(rel, order):
    return sum(
        ((rel >> (flip.bit_length() - 1)) & 1) << (len(order) - 1 - i) for i, flip in enumerate(order)
    )


def rel_of(slot, order):
    return sum(
        ((slot >> (len(order) - 1 - i)) & 1) << (flip.bit_length() - 1) for i, flip in enumerate(order)
    )


def choose(core, function, count):
    first, second = (function(order) for order in flips(count))
    return jnp.where(core == 0, first, second)


def hop(values, stage, count):
    pairs = []
    for stream, order in enumerate(flips(count)):
        pairs += [(stream * count + i, stream * count + (i ^ order[stage])) for i in range(count)]
    return lax.ppermute(values, ("stream", "dp"), pairs)


def swap(values):
    return lax.ppermute(values, "stream", [(0, 1), (1, 0)])


def after(value, *others):
    return lax.optimization_barrier((value, *others))[0]


def gather_both(first, first_stages, second, second_stages, count):
    pending = [(first, list(first_stages)), (second, list(second_stages))]
    while any(stages for _, stages in pending):
        got = [hop(values, stages[-1], count) if stages else None for values, stages in pending]
        values = lax.optimization_barrier([x for pair in zip(pending, got) for x in (pair[0][0], pair[1]) if x is not None])
        joined = []
        for (_, stages), arrived in zip(pending, got):
            value = values.pop(0)
            if arrived is not None:
                value = jnp.concatenate([value, values.pop(0)], 0)
            joined.append((value, stages[:-1]))
        held = lax.optimization_barrier([value for value, _ in joined])
        pending = [(value, stages) for value, (_, stages) in zip(held, joined)]
    return [value for value, _ in pending]


def take_in(keep, got):
    half = keep.shape[0] // 2
    if half == 0:
        return keep[0] + got[0].astype(f32), None
    return keep[:half] + got[:half].astype(f32), (keep[half:] + got[half:].astype(f32)).astype(bf16)


def scatter_sum(keep, send, stage, count, got=None):
    if got is not None:
        keep, send = take_in(keep, got)
    while send is not None:
        keep, send = take_in(keep, hop(send, stage, count))
        stage += 1
    return keep


def total_sum(values, stage, count):
    for later in range(stage, count.bit_length() - 1):
        values = values + hop(values, later, count)
    return values


def body(
    tokens, doc_lengths, cand_docs, group_sizes, w_qkv, b_qkv, w_attn_out, b_attn_out, gain_one, bias_one,
    w_up, b_up, w_down, b_down, gain_two, bias_two, w_proj,
):
    stream = lax.axis_index("stream")
    me = lax.axis_index("dp")
    count = lax.axis_size("dp")
    hidden = tokens[0]
    rows, width = hidden.shape
    half = rows // 2
    ids = jnp.stack([stream, me]).astype(jnp.int32)
    tables = [jnp.asarray(table) for table in rotation_tables()]
    group = {16: 4, 64: 16}[count]

    hold = lax.optimization_barrier
    levels = {16: 2, 64: 4}[count]
    last_stage = count.bit_length() - 1
    shape = (count, levels)
    info = jnp.concatenate([cand_docs.reshape(QH, CAND), group_sizes.reshape(QH, 1)], 1).astype(jnp.int32)
    hidden_, info = hold((hidden, info))
    info_got = hop(info, last_stage - 1, count)
    qkv, attended, hat1, rstd1, normed = attend(
        ids, doc_lengths, hidden_, w_qkv, b_qkv, tables, w_attn_out, b_attn_out, gain_one, bias_one
    )
    info, info_got, normed = hold((info, info_got, normed))
    info = jnp.concatenate([info, info_got], 0)
    info, normed = hold((info, normed))
    info_got = hop(info, last_stage - 2, count)
    active, der, hat2, rstd2, final, projected, vecs = feed(
        normed, w_up, b_up, w_down, b_down, hat1, gain_one, bias_one, gain_two, bias_two, w_proj
    )
    info, info_got, vecs = hold((info, info_got, vecs))
    info = jnp.concatenate([info, info_got], 0)

    on_docs = stream == 1
    other = swap(jnp.where(on_docs, vecs[:half], vecs[half:]))
    own_docs = jnp.where(on_docs, vecs[half:], other)
    queries = jnp.where(on_docs, other, vecs[:half])
    queries, near = gather_both(queries, range(levels, last_stage), own_docs, range(levels), count)
    queries = queries.reshape(-1, QLEN, PROJ)
    far = swap(near)
    scores, entries = score(ids, info, doc_lengths, queries, near, far, shape)
    scores = total_sum(scores, levels, count)
    loss, dq_keep, dq_send, keep, send = score_back(
        ids, info, doc_lengths, entries, scores, queries, near, far, shape
    )
    loss = lax.dynamic_slice_in_dim(loss, (me >> levels) * QH, QH, 0)
    by_row = (-1, half, PROJ)
    keep, q_keep = keep.reshape(by_row), dq_keep.reshape(by_row)
    got, q_got = swap(send).reshape(by_row), hop(dq_send.reshape(by_row), levels, count)
    keep, got, q_keep, q_got = hold((keep, got, q_keep, q_got))
    keep, send = take_in(keep, got)
    q_keep, q_send = take_in(q_keep, q_got)
    keep, send, q_keep, q_send = hold((keep, send, q_keep, q_send))
    got, q_got = hop(send, 0, count), hop(q_send, levels + 1, count)
    keep, got, q_keep, q_got = hold((keep, got, q_keep, q_got))
    keep, send = take_in(keep, got)
    dqueries = scatter_sum(q_keep, None, last_stage, count, q_got)
    ddocs = scatter_sum(keep, send, 1, count)
    back = swap(jnp.where(on_docs, dqueries, ddocs))
    grad_vectors = jnp.where(
        on_docs, jnp.concatenate([back, ddocs], 0), jnp.concatenate([dqueries, back], 0)
    )

    def add_first(keep, got):
        half = keep.shape[0] // 2
        return (keep[half:] + got.astype(f32)).astype(bf16)

    def add_second(keep, got):
        half = keep.shape[0] // 2
        return keep[:half] + got.astype(f32)

    dproj, dresid2, dffn, sums2 = head_back(grad_vectors, projected, w_proj, hat2, rstd2, gain_two)
    down = lambda left, received=None: outer_rows(
        ids, left, dffn, final, dproj, count, group, received
    )
    units = w_up.shape[1]
    up = lambda left, received=None: outer_cols(ids, [(left, dup, 0, units)], count, received)
    mix_out = lambda left: outer_cols(ids, [(left, dmixed, 0, 3 * width), (attended, dbranch, 0, width)], count)
    mix_a = lambda left, received: outer_cols(ids, [(left, dmixed, 0, 2 * width)], count, received)
    mix_b = lambda left, received: outer_cols(
        ids, [(left, dmixed, 2 * width, width), (attended, dbranch, 0, width)], count, received, 1, 2 * width
    )

    d_out = down(active)
    d_got = swap(d_out)
    dffn_, d_out = hold((dffn, d_out))
    dup, sum_up = active_back(dffn_, w_down, der)
    active_, d_got, dup = hold((active, d_got, dup))
    d_keep, d_low, d_high = down(active_, d_got)
    d_high, d_low, normed_, d_keep = hold((d_high, d_low, normed, d_keep))
    u_out = up(normed_)
    d_high, d_low, u_out, dup_ = hold((d_high, d_low, u_out, dup))
    d_high_got, d_low_got, u_got = hop(d_high, 0, count), hop(d_low, 0, count), swap(u_out)
    dresid1, dbranch, dattended, sums1 = feed_back(dup_, w_up, dresid2, hat1, rstd1, w_attn_out, gain_one)
    d_keep, d_high_got, d_low_got, dbranch = hold((d_keep, d_high_got, d_low_got, dbranch))
    d_send = add_first(d_keep, d_high_got)
    d_keep = add_second(d_keep, d_low_got)
    d_keep, d_send, normed_, u_got = hold((d_keep, d_send, normed, u_got))
    d_got = hop(d_send, 1, count)
    u_keep, u_send = up(normed_, u_got)
    d_keep, d_got, u_keep = hold((d_keep, d_got, u_keep))
    d_keep, d_send = take_in(d_keep, d_got)
    u_send, d_keep, d_send, dattended = hold((u_send, d_keep, d_send, dattended))
    u_got, d_got = hop(u_send, 0, count), hop(d_send, 2, count)
    dmixed, sum_qkv = attend_back(ids, doc_lengths, qkv, dattended, tables)
    d_keep, d_got, u_keep, u_got, dmixed = hold((d_keep, d_got, u_keep, u_got, dmixed))
    u_keep, u_send = take_in(u_keep, u_got)
    d_keep, d_send = take_in(d_keep, d_got)
    sums = [sum_qkv[0], sums1[2], sums1[0], sums1[1], sum_up[0], sums2[2], sums2[0], sums2[1]]
    late = jnp.concatenate([v.reshape(2 * count, -1) for v in sums], 1)
    u_send, u_keep, hidden_, late, d_keep, d_send = hold((u_send, u_keep, hidden, late, d_keep, d_send))
    u_got, l_got, d_got = hop(u_send, 1, count), swap(late), hop(d_send, 3, count)
    m_out = mix_out(hidden_)
    m_out, late, l_got, u_keep, u_got, d_keep, d_got = hold((m_out, late, l_got, u_keep, u_got, d_keep, d_got))
    g_down = scatter_sum(d_keep, d_send, 4, count, d_got)
    u_keep, u_send = take_in(u_keep, u_got)
    late = late + l_got
    m_out, hidden_, late, g_down, u_send, u_keep = hold((m_out, hidden_, late, g_down, u_send, u_keep))
    m_got, l_got, u_got = swap(m_out), hop(late, 0, count), hop(u_send, 2, count)
    a_keep, a_send = mix_a(hidden_, m_got)
    u_keep, u_got, a_send, late, l_got = hold((u_keep, u_got, a_send, late, l_got))
    u_keep, u_send = take_in(u_keep, u_got)
    late = late + l_got
    u_keep, u_send, a_send, hidden_, late = hold((u_keep, u_send, a_send, hidden_, late))
    a_got, u_got, l_got = hop(a_send, 0, count), hop(u_send, 3, count), hop(late, 1, count)
    b_keep, b_send = mix_b(hidden_, m_got)
    u_keep, u_got, b_keep, late, l_got = hold((u_keep, u_got, b_keep, late, l_got))
    g_up = scatter_sum(u_keep, u_send, 4, count, u_got)
    late = late + l_got
    a_keep, a_got, g_up, b_send, late = hold((a_keep, a_got, g_up, b_send, late))
    a_keep, a_send = take_in(a_keep, a_got)
    a_keep, a_send, b_send, dmixed_, late = hold((a_keep, a_send, b_send, dmixed, late))
    a_got, b_got = hop(a_send, 1, count), hop(b_send, 0, count)
    l_got = hop(late, 2, count)
    grad_hidden = input_grad(dmixed_, w_qkv, dresid1)
    a_keep, a_got, grad_hidden, b_got = hold((a_keep, a_got, grad_hidden, b_got))
    b_keep, b_send = take_in(b_keep, b_got)
    b_got = hop(b_send, 1, count)
    a_keep, a_send = take_in(a_keep, a_got)
    g_a = scatter_sum(a_keep, a_send, 2, count)
    b_keep, b_send = take_in(b_keep, b_got)
    g_b = scatter_sum(b_keep, b_send, 2, count)

    late = total_sum(late + l_got, 3, count)
    mine = lax.dynamic_slice_in_dim(late, stream * count + me, 1, 0)[0]
    sizes = [v.shape[0] // (2 * count) for v in sums]
    parts = [mine[end - size : end] for end, size in zip(np.cumsum(sizes), sizes)]
    g_bqkv, g_bout, g_gain1, g_bias1, g_bup, g_bdown, g_gain2, g_bias2 = parts
    tall = w_down.shape[0] // (2 * count)
    short = width // (2 * count)
    pieces = width // PROJ
    fold = max(short // pieces, 1)
    g_proj = g_down[tall : tall + fold].reshape(fold, pieces, PROJ).transpose(1, 0, 2)[: short // fold].reshape(short, PROJ)
    return (
        loss[:, 0][None, None, :],
        grad_hidden[None],
        jnp.concatenate([g_a, g_b[:, :width]], 1),
        g_bqkv,
        g_b[:, width:],
        g_bout,
        g_gain1,
        g_bias1,
        g_up,
        g_bup,
        g_down[:tall],
        g_bdown,
        g_gain2,
        g_bias2,
        g_proj,
    )


def solution(mesh):
    every = P(("stream", "dp"))
    rows = P(("stream", "dp"), None)
    return jax.shard_map(
        body,
        mesh=mesh,
        in_specs=(P("stream", "dp", None), P(), P("dp", "stream", None, None), P("dp", "stream", None)) + (P(),) * 13,
        out_specs=(
            P("dp", "stream", None), P("stream", "dp", None), rows, every, rows, every, every, every, rows, every,
            rows, every, every, every, rows,
        ),
        check_vma=False,
    )
```

```python
import functools
import math

import jax
import jax.numpy as jnp
import numpy as np
from jax import lax
from jax.experimental import pallas as pl
from jax.experimental.pallas import tpu as pltpu
from jax.sharding import PartitionSpec as P

HD = 64
PROJ = 128
QLEN = 32
CAND = 8
QH = 16
PAIR = 256

score_scale = 0.125
sim_temp = 0.05
loss_temp = 0.08
masked_value = -1e30
norm_eps = 1e-05
vector_eps = 1e-06

f32 = jnp.float32
bf16 = jnp.bfloat16
MIB = 1 << 20

NN = (((1,), (0,)), ((), ()))
NT = (((1,), (1,)), ((), ()))
TN = (((0,), (0,)), ((), ()))


def mm(left, right, dims=NN):
    return lax.dot_general(left, right, dims, preferred_element_type=f32)


def params(mib):
    return pltpu.CompilerParams(vmem_limit_bytes=mib * MIB)


def cost(flops, moved):
    return pl.CostEstimate(flops=int(flops), bytes_accessed=int(moved), transcendentals=0)


def whole(shape):
    return pl.BlockSpec(shape, lambda *_: (0,) * len(shape))


def vector(length):
    return pl.BlockSpec((length,), lambda *_: (0,), pipeline_mode=pl.Buffered(1))


def line(ref):
    return ref[...].astype(f32)[None, :]


def once(shape):
    return pl.BlockSpec(shape, lambda *_: (0,) * len(shape), pipeline_mode=pl.Buffered(1))


def rotation_tables():
    freq = np.exp(np.arange(HD // 2) * (-2.0 * math.log(10000.0) / HD))
    lane = np.arange(2 * HD)
    place = np.concatenate([np.arange(PAIR) % QLEN, np.arange(PAIR), np.arange(PAIR)])
    angle = place[:, None] * freq[lane % (HD // 2)][None, :]
    sign = np.where(lane % HD < HD // 2, -1.0, 1.0)[None, :]
    return np.cos(angle).astype(np.float32), (np.sin(angle) * sign).astype(np.float32)


def first_length(ids_ref, lengths_ref, block):
    return lengths_ref[ids_ref[1], 2 * block]


def table_here(ids_ref, lengths_ref, table_ref, block):
    first = first_length(ids_ref, lengths_ref, block)
    row = lax.broadcasted_iota(jnp.int32, (PAIR, 2 * HD), 0)
    moved = table_ref[pl.ds(2 * PAIR - first, PAIR), :]
    doc = jnp.where(row < first, table_ref[PAIR : 2 * PAIR, :], moved)
    return jnp.where(ids_ref[0] == 1, doc, table_ref[:PAIR, :])


def partner(values):
    lane = lax.broadcasted_iota(jnp.int32, values.shape, 1)
    ahead = pltpu.roll(values, 2 * HD - HD // 2, 1)
    behind = pltpu.roll(values, HD // 2, 1)
    return jnp.where(lane % HD < HD // 2, ahead, behind)


def same_segment(ids_ref, lengths_ref, block):
    is_doc = ids_ref[0] == 1
    first = first_length(ids_ref, lengths_ref, block)
    row = lax.broadcasted_iota(jnp.int32, (PAIR, PAIR), 0)
    col = lax.broadcasted_iota(jnp.int32, (PAIR, PAIR), 1)
    doc = ((row >= first) ^ (col >= first)).astype(jnp.int32)
    query = ((row // QLEN) ^ (col // QLEN)).astype(jnp.int32)
    return jnp.where(is_doc, doc, query) == 0


def normalise(values):
    mean = jnp.mean(values, -1, keepdims=True)
    center = values - mean
    rstd = lax.rsqrt(jnp.mean(center * center, -1, keepdims=True) + norm_eps)
    return center * rstd, rstd


def norm_back(grad, hat, rstd, gain):
    scaled = grad * gain
    return (
        scaled - jnp.mean(scaled, -1, keepdims=True) - hat * jnp.mean(scaled * hat, -1, keepdims=True)
    ) * rstd


def column_sum(values):
    return jnp.sum(values, 0, keepdims=True)


def attend_kernel(
    ids_ref, lengths_ref, x_ref, wqkv_ref, bqkv_ref, cos_ref, sin_ref, wo_ref, bo_ref, g_ref, c_ref,
    qkv_ref, att_ref, hat_ref, rstd_ref, normb_ref, mask_ref,
):
    width = x_ref.shape[1]
    x = x_ref[...]
    block = pl.program_id(0)
    cosine = table_here(ids_ref, lengths_ref, cos_ref, block)
    sine = table_here(ids_ref, lengths_ref, sin_ref, block)
    step = 512
    for start in range(0, 3 * width, step):
        mixed = mm(x, wqkv_ref[:, start : start + step]) + bqkv_ref[start : start + step].astype(f32)[None, :]
        if start < 2 * width:
            parts = []
            for off in range(0, step, 2 * HD):
                one = mixed[:, off : off + 2 * HD]
                one = one * cosine + partner(one) * sine
                parts.append(one.astype(bf16))
            mixed = jnp.concatenate(parts, 1)
            if start < width:
                mixed = mixed * jnp.asarray(score_scale, bf16)
        qkv_ref[:, start : start + step] = mixed.astype(bf16)
    mask_ref[...] = jnp.where(same_segment(ids_ref, lengths_ref, pl.program_id(0)), 0.0, masked_value)
    lane = lax.broadcasted_iota(jnp.int32, (PAIR, 2 * HD), 1)
    mask = mask_ref[...]
    group = 4
    for begin in range(0, width // (2 * HD), group):
        heads = [(pair * 2 * HD, head) for pair in range(begin, begin + group) for head in range(2)]
        mine = lambda head: (lane < HD) if head == 0 else (lane >= HD)
        pick = lambda at, head: jnp.where(mine(head), qkv_ref[:, at : at + 2 * HD], jnp.zeros((PAIR, 2 * HD), bf16))
        scores = [mm(qkv_ref[:, at : at + 2 * HD], pick(width + at, head), NT) + mask for at, head in heads]
        terms = [jnp.exp(s - jnp.max(s, -1, keepdims=True)) for s in scores]
        weights = [(t * (1.0 / jnp.sum(t, -1, keepdims=True))).astype(bf16) for t in terms]
        parts = [mm(w, pick(2 * width + at, head)) for w, (at, head) in zip(weights, heads)]
        for k in range(group):
            at = heads[2 * k][0]
            att_ref[:, at : at + 2 * HD] = (parts[2 * k] + parts[2 * k + 1]).astype(bf16)
    branch = mm(att_ref[...], wo_ref[...]) + line(bo_ref)
    hat, rstd = normalise(x.astype(f32) + branch)
    hat_ref[...] = hat
    rstd_ref[...] = jnp.broadcast_to(rstd, rstd_ref.shape)
    normb_ref[...] = (hat * line(g_ref) + line(c_ref)).astype(bf16)


def attend(ids, lengths, x, w_qkv, b_qkv, tables, w_out, b_out, gain, bias):
    rows, width = x.shape
    block = lambda cols: pl.BlockSpec((PAIR, cols), lambda i, *_: (i, 0))
    return pl.pallas_call(
        attend_kernel,
        grid_spec=pltpu.PrefetchScalarGridSpec(
            num_scalar_prefetch=2,
            grid=(rows // PAIR,),
            in_specs=[
                block(width), once((width, 3 * width)), vector(3 * width), once(tables[0].shape),
                once(tables[0].shape), once((width, width)), vector(width), vector(width), vector(width),
            ],
            out_specs=[block(3 * width), block(width), block(width), block(128), block(width)],
            scratch_shapes=[pltpu.VMEM((PAIR, PAIR), f32)],
        ),
        out_shape=[
            jax.ShapeDtypeStruct((rows, 3 * width), bf16),
            jax.ShapeDtypeStruct((rows, width), bf16),
            jax.ShapeDtypeStruct((rows, width), f32),
            jax.ShapeDtypeStruct((rows, 128), f32),
            jax.ShapeDtypeStruct((rows, width), bf16),
        ],
        compiler_params=params(62),
        cost_estimate=cost(2 * rows * width * 4 * width, 30 * MIB),
        name="attend",
    )(ids, lengths, x, w_qkv, b_qkv, *tables, w_out, b_out, gain, bias)


def stream_out(i, at, pairs, sem):
    copies = [
        pltpu.make_async_copy(ref.at[pl.ds(at, PAIR)], hbm.at[pl.ds(at, PAIR)], sem.at[j, i])
        for j, (ref, hbm) in enumerate(pairs)
    ]
    for copy in copies:
        copy.start()
    return copies


def feed_kernel(
    x_ref, wup_ref, bup_ref, wdown_ref, bdown_ref, hat1_ref, g1_ref, c1_ref, g2_ref, c2_ref, wproj_ref,
    act_ref, der_ref, hat2_hbm, rstd2_ref, final_hbm, proj_ref, vec_ref,
    acc_ref, hat_ref, final_ref, in_sem, out_sem,
):
    step = pl.program_id(0)
    load = pltpu.make_async_copy(hat1_ref, hat_ref, in_sem)

    @pl.when(step == 0)
    def _():
        load.start()

    upward = mm(x_ref[...], wup_ref[...]) + line(bup_ref)
    below = 0.5 + 0.5 * lax.erf(upward * (2.0**-0.5))
    density = jnp.exp(-0.5 * upward * upward) * ((2.0 * math.pi) ** -0.5)
    active = (upward * below).astype(bf16)
    act_ref[...] = active
    der_ref[...] = (below + upward * density).astype(bf16)
    part = mm(active, wdown_ref[...])

    @pl.when(step == 0)
    def _():
        acc_ref[...] = part

    @pl.when(step > 0)
    def _():
        acc_ref[...] += part

    @pl.when(step == pl.num_programs(0) - 1)
    def _():
        load.wait()
        copies = []
        for i, at in enumerate(range(0, acc_ref.shape[0], PAIR)):
            span = slice(at, at + PAIR)
            normed = hat_ref[span, :] * line(g1_ref) + line(c1_ref)
            hat, rstd = normalise(normed + acc_ref[span, :] + line(bdown_ref))
            hat_ref[span, :] = hat
            rstd2_ref[span, :] = jnp.broadcast_to(rstd, (PAIR, 128))
            final = (hat * line(g2_ref) + line(c2_ref)).astype(bf16)
            final_ref[span, :] = final
            copies += stream_out(i, at, ((hat_ref, hat2_hbm), (final_ref, final_hbm)), out_sem)
            projected = mm(final, wproj_ref[...])
            proj_ref[span, :] = projected
            inverse = lax.rsqrt(jnp.sum(projected * projected, -1, keepdims=True) + vector_eps)
            vec_ref[span, :] = (projected * inverse).astype(bf16)
        for copy in copies:
            copy.wait()


def feed(x, w_up, b_up, w_down, b_down, hat1, g1, c1, g2, c2, w_proj):
    rows, width = x.shape
    units = w_up.shape[1]
    step = 1024
    cols = pl.BlockSpec((rows, step), lambda i: (0, i))
    anywhere = pl.BlockSpec(memory_space=pl.ANY)
    return pl.pallas_call(
        feed_kernel,
        grid=(units // step,),
        in_specs=[
            once((rows, width)),
            pl.BlockSpec((width, step), lambda i: (0, i)),
            pl.BlockSpec((step,), lambda i: (i,)),
            pl.BlockSpec((step, width), lambda i: (i, 0)),
            vector(width), anywhere, vector(width), vector(width), vector(width), vector(width),
            once((width, PROJ)),
        ],
        out_specs=[cols, cols, anywhere, whole((rows, 128)), anywhere, whole((rows, PROJ)), whole((rows, PROJ))],
        out_shape=[
            jax.ShapeDtypeStruct((rows, units), bf16),
            jax.ShapeDtypeStruct((rows, units), bf16),
            jax.ShapeDtypeStruct((rows, width), f32),
            jax.ShapeDtypeStruct((rows, 128), f32),
            jax.ShapeDtypeStruct((rows, width), bf16),
            jax.ShapeDtypeStruct((rows, PROJ), f32),
            jax.ShapeDtypeStruct((rows, PROJ), bf16),
        ],
        scratch_shapes=[
            pltpu.VMEM((rows, width), f32),
            pltpu.VMEM((rows, width), f32),
            pltpu.VMEM((rows, width), bf16),
            pltpu.SemaphoreType.DMA,
            pltpu.SemaphoreType.DMA((2, rows // PAIR)),
        ],
        compiler_params=params(62),
        cost_estimate=cost(4 * rows * width * units, 50 * MIB),
        name="feed",
    )(x, w_up, b_up, w_down, b_down, hat1, g1, c1, g2, c2, w_proj)


UNROLL = 8


def load_docs(near_ref, far_ref, docs_ref, sem):
    half_rows = near_ref.shape[0]
    copies = [
        pltpu.make_async_copy(near_ref, docs_ref.at[pl.ds(0, half_rows)], sem.at[0]),
        pltpu.make_async_copy(far_ref, docs_ref.at[pl.ds(half_rows, half_rows)], sem.at[1]),
    ]
    for copy in copies:
        copy.start()
    return copies


def pair_scores(ids_ref, info_ref, length_ref, q_ref, docs_ref, entry, shape):
    count, levels = shape
    lane = lax.broadcasted_iota(jnp.int32, (QLEN, PAIR), 1)
    index = jnp.minimum(entry >> 3, q_ref.shape[0] - 1)
    doc = info_ref[index, entry & 7]
    row = doc >> 3
    pair = (doc >> 1) & 3
    first = length_ref[row, 2 * pair]
    odd = (doc & 1) == 1
    low = jnp.where(odd, first, 0)
    high = jnp.where(odd, PAIR, first)
    core = pair >> 1
    plane = 1 << levels
    rel = (row ^ ids_ref[1]) & (plane - 1)
    slot = choose(core, lambda order: slot_of(rel, order[:levels]), count)
    start = pl.multiple_of((((core ^ ids_ref[0]) * plane + slot) * 2 + (pair & 1)) * PAIR, PAIR)
    scaled = mm(q_ref[index], docs_ref[pl.ds(start, PAIR), :], NT) * (1.0 / sim_temp)
    return start, jnp.where((lane >= low) & (lane < high), scaled, masked_value)


def natural_row(ids_ref, entry, shape):
    count, levels = shape
    slot = entry >> (3 + QH.bit_length() - 1)
    rel = choose(ids_ref[0], lambda order: rel_of(slot, order[levels:]), count)
    z = (ids_ref[1] ^ rel) >> levels
    return z * QH + ((entry >> 3) & (QH - 1))


def score_kernel(
    shape, ids_ref, info_ref, length_ref, q_ref, near_ref, far_ref, score_ref, list_ref, docs_ref, sem,
):
    copies = load_docs(near_ref, far_ref, docs_ref, sem)
    count, levels = shape
    queries = q_ref.shape[0]
    score_ref[...] = jnp.zeros_like(score_ref)
    lane = lax.broadcasted_iota(jnp.int32, (1, 128), 1)
    z = ids_ref[1] >> levels

    def scan(q, found):
        size = info_ref[q, CAND]
        for c in range(CAND):
            here = ((info_ref[q, c] >> (3 + levels)) == z) & (c < size)
            list_ref[1 + found] = q * CAND + c
            found = found + here.astype(jnp.int32)
        return found

    found = lax.fori_loop(0, queries, scan, 0)
    list_ref[0] = found
    for u in range(UNROLL):
        list_ref[1 + found + u] = queries * CAND
    for j in range(QH):
        row = z * QH + j
        score_ref[pl.ds(row, 1), :] = jnp.where(lane == CAND, info_ref[j, CAND].astype(f32), 0.0)
    for copy in copies:
        copy.wait()

    @pl.loop(0, (found + UNROLL - 1) // UNROLL)
    def _(i):
        entries = [list_ref[1 + i * UNROLL + u] for u in range(UNROLL)]
        scaled = [pair_scores(ids_ref, info_ref, length_ref, q_ref, docs_ref, entry, shape)[1] for entry in entries]
        highest = [jnp.max(x, -1, keepdims=True) for x in scaled]
        totals = [jnp.sum(jnp.exp(x - m), -1, keepdims=True) for x, m in zip(scaled, highest)]
        results = [
            jnp.sum(sim_temp * (m + jnp.log(total)), 0, keepdims=True) for m, total in zip(highest, totals)
        ]
        for entry, result in zip(entries, results):
            row = jnp.where(entry >= queries * CAND, queries, natural_row(ids_ref, entry, shape))
            score_ref[pl.ds(row, 1), :] = jnp.where(lane == (entry & 7), result, score_ref[pl.ds(row, 1), :])


def score(ids, info, lengths, queries, near, far, shape):
    total = queries.shape[0]
    anywhere = pl.BlockSpec(memory_space=pl.ANY)
    return pl.pallas_call(
        functools.partial(score_kernel, shape),
        grid_spec=pltpu.PrefetchScalarGridSpec(
            num_scalar_prefetch=3,
            grid=(1,),
            in_specs=[whole(queries.shape), anywhere, anywhere],
            out_specs=[whole((total + 8, 128)), pl.BlockSpec(memory_space=pltpu.SMEM)],
            scratch_shapes=[pltpu.VMEM((2 * near.shape[0], PROJ), bf16), pltpu.SemaphoreType.DMA((2,))],
        ),
        out_shape=[
            jax.ShapeDtypeStruct((total + 8, 128), f32),
            jax.ShapeDtypeStruct((total * CAND + 2 * UNROLL,), jnp.int32),
        ],
        compiler_params=params(62),
        cost_estimate=cost(1e10, 4 * MIB),
        name="score",
    )(ids, info, lengths, queries, near, far)


def score_back_kernel(
    shape, ids_ref, info_ref, length_ref, list_ref, score_ref, q_ref, near_ref, far_ref,
    loss_ref, dq_keep_ref, dq_send_ref, keep_ref, send_ref, docs_ref, acc_ref, pull_ref, dq_ref, sem,
):
    copies = load_docs(near_ref, far_ref, docs_ref, sem)
    count, levels = shape
    queries = q_ref.shape[0]
    half_rows = near_ref.shape[0]
    scores = score_ref[:queries, :]
    lane = lax.broadcasted_iota(jnp.int32, (queries, 128), 1)
    size = jnp.sum(jnp.where(lane == CAND, scores, 0.0), -1, keepdims=True)
    counted = lane.astype(f32) < jnp.where(lane < CAND, size, 0.0)
    logits = jnp.where(counted, scores * (1.0 / loss_temp), masked_value)
    top = jnp.max(logits, -1, keepdims=True)
    norm = top + jnp.log(jnp.sum(jnp.exp(logits - top), -1, keepdims=True))
    positive = (lane == 0).astype(f32)
    pull_ref[:queries, :] = (jnp.exp(logits - norm) - positive) * (1.0 / loss_temp)
    pull_ref[queries:, :] = jnp.zeros((8, 128), f32)
    loss = norm - jnp.sum(logits * positive, -1, keepdims=True)
    loss_ref[...] = jnp.broadcast_to(loss, loss_ref.shape)
    dq_ref[...] = jnp.zeros_like(dq_ref)
    chunk = 512

    @pl.loop(0, 2 * half_rows // chunk)
    def _(i):
        acc_ref[pl.ds(pl.multiple_of(i * chunk, chunk), chunk), :] = jnp.zeros((chunk, PROJ), f32)

    for copy in copies:
        copy.wait()
    one = lax.broadcasted_iota(jnp.int32, (1, 128), 1)

    @pl.loop(0, (list_ref[0] + UNROLL - 1) // UNROLL)
    def _(i):
        entries = [list_ref[1 + i * UNROLL + u] for u in range(UNROLL)]
        found = [pair_scores(ids_ref, info_ref, length_ref, q_ref, docs_ref, entry, shape) for entry in entries]
        terms = [jnp.exp(scaled - jnp.max(scaled, -1, keepdims=True)) for _, scaled in found]
        totals = [jnp.sum(x, -1, keepdims=True) for x in terms]
        pulls = []
        for entry in entries:
            row = jnp.where(entry >= queries * CAND, queries, natural_row(ids_ref, entry, shape))
            pulls.append(
                jnp.sum(jnp.where(one == (entry & 7), pull_ref[pl.ds(row, 1), :], 0.0), -1, keepdims=True)
            )
        dsims = [(pull * (x * (1.0 / total))).astype(bf16) for pull, x, total in zip(pulls, terms, totals)]
        for entry, (start, _), dsim in zip(entries, found, dsims):
            index = entry >> 3
            acc_ref[pl.ds(start, PAIR), :] += mm(dsim, q_ref[jnp.minimum(index, queries - 1)], TN)
            dq_ref[index] += mm(dsim, docs_ref[pl.ds(start, PAIR), :])

    near_q = dq_keep_ref.shape[0]
    dq_keep_ref[...] = dq_ref[:near_q]
    dq_send_ref[...] = dq_ref[near_q:queries].astype(bf16)

    @pl.loop(0, half_rows // chunk)
    def _(i):
        at = pl.multiple_of(i * chunk, chunk)
        keep_ref[pl.ds(at, chunk), :] = acc_ref[pl.ds(at, chunk), :]
        send_ref[pl.ds(at, chunk), :] = acc_ref[pl.ds(half_rows + at, chunk), :].astype(bf16)


def score_back(ids, info, lengths, entries, scores, queries, near, far, shape):
    total = queries.shape[0]
    half_rows = near.shape[0]
    anywhere = pl.BlockSpec(memory_space=pl.ANY)
    half = (total // 2, QLEN, PROJ)
    return pl.pallas_call(
        functools.partial(score_back_kernel, shape),
        grid_spec=pltpu.PrefetchScalarGridSpec(
            num_scalar_prefetch=4,
            grid=(1,),
            in_specs=[whole(scores.shape), whole(queries.shape), anywhere, anywhere],
            out_specs=[whole((total, 128)), whole(half), whole(half), whole((half_rows, PROJ)), whole((half_rows, PROJ))],
            scratch_shapes=[
                pltpu.VMEM((2 * half_rows, PROJ), bf16),
                pltpu.VMEM((2 * half_rows, PROJ), f32),
                pltpu.VMEM((total + 8, 128), f32),
                pltpu.VMEM((total + 1, QLEN, PROJ), f32),
                pltpu.SemaphoreType.DMA((2,)),
            ],
        ),
        out_shape=[
            jax.ShapeDtypeStruct((total, 128), f32),
            jax.ShapeDtypeStruct(half, f32),
            jax.ShapeDtypeStruct(half, bf16),
            jax.ShapeDtypeStruct((half_rows, PROJ), f32),
            jax.ShapeDtypeStruct((half_rows, PROJ), bf16),
        ],
        compiler_params=params(62),
        cost_estimate=cost(1e10, 8 * MIB),
        name="score_back",
    )(ids, info, lengths, entries, scores, queries, near, far)


def head_kernel(
    grad_ref, proj_ref, wproj_ref, hat_ref, rstd_ref, gain_ref,
    dproj_ref, dresid_ref, dffn_ref, sums_ref,
):
    projected = proj_ref[...]
    grad = grad_ref[...]
    inverse = lax.rsqrt(jnp.sum(projected * projected, -1, keepdims=True) + vector_eps)
    inner = jnp.sum(projected * grad, -1, keepdims=True)
    dproj = (grad * inverse - projected * (inner * inverse * inverse * inverse)).astype(bf16)
    dproj_ref[...] = dproj
    dfinal = mm(dproj, wproj_ref[...], NT)
    hat = hat_ref[...]
    dresid = norm_back(dfinal, hat, rstd_ref[:, :1], line(gain_ref))
    dresid_ref[...] = dresid
    dffn = dresid.astype(bf16)
    dffn_ref[...] = dffn

    @pl.when(pl.program_id(0) == 0)
    def _():
        sums_ref[...] = jnp.zeros_like(sums_ref)

    sums_ref[0:1, :] += column_sum(dfinal * hat)
    sums_ref[1:2, :] += column_sum(dfinal)
    sums_ref[2:3, :] += column_sum(dffn.astype(f32))


def head_back(grad, projected, w_proj, hat, rstd, gain):
    rows, width = hat.shape
    block = lambda cols: pl.BlockSpec((2 * PAIR, cols), lambda i: (i, 0))
    return pl.pallas_call(
        head_kernel,
        grid=(rows // (2 * PAIR),),
        in_specs=[block(PROJ), block(PROJ), once((width, PROJ)), block(width), block(128),
                  vector(width)],
        out_specs=[block(PROJ), block(width), block(width), whole((8, width))],
        out_shape=[
            jax.ShapeDtypeStruct((rows, PROJ), bf16),
            jax.ShapeDtypeStruct((rows, width), f32),
            jax.ShapeDtypeStruct((rows, width), bf16),
            jax.ShapeDtypeStruct((8, width), f32),
        ],
        compiler_params=params(62),
        cost_estimate=cost(2 * rows * width * PROJ, 12 * MIB),
        name="head_back",
    )(grad, projected, w_proj, hat, rstd, gain)


def active_back_kernel(dffn_ref, wdown_ref, der_ref, dup_ref, bup_ref):
    dactive = mm(dffn_ref[...], wdown_ref[...], NT)
    dup = (dactive * der_ref[...].astype(f32)).astype(bf16)
    dup_ref[...] = dup
    bup_ref[...] = column_sum(dup.astype(f32))


def active_back(dffn, w_down, der):
    rows, width = dffn.shape
    units = w_down.shape[0]
    step = 1024
    cols = pl.BlockSpec((rows, step), lambda i: (0, i))
    return pl.pallas_call(
        active_back_kernel,
        grid=(units // step,),
        in_specs=[once((rows, width)), pl.BlockSpec((step, width), lambda i: (i, 0)), cols],
        out_specs=[cols, pl.BlockSpec((1, step), lambda i: (0, i))],
        out_shape=[jax.ShapeDtypeStruct((rows, units), bf16), jax.ShapeDtypeStruct((1, units), f32)],
        compiler_params=params(62),
        cost_estimate=cost(2 * rows * width * units, 27 * MIB),
        name="active_back",
    )(dffn, w_down, der)


def feed_back_kernel(
    dup_ref, wup_ref, dresid2_hbm, hat_hbm, rstd_hbm, gain_ref, wo_hbm,
    dresid1_hbm, dbranch_hbm, datt_hbm, sums_ref,
    acc_ref, dresid_ref, hat_ref, rstd_ref, wo_ref, dbranch_ref, datt_ref, in_sem, out_sem,
):
    step = pl.program_id(0)
    loads = [
        pltpu.make_async_copy(hbm, ref, in_sem.at[i])
        for i, (hbm, ref) in enumerate(
            ((dresid2_hbm, dresid_ref), (hat_hbm, hat_ref), (rstd_hbm, rstd_ref), (wo_hbm, wo_ref))
        )
    ]

    @pl.when(step == 0)
    def _():
        for load in loads:
            load.start()

    part = mm(dup_ref[...], wup_ref[...], NT)

    @pl.when(step == 0)
    def _():
        acc_ref[...] = part

    @pl.when(step > 0)
    def _():
        acc_ref[...] += part

    @pl.when(step == pl.num_programs(0) - 1)
    def _():
        for load in loads:
            load.wait()
        sums = [0.0, 0.0, 0.0]
        copies = []
        for i, at in enumerate(range(0, acc_ref.shape[0], PAIR)):
            span = slice(at, at + PAIR)
            dnormed = acc_ref[span, :] + dresid_ref[span, :]
            hat = hat_ref[span, :]
            dresid = norm_back(dnormed, hat, rstd_ref[span, :1], line(gain_ref))
            dresid_ref[span, :] = dresid
            dbranch = dresid.astype(bf16)
            dbranch_ref[span, :] = dbranch
            datt_ref[span, :] = mm(dbranch, wo_ref[...], NT).astype(bf16)
            sums[0] += column_sum(dnormed * hat)
            sums[1] += column_sum(dnormed)
            sums[2] += column_sum(dbranch.astype(f32))
            outs = ((dresid_ref, dresid1_hbm), (dbranch_ref, dbranch_hbm), (datt_ref, datt_hbm))
            copies += stream_out(i, at, outs, out_sem)
        for i in range(3):
            sums_ref[i : i + 1, :] = sums[i]
        for copy in copies:
            copy.wait()


def feed_back(dup, w_up, dresid2, hat, rstd, w_out, gain):
    rows, width = hat.shape
    units = w_up.shape[1]
    step = 1024
    anywhere = pl.BlockSpec(memory_space=pl.ANY)
    return pl.pallas_call(
        feed_back_kernel,
        grid=(units // step,),
        in_specs=[
            pl.BlockSpec((rows, step), lambda i: (0, i)),
            pl.BlockSpec((width, step), lambda i: (0, i)),
            anywhere, anywhere, anywhere, vector(width), anywhere,
        ],
        out_specs=[anywhere, anywhere, anywhere, whole((8, width))],
        out_shape=[
            jax.ShapeDtypeStruct((rows, width), f32),
            jax.ShapeDtypeStruct((rows, width), bf16),
            jax.ShapeDtypeStruct((rows, width), bf16),
            jax.ShapeDtypeStruct((8, width), f32),
        ],
        scratch_shapes=[
            pltpu.VMEM((rows, width), f32),
            pltpu.VMEM((rows, width), f32),
            pltpu.VMEM((rows, width), f32),
            pltpu.VMEM((rows, 128), f32),
            pltpu.VMEM((width, width), bf16),
            pltpu.VMEM((rows, width), bf16),
            pltpu.VMEM((rows, width), bf16),
            pltpu.SemaphoreType.DMA((4,)),
            pltpu.SemaphoreType.DMA((3, rows // PAIR)),
        ],
        compiler_params=params(62),
        cost_estimate=cost(2 * rows * width * units, 36 * MIB),
        name="feed_back",
    )(dup, w_up, dresid2, hat, rstd, gain, w_out)


def attend_back_kernel(ids_ref, lengths_ref, qkv_ref, datt_ref, cos_ref, sin_ref, dmixed_ref, sums_ref, mask_ref):
    width = datt_ref.shape[1]
    block = pl.program_id(0)
    cosine = table_here(ids_ref, lengths_ref, cos_ref, block)
    sine = table_here(ids_ref, lengths_ref, sin_ref, block)
    mask_ref[...] = jnp.where(same_segment(ids_ref, lengths_ref, pl.program_id(0)), 0.0, masked_value)
    lane = lax.broadcasted_iota(jnp.int32, (PAIR, 2 * HD), 1)

    @pl.when(pl.program_id(0) == 0)
    def _():
        sums_ref[...] = jnp.zeros_like(sums_ref)

    mask = mask_ref[...]
    masks = (lane < HD, lane >= HD)
    group = 4
    for begin in range(0, width // (2 * HD), group):
        spots = [pair * 2 * HD for pair in range(begin, begin + group)]
        heads = [(at, m) for at in spots for m in masks]
        read = lambda ref, at: ref[:, at : at + 2 * HD]
        pick = lambda ref, at, m: jnp.where(m, read(ref, at), jnp.zeros((PAIR, 2 * HD), bf16))
        scores = [mm(read(qkv_ref, width + at), pick(qkv_ref, at, m), NT) + mask for at, m in heads]
        terms = [jnp.exp(x - jnp.max(x, 0, keepdims=True)) for x in scores]
        dweights = [mm(read(qkv_ref, 2 * width + at), pick(datt_ref, at, m), NT) for at, m in heads]
        weights = [x * (1.0 / jnp.sum(x, 0, keepdims=True)) for x in terms]
        dvalues = [mm(w.astype(bf16), pick(datt_ref, at, m)) for w, (at, m) in zip(weights, heads)]
        moved = [w * d for w, d in zip(weights, dweights)]
        dscores = [(m - w * jnp.sum(m, 0, keepdims=True)).astype(bf16) for w, m in zip(weights, moved)]
        dkeys = [mm(d, pick(qkv_ref, at, m)) for d, (at, m) in zip(dscores, heads)]
        dqueries = [mm(d, pick(qkv_ref, width + at, m), TN) for d, (at, m) in zip(dscores, heads)]
        for k, at in enumerate(spots):
            dquery, dkey, dvalue = (x[2 * k] + x[2 * k + 1] for x in (dqueries, dkeys, dvalues))
            dquery = dquery * score_scale
            dquery = dquery * cosine - partner(dquery) * sine
            dkey = dkey * cosine - partner(dkey) * sine
            for i, grad in enumerate((dquery, dkey, dvalue)):
                low = grad.astype(bf16)
                dmixed_ref[:, i * width + at : i * width + at + 2 * HD] = low
                sums_ref[:, i * width + at : i * width + at + 2 * HD] += column_sum(low.astype(f32))


def attend_back(ids, lengths, qkv, datt, tables):
    rows, width = datt.shape
    block = lambda cols: pl.BlockSpec((PAIR, cols), lambda i, *_: (i, 0))
    return pl.pallas_call(
        attend_back_kernel,
        grid_spec=pltpu.PrefetchScalarGridSpec(
            num_scalar_prefetch=2,
            grid=(rows // PAIR,),
            in_specs=[block(3 * width), block(width), once(tables[0].shape), once(tables[0].shape)],
            out_specs=[block(3 * width), whole((1, 3 * width))],
            scratch_shapes=[pltpu.VMEM((PAIR, PAIR), f32)],
        ),
        out_shape=[jax.ShapeDtypeStruct((rows, 3 * width), bf16), jax.ShapeDtypeStruct((1, 3 * width), f32)],
        compiler_params=params(62),
        cost_estimate=cost(2e10, 16 * MIB),
        name="attend_back",
    )(ids, lengths, qkv, datt, *tables)


def input_grad_kernel(dmixed_ref, w_ref, dresid_hbm, out_ref, dresid_ref, sem):
    step = pl.program_id(0)
    load = pltpu.make_async_copy(dresid_hbm, dresid_ref, sem)

    @pl.when(step == 0)
    def _():
        load.start()

    part = mm(dmixed_ref[...], w_ref[...], NT)

    @pl.when(step == 0)
    def _():
        out_ref[...] = part

    @pl.when((step > 0) & (step < pl.num_programs(0) - 1))
    def _():
        out_ref[...] += part

    @pl.when(step == pl.num_programs(0) - 1)
    def _():
        load.wait()
        out_ref[...] += part + dresid_ref[...]


def input_grad(dmixed, w_qkv, dresid):
    rows, width = dresid.shape
    return pl.pallas_call(
        input_grad_kernel,
        grid=(3,),
        in_specs=[
            pl.BlockSpec((rows, width), lambda i: (0, i)),
            pl.BlockSpec((width, width), lambda i: (0, i)),
            pl.BlockSpec(memory_space=pl.ANY),
        ],
        out_specs=whole((rows, width)),
        out_shape=jax.ShapeDtypeStruct((rows, width), f32),
        scratch_shapes=[pltpu.VMEM((rows, width), f32), pltpu.SemaphoreType.DMA],
        compiler_params=params(62),
        cost_estimate=cost(6 * rows * width * width, 20 * MIB),
        name="input_grad",
    )(dmixed, w_qkv, dresid)


def target_of(ids_ref, keep):
    return ids_ref[0] if keep else 1 - ids_ref[0]


def put(value, received, out_refs):
    if received is None:
        out_refs[0][...] = value.reshape(out_refs[0].shape).astype(bf16)
        return
    each, at = out_refs[0].shape[1], 0
    for out_ref in out_refs:
        count = out_ref.shape[0]
        part = value[at * each : (at + count) * each].reshape(out_ref.shape) + received[at : at + count].astype(f32)
        out_ref[...] = part.astype(out_ref.dtype)
        at += count


def outer_cols_kernel(counts, keep, slots, ids_ref, *refs):
    number = len(counts)
    received = refs[2 * number] if keep else None
    out_refs = refs[2 * number + 1 : -number] if keep else refs[2 * number : 2 * number + 1]
    turned_refs = refs[-number:]
    step = pl.program_id(0)
    each = turned_refs[0].shape[0] // slots
    target = target_of(ids_ref, keep)

    @pl.when(step == 0)
    def _():
        for left_ref, turned_ref in zip(refs[0 : 2 * number : 2], turned_refs):
            for at in range(0, left_ref.shape[1], 128):
                turned = left_ref[:, at : at + 128].T.astype(turned_ref.dtype)
                for k in range(128 // each):
                    rel = (at // each + k) ^ ids_ref[1]
                    slot = choose(target, lambda order: slot_of(rel, order), slots)
                    turned_ref[pl.ds(pl.multiple_of(slot * each, each), each), :] = turned[k * each : (k + 1) * each]

    done = 0
    for i, count in enumerate(counts):

        @pl.when((step >= done) & (step < done + count))
        def _(right_ref=refs[2 * i + 1], turned_ref=turned_refs[i]):
            put(mm(turned_ref[...].astype(bf16), right_ref[...]), received, out_refs)

        done += count


def outer_cols(ids, pairs, slots, received=None, parts=1, begin_at=0):
    rows = pairs[0][0].shape[1] // 2
    each = rows // slots
    keep = received is not None
    step = 1024
    specs, args, counts = [], [], []
    for left, right, begin, number in pairs:
        count = number // step
        first = sum(counts)
        specs.append(
            pl.BlockSpec((left.shape[0], rows), lambda i, ids: (0, target_of(ids, keep)), pipeline_mode=pl.Buffered(1))
        )
        specs.append(
            pl.BlockSpec(
                (right.shape[0], step),
                lambda i, *_, first=first, count=count, at=begin // step: (0, at + jnp.clip(i - first, 0, count - 1)),
            )
        )
        args += [left, right]
        counts.append(count)
    cols = sum(counts) * step
    spec = lambda count: pl.BlockSpec((count, each, step), lambda i, *_: (0, 0, i))
    shape = lambda count, kind: jax.ShapeDtypeStruct((count, each, cols), kind)
    if keep:
        specs.append(pl.BlockSpec((slots, each, step), lambda i, *_: (0, 0, begin_at // step + i)))
        args.append(received)
        outs = [spec(slots // 2)] + [spec(slots // 2 // parts)] * parts
        shapes = [shape(slots // 2, f32)] + [shape(slots // 2 // parts, bf16)] * parts
    else:
        outs, shapes = [spec(slots)], [shape(slots, bf16)]
    kind = bf16 if each % 16 == 0 else f32
    out = pl.pallas_call(
        functools.partial(outer_cols_kernel, counts, keep, slots),
        grid_spec=pltpu.PrefetchScalarGridSpec(
            num_scalar_prefetch=1, grid=(sum(counts),), in_specs=specs, out_specs=outs,
            scratch_shapes=[pltpu.VMEM((rows, left.shape[0]), kind) for left, *_ in pairs],
        ),
        out_shape=shapes,
        compiler_params=params(62),
        cost_estimate=cost(2 * args[0].shape[0] * rows * cols, (20 if keep else 15) * MIB),
        name="outer_cols",
    )(ids, *args)
    return out if keep else out[0]


def outer_rows_kernel(group, slots_apart, keep, ids_ref, *refs):
    left_refs, (right_ref, final_ref, dproj_ref) = refs[:group], refs[group : group + 3]
    received = refs[group + 3] if keep else None
    out_refs, proj_ref = refs[group + (4 if keep else 3) : -1], refs[-1]
    left = jnp.concatenate([ref[...].reshape(ref.shape[-2:]) for ref in left_refs], 1)
    value = mm(left, right_ref[...], TN)
    proj_ref[...] = mm(final_ref[...], dproj_ref[...], TN)
    tall, width = out_refs[0].shape[-2], value.shape[1]
    each = value.shape[0] // group
    short = proj_ref.shape[0] // group
    pieces = width // PROJ
    half = group // 2
    target = target_of(ids_ref, keep)
    for j in range(group):
        slot = j * slots_apart + pl.program_id(0)
        block = (choose(target, lambda order: rel_of(slot, order), group * slots_apart) ^ ids_ref[1]) & (group - 1)
        part = value[j * each : (j + 1) * each, :]
        small = proj_ref[pl.ds(pl.multiple_of(block * short, short), short), :]
        fold = short // pieces if short >= pieces else 1
        low = [small[i * fold : (i + 1) * fold, :] for i in range(short // fold)]
        if keep:
            part = part + received[j, 0, :each, :].astype(f32)
            low = [
                x + received[j, 0, each : each + fold, i * PROJ : (i + 1) * PROJ].astype(f32) for i, x in enumerate(low)
            ]
            out_ref, at = (out_refs[0], j) if j < half else (out_refs[1 + 2 * (j - half) // half], j % (half // 2))
        else:
            out_ref, at = out_refs[0], j
        kind = out_ref.dtype
        out_ref[at, 0, :each, :] = part.astype(kind)
        out_ref[at, 0, each:, :] = jnp.zeros((tall - each, width), kind)
        for i, x in enumerate(low):
            out_ref[at, 0, each : each + fold, i * PROJ : (i + 1) * PROJ] = x.astype(kind)


def outer_rows(ids, left, right, final, dproj, slots, group, received=None):
    tokens_here, rows = left.shape
    width = right.shape[1]
    rest = slots // group
    each = rows // (2 * slots)
    tall = each + 8
    keep = received is not None
    spec = lambda count: pl.BlockSpec((count, 1, tall, width), lambda i, *_: (0, i, 0, 0))
    shape = lambda count, kind: jax.ShapeDtypeStruct((count, rest, tall, width), kind)

    def owner(slot, ids):
        target = target_of(ids, keep)
        return target * slots + (choose(target, lambda order: rel_of(slot, order), slots) ^ ids[1])

    specs = [
        pl.BlockSpec((tokens_here, each), lambda i, ids, j=j: (0, owner(j * rest + i, ids))) for j in range(group)
    ]
    lefts = [left] * group
    if each < 128:
        specs = [
            pl.BlockSpec((1, tokens_here, each), lambda i, ids, j=j: (owner(j * rest + i, ids), 0, 0)) for j in range(group)
        ]
        lefts = [left.reshape(tokens_here, -1, each).transpose(1, 0, 2)] * group
    specs += [
        once((tokens_here, width)),
        pl.BlockSpec((tokens_here, final.shape[1] // (2 * rest)), lambda i, ids: (0, owner(i, ids) // group)),
        once((tokens_here, PROJ)),
    ]
    args = lefts + [right, final, dproj]
    if keep:
        specs.append(spec(group))
        args.append(received.reshape(group, rest, tall, width))
        outs = [spec(group // 2), spec(group // 4), spec(group // 4)]
        shapes = [shape(group // 2, f32), shape(group // 4, bf16), shape(group // 4, bf16)]
    else:
        outs, shapes = [spec(group)], [shape(group, bf16)]
    out = pl.pallas_call(
        functools.partial(outer_rows_kernel, group, rest, keep),
        grid_spec=pltpu.PrefetchScalarGridSpec(
            num_scalar_prefetch=1, grid=(rest,), in_specs=specs, out_specs=outs,
            scratch_shapes=[pltpu.VMEM((final.shape[1] // (2 * rest), PROJ), f32)],
        ),
        out_shape=shapes,
        compiler_params=params(62),
        cost_estimate=cost(tokens_here * rows * width, (20 if keep else 15) * MIB),
        name="outer_rows",
    )(ids, *args)
    out = [o.reshape(-1, tall, width) for o in out]
    return out if keep else out[0]


def flips(count):
    bits = [1 << i for i in range(count.bit_length() - 1)]
    third = {16: 1, 64: 2}[count]
    swapped = bits[third : 2 * third] + bits[:third] + bits[2 * third :][::-1]
    return bits, swapped


def slot_of(rel, order):
    return sum(
        ((rel >> (flip.bit_length() - 1)) & 1) << (len(order) - 1 - i) for i, flip in enumerate(order)
    )


def rel_of(slot, order):
    return sum(
        ((slot >> (len(order) - 1 - i)) & 1) << (flip.bit_length() - 1) for i, flip in enumerate(order)
    )


def choose(core, function, count):
    first, second = (function(order) for order in flips(count))
    return jnp.where(core == 0, first, second)


def hop(values, stage, count):
    pairs = []
    for stream, order in enumerate(flips(count)):
        pairs += [(stream * count + i, stream * count + (i ^ order[stage])) for i in range(count)]
    return lax.ppermute(values, ("stream", "dp"), pairs)


def swap(values):
    return lax.ppermute(values, "stream", [(0, 1), (1, 0)])


def after(value, *others):
    return lax.optimization_barrier((value, *others))[0]


def gather_both(first, first_stages, second, second_stages, count):
    pending = [(first, list(first_stages)), (second, list(second_stages))]
    while any(stages for _, stages in pending):
        got = [hop(values, stages[-1], count) if stages else None for values, stages in pending]
        values = lax.optimization_barrier([x for pair in zip(pending, got) for x in (pair[0][0], pair[1]) if x is not None])
        joined = []
        for (_, stages), arrived in zip(pending, got):
            value = values.pop(0)
            if arrived is not None:
                value = jnp.concatenate([value, values.pop(0)], 0)
            joined.append((value, stages[:-1]))
        held = lax.optimization_barrier([value for value, _ in joined])
        pending = [(value, stages) for value, (_, stages) in zip(held, joined)]
    return [value for value, _ in pending]


def take_in(keep, got):
    half = keep.shape[0] // 2
    if half == 0:
        return keep[0] + got[0].astype(f32), None
    return keep[:half] + got[:half].astype(f32), (keep[half:] + got[half:].astype(f32)).astype(bf16)


def scatter_sum(keep, send, stage, count, got=None):
    if got is not None:
        keep, send = take_in(keep, got)
    while send is not None:
        keep, send = take_in(keep, hop(send, stage, count))
        stage += 1
    return keep


def total_sum(values, stage, count):
    for later in range(stage, count.bit_length() - 1):
        values = values + hop(values, later, count)
    return values


def body(
    tokens, doc_lengths, cand_docs, group_sizes, w_qkv, b_qkv, w_attn_out, b_attn_out, gain_one, bias_one,
    w_up, b_up, w_down, b_down, gain_two, bias_two, w_proj,
):
    stream = lax.axis_index("stream")
    me = lax.axis_index("dp")
    count = lax.axis_size("dp")
    hidden = tokens[0]
    rows, width = hidden.shape
    half = rows // 2
    ids = jnp.stack([stream, me]).astype(jnp.int32)
    tables = [jnp.asarray(table) for table in rotation_tables()]
    group = {16: 4, 64: 16}[count]

    hold = lax.optimization_barrier
    levels = {16: 2, 64: 4}[count]
    last_stage = count.bit_length() - 1
    shape = (count, levels)
    info = jnp.concatenate([cand_docs.reshape(QH, CAND), group_sizes.reshape(QH, 1)], 1).astype(jnp.int32)
    hidden_, info = hold((hidden, info))
    info_got = hop(info, last_stage - 1, count)
    qkv, attended, hat1, rstd1, normed = attend(
        ids, doc_lengths, hidden_, w_qkv, b_qkv, tables, w_attn_out, b_attn_out, gain_one, bias_one
    )
    info, info_got, normed = hold((info, info_got, normed))
    info = jnp.concatenate([info, info_got], 0)
    info, normed = hold((info, normed))
    info_got = hop(info, last_stage - 2, count)
    active, der, hat2, rstd2, final, projected, vecs = feed(
        normed, w_up, b_up, w_down, b_down, hat1, gain_one, bias_one, gain_two, bias_two, w_proj
    )
    info, info_got, vecs = hold((info, info_got, vecs))
    info = jnp.concatenate([info, info_got], 0)

    on_docs = stream == 1
    other = swap(jnp.where(on_docs, vecs[:half], vecs[half:]))
    own_docs = jnp.where(on_docs, vecs[half:], other)
    queries = jnp.where(on_docs, other, vecs[:half])
    queries, near = gather_both(queries, range(levels, last_stage), own_docs, range(levels), count)
    queries = queries.reshape(-1, QLEN, PROJ)
    far = swap(near)
    scores, entries = score(ids, info, doc_lengths, queries, near, far, shape)
    scores = total_sum(scores, levels, count)
    loss, dq_keep, dq_send, keep, send = score_back(
        ids, info, doc_lengths, entries, scores, queries, near, far, shape
    )
    loss = lax.dynamic_slice_in_dim(loss, (me >> levels) * QH, QH, 0)
    by_row = (-1, half, PROJ)
    keep, q_keep = keep.reshape(by_row), dq_keep.reshape(by_row)
    got, q_got = swap(send).reshape(by_row), hop(dq_send.reshape(by_row), levels, count)
    keep, got, q_keep, q_got = hold((keep, got, q_keep, q_got))
    keep, send = take_in(keep, got)
    q_keep, q_send = take_in(q_keep, q_got)
    keep, send, q_keep, q_send = hold((keep, send, q_keep, q_send))
    got, q_got = hop(send, 0, count), hop(q_send, levels + 1, count)
    keep, got, q_keep, q_got = hold((keep, got, q_keep, q_got))
    keep, send = take_in(keep, got)
    dqueries = scatter_sum(q_keep, None, last_stage, count, q_got)
    ddocs = scatter_sum(keep, send, 1, count)
    back = swap(jnp.where(on_docs, dqueries, ddocs))
    grad_vectors = jnp.where(
        on_docs, jnp.concatenate([back, ddocs], 0), jnp.concatenate([dqueries, back], 0)
    )

    def add_first(keep, got):
        half = keep.shape[0] // 2
        return (keep[half:] + got.astype(f32)).astype(bf16)

    def add_second(keep, got):
        half = keep.shape[0] // 2
        return keep[:half] + got.astype(f32)

    dproj, dresid2, dffn, sums2 = head_back(grad_vectors, projected, w_proj, hat2, rstd2, gain_two)
    down = lambda left, received=None: outer_rows(
        ids, left, dffn, final, dproj, count, group, received
    )
    units = w_up.shape[1]
    up = lambda left, received=None: outer_cols(ids, [(left, dup, 0, units)], count, received)
    mix_out = lambda left: outer_cols(ids, [(left, dmixed, 0, 3 * width), (attended, dbranch, 0, width)], count)
    mix_a = lambda left, received: outer_cols(ids, [(left, dmixed, 0, 2 * width)], count, received)
    mix_b = lambda left, received: outer_cols(
        ids, [(left, dmixed, 2 * width, width), (attended, dbranch, 0, width)], count, received, 1, 2 * width
    )

    d_out = down(active)
    d_got = swap(d_out)
    dffn_, d_out = hold((dffn, d_out))
    dup, sum_up = active_back(dffn_, w_down, der)
    active_, d_got, dup = hold((active, d_got, dup))
    d_keep, d_low, d_high = down(active_, d_got)
    d_high, d_low, normed_, d_keep = hold((d_high, d_low, normed, d_keep))
    u_out = up(normed_)
    d_high, d_low, u_out, dup_ = hold((d_high, d_low, u_out, dup))
    d_high_got, d_low_got, u_got = hop(d_high, 0, count), hop(d_low, 0, count), swap(u_out)
    dresid1, dbranch, dattended, sums1 = feed_back(dup_, w_up, dresid2, hat1, rstd1, w_attn_out, gain_one)
    d_keep, d_high_got, d_low_got, dbranch = hold((d_keep, d_high_got, d_low_got, dbranch))
    d_send = add_first(d_keep, d_high_got)
    d_keep = add_second(d_keep, d_low_got)
    d_keep, d_send, normed_, u_got = hold((d_keep, d_send, normed, u_got))
    d_got = hop(d_send, 1, count)
    u_keep, u_send = up(normed_, u_got)
    d_keep, d_got, u_keep = hold((d_keep, d_got, u_keep))
    d_keep, d_send = take_in(d_keep, d_got)
    u_send, d_keep, d_send, dattended = hold((u_send, d_keep, d_send, dattended))
    u_got, d_got = hop(u_send, 0, count), hop(d_send, 2, count)
    dmixed, sum_qkv = attend_back(ids, doc_lengths, qkv, dattended, tables)
    d_keep, d_got, u_keep, u_got, dmixed = hold((d_keep, d_got, u_keep, u_got, dmixed))
    u_keep, u_send = take_in(u_keep, u_got)
    d_keep, d_send = take_in(d_keep, d_got)
    sums = [sum_qkv[0], sums1[2], sums1[0], sums1[1], sum_up[0], sums2[2], sums2[0], sums2[1]]
    late = jnp.concatenate([v.reshape(2 * count, -1) for v in sums], 1)
    u_send, u_keep, hidden_, late, d_keep, d_send = hold((u_send, u_keep, hidden, late, d_keep, d_send))
    u_got, l_got, d_got = hop(u_send, 1, count), swap(late), hop(d_send, 3, count)
    m_out = mix_out(hidden_)
    m_out, late, l_got, u_keep, u_got, d_keep, d_got = hold((m_out, late, l_got, u_keep, u_got, d_keep, d_got))
    g_down = scatter_sum(d_keep, d_send, 4, count, d_got)
    u_keep, u_send = take_in(u_keep, u_got)
    late = late + l_got
    m_out, hidden_, late, g_down, u_send, u_keep = hold((m_out, hidden_, late, g_down, u_send, u_keep))
    m_got, l_got, u_got = swap(m_out), hop(late, 0, count), hop(u_send, 2, count)
    a_keep, a_send = mix_a(hidden_, m_got)
    u_keep, u_got, a_send, late, l_got = hold((u_keep, u_got, a_send, late, l_got))
    u_keep, u_send = take_in(u_keep, u_got)
    late = late + l_got
    u_keep, u_send, a_send, hidden_, late = hold((u_keep, u_send, a_send, hidden_, late))
    a_got, u_got, l_got = hop(a_send, 0, count), hop(u_send, 3, count), hop(late, 1, count)
    b_keep, b_send = mix_b(hidden_, m_got)
    u_keep, u_got, b_keep, late, l_got = hold((u_keep, u_got, b_keep, late, l_got))
    g_up = scatter_sum(u_keep, u_send, 4, count, u_got)
    late = late + l_got
    a_keep, a_got, g_up, b_send, late = hold((a_keep, a_got, g_up, b_send, late))
    a_keep, a_send = take_in(a_keep, a_got)
    a_keep, a_send, b_send, dmixed_, late = hold((a_keep, a_send, b_send, dmixed, late))
    a_got, b_got = hop(a_send, 1, count), hop(b_send, 0, count)
    l_got = hop(late, 2, count)
    grad_hidden = input_grad(dmixed_, w_qkv, dresid1)
    a_keep, a_got, grad_hidden, b_got = hold((a_keep, a_got, grad_hidden, b_got))
    b_keep, b_send = take_in(b_keep, b_got)
    b_got = hop(b_send, 1, count)
    a_keep, a_send = take_in(a_keep, a_got)
    g_a = scatter_sum(a_keep, a_send, 2, count)
    b_keep, b_send = take_in(b_keep, b_got)
    g_b = scatter_sum(b_keep, b_send, 2, count)

    late = total_sum(late + l_got, 3, count)
    mine = lax.dynamic_slice_in_dim(late, stream * count + me, 1, 0)[0]
    sizes = [v.shape[0] // (2 * count) for v in sums]
    parts = [mine[end - size : end] for end, size in zip(np.cumsum(sizes), sizes)]
    g_bqkv, g_bout, g_gain1, g_bias1, g_bup, g_bdown, g_gain2, g_bias2 = parts
    tall = w_down.shape[0] // (2 * count)
    short = width // (2 * count)
    pieces = width // PROJ
    fold = max(short // pieces, 1)
    g_proj = g_down[tall : tall + fold].reshape(fold, pieces, PROJ).transpose(1, 0, 2)[: short // fold].reshape(short, PROJ)
    return (
        loss[:, 0][None, None, :],
        grad_hidden[None],
        jnp.concatenate([g_a, g_b[:, :width]], 1),
        g_bqkv,
        g_b[:, width:],
        g_bout,
        g_gain1,
        g_bias1,
        g_up,
        g_bup,
        g_down[:tall],
        g_bdown,
        g_gain2,
        g_bias2,
        g_proj,
    )


def solution(mesh):
    every = P(("stream", "dp"))
    rows = P(("stream", "dp"), None)
    return jax.shard_map(
        body,
        mesh=mesh,
        in_specs=(P("stream", "dp", None), P(), P("dp", "stream", None, None), P("dp", "stream", None)) + (P(),) * 13,
        out_specs=(
            P("dp", "stream", None), P("stream", "dp", None), rows, every, rows, every, every, every, rows, every,
            rows, every, every, every, rows,
        ),
        check_vma=False,
    )
```
